32 devices in a mesh: section: 4 (over y, core), dp: 8 (over z, x).
Axes of the slice: x: 2, y: 2, z: 4, core: 2. Of those that a mesh axis runs over, the one named last changes fastest.
Arguments:
- patches: bfloat16 [16, 197, 768], P('dp'), may hold values from -6 to 6
- page_mask: int32 [16, 197], P('dp'), may hold values from 0 to 1, as said below
- mask_token: bfloat16 [768], replicated, may hold values from -6 to 6
- buckets: int32 [197, 197], replicated, may hold values from 0 to 731
- ln_gain: bfloat16 [4, 768], P('section'), may hold values from 0.25 to 1.75
- ln_shift: bfloat16 [4, 768], P('section'), may hold values from -4 to 4
- layer_scale: bfloat16 [4, 768], P('section'), may hold values from 0.25 to 1.75
- branch_bias: bfloat16 [4, 768], P('section'), may hold values from -4 to 4
- qkv_weight: bfloat16 [2, 768, 2304], P(None, 'dp'), may hold values from -0.21875 to 0.21875
- qv_bias: bfloat16 [2, 1536], replicated, may hold values from -4 to 4
- out_weight: bfloat16 [2, 768, 768], P(None, 'dp'), may hold values from -1.25 to 1.25
- rel_table: bfloat16 [2, 12, 732], replicated, may hold values from -6 to 6
- up_weight: bfloat16 [2, 768, 3072], P(None, 'dp'), may hold values from -0.21875 to 0.21875
- up_bias: bfloat16 [2, 3072], replicated, may hold values from -4 to 4
- down_weight: bfloat16 [2, 3072, 768], P(None, 'dp'), may hold values from -0.109375 to 0.109375
- cotangent: bfloat16 [16, 197, 768], P('dp'), may hold values from -6 to 6
Outputs:
- block_out: bfloat16 [16, 197, 768], P('dp', None, 'section')
- input_grad: float32 [16, 197, 768], P('dp', None, 'section')
- qkv_grad: float32 [2, 768, 2304], P(None, 'dp', 'section')
- out_grad: float32 [2, 768, 768], P(None, 'dp', 'section')
- up_grad: float32 [2, 768, 3072], P(None, 'dp', 'section')
- down_grad: float32 [2, 3072, 768], P(None, 'dp', 'section')
- qv_bias_grad: float32 [2, 1536], replicated
- up_bias_grad: float32 [2, 3072], replicated
- table_grad: float32 [2, 12, 732], replicated
- gain_grad: float32 [4, 768], P('section')
- shift_grad: float32 [4, 768], P('section')
- scale_grad: float32 [4, 768], P('section')
- bias_grad: float32 [4, 768], P('section')
- mask_token_grad: float32 [768], replicated
The draws below stay inside these ranges and needn't reach their ends.
Inputs may be any that keep to these rules, and one draw needn't show every extreme that they name: `page_mask`: each page masks its patches independently, with a probability of its own drawn per page between 20 and 60 percent.
All inputs are finite; a program needn't handle non-finite values.
Results may differ from the reference program's by a relative error of at most 0.018.
Values may be sent and summed in bfloat16 or wider, within the bound.
A program may use at most 256 MiB of HBM per device.

```python
import jax
import jax.numpy as jnp
from jax import lax

D = 768
H = 12
FF = 3072
L = 197
NB = 732
LAYERS = 2
HALVES = 4
PAGES_DEV = 2
PAGES = 16


def draw_page_mask(key, part):
    rate_key, cell_key = jax.random.split(key)
    rates = jax.random.randint(rate_key, (PAGES, 1), 20, 61)
    cells = jax.random.randint(cell_key, (PAGES, L), 0, 100)
    return (cells < rates).astype(jnp.int32)


def touch_ends(array, rng, least, top_value):
    place = [jax.random.randint(jax.random.fold_in(rng, axis), (), 0, length) for axis, length in enumerate(array.shape)]
    main_axis = array.shape.index(max(array.shape))
    neighbour = place[:main_axis] + [(place[main_axis] + 1) % array.shape[main_axis]] + place[main_axis + 1:]
    return array.at[tuple(place)].set(least).at[tuple(neighbour)].set(top_value)


def block_levels(rng, dims, cuts, least, top_value):
    def one(dim, shards_of):
        heights = jax.random.uniform(jax.random.fold_in(jax.random.fold_in(rng, 6), dim), (shards_of,), jnp.float32, least / len(cuts), top_value / len(cuts))
        return jnp.repeat(jnp.exp(heights), dims[dim] // shards_of).reshape((-1,) + (1,) * (len(dims) - dim - 1))

    level = one(*cuts[0])
    for cut in cuts[1:]:
        level = level * one(*cut)
    return level


def normal_values(rng, dims, width, most, cuts=(), held_as=jnp.bfloat16):
    level = block_levels(rng, dims, cuts, -0.22, 0.18) if cuts else 1.0
    result = jax.random.normal(rng, dims, jnp.float32) * width * level
    return jnp.minimum(jnp.maximum(result, -most), most).astype(held_as)


def setup_inputs(seed: int = 0) -> dict:
    splits = jax.random.split(jax.random.key(seed), 17)
    patches = normal_values(splits[0], (PAGES, L, D), 1.0, 6.0, ((0, 8),))
    page_mask = draw_page_mask(jax.random.fold_in(splits[16], 71), 0)
    mask_token = normal_values(splits[2], (D,), 1.0, 6.0)
    buckets = touch_ends(jax.random.randint(splits[3], (L, L), 0, NB), jax.random.fold_in(splits[3], 1), 0, NB - 1).astype(jnp.int32)
    ln_gain = jnp.clip(1.0 + 0.15 * jax.random.normal(splits[4], (HALVES, D), jnp.float32), 0.25, 1.75).astype(jnp.bfloat16)
    ln_shift = normal_values(splits[5], (HALVES, D), 0.3, 4.0, ((0, 4),))
    layer_scale = jnp.clip(1.0 + 0.15 * jax.random.normal(splits[6], (HALVES, D), jnp.float32), 0.25, 1.75).astype(jnp.bfloat16)
    branch_bias = normal_values(splits[7], (HALVES, D), 0.3, 4.0, ((0, 4),))
    qkv_weight = normal_values(splits[8], (LAYERS, D, 3 * D), D ** -0.5, 0.21875, ((1, 8),))
    qv_bias = normal_values(splits[9], (LAYERS, 2 * D), 0.3, 4.0)
    out_weight = normal_values(splits[10], (LAYERS, D, D), (D // 32) ** -0.5, 1.25, ((1, 8),))
    rel_table = normal_values(splits[11], (LAYERS, H, NB), 1.0, 6.0)
    up_weight = normal_values(splits[12], (LAYERS, D, FF), D ** -0.5, 0.21875, ((1, 8),))
    up_bias = normal_values(splits[13], (LAYERS, FF), 0.3, 4.0)
    down_weight = normal_values(splits[14], (LAYERS, FF, D), FF ** -0.5, 0.109375, ((1, 8),))
    cotangent = normal_values(splits[15], (PAGES, L, D), 1.0, 6.0, ((0, 8),))
    return dict(patches=patches, page_mask=page_mask, mask_token=mask_token, buckets=buckets, ln_gain=ln_gain, ln_shift=ln_shift, layer_scale=layer_scale, branch_bias=branch_bias, qkv_weight=qkv_weight, qv_bias=qv_bias, out_weight=out_weight, rel_table=rel_table, up_weight=up_weight, up_bias=up_bias, down_weight=down_weight, cotangent=cotangent)


eps_norm = 1e-06
highest = lax.Precision.HIGHEST

@jax.custom_vjp
def low(v):
    return lax.optimization_barrier(v.astype(jnp.bfloat16)).astype(jnp.float32)

@jax.custom_vjp
def low_back(v):
    return v

def low_keep(v):
    return (low(v), None)

def low_pass(kept, grad):
    return (grad,)

def back_keep(v):
    return (v, None)

def back_low(kept, grad):
    return (low(grad),)
low.defvjp(low_keep, low_pass)
low_back.defvjp(back_keep, back_low)

def norm_rows(values, gain_row, shift_row):
    row_mean = lax.optimization_barrier(jnp.mean(values, -1, keepdims=True))
    centered = values - row_mean
    spread = lax.optimization_barrier(jnp.mean(centered * centered, -1, keepdims=True))
    return centered * lax.rsqrt(spread + eps_norm) * gain_row + shift_row

def attention_half(values, gain_row, shift_row, scale_row, bias_row, w_qkv, qv_pair, w_out, table_now, bucket_ids):
    page_count, page_rows, model_width = values.shape
    head_count = table_now.shape[0]
    head_size = model_width // head_count
    normed = low(norm_rows(values, gain_row, shift_row))
    projected = jnp.matmul(normed, w_qkv, precision=highest)
    queries = low_back(low(projected[..., :model_width] + qv_pair[:model_width]))
    keys_all = low_back(low(projected[..., model_width:2 * model_width]))
    values_all = low_back(low(projected[..., 2 * model_width:] + qv_pair[model_width:]))
    split_shape = (page_count, page_rows, head_count, head_size)
    raw_scores = jnp.einsum('pihd,pjhd->phij', queries.reshape(split_shape), keys_all.reshape(split_shape), precision=highest)
    position_bias = jnp.take(table_now, bucket_ids, axis=1)
    scores = low_back(raw_scores * head_size ** (-0.5) + position_bias[None])
    attention_probs = jax.nn.softmax(scores, axis=-1)
    context = jnp.einsum('phij,pjhd->pihd', low(attention_probs), values_all.reshape(split_shape), precision=highest)
    context = low_back(low(context.reshape(page_count, page_rows, model_width)))
    branch = low_back(jnp.matmul(context, w_out, precision=highest) + bias_row)
    return low_back(low(values + scale_row * branch))

def mlp_half(values, gain_row, shift_row, scale_row, bias_row, w_up, up_vec, w_down):
    normed = low(norm_rows(values, gain_row, shift_row))
    pre_act = low_back(jnp.matmul(normed, w_up, precision=highest) + up_vec)
    activated = low(jax.nn.gelu(pre_act, approximate=True))
    branch = low_back(jnp.matmul(activated, w_down, precision=highest) + bias_row)
    return low_back(low(values + scale_row * branch))

def reference(patches, page_mask, mask_token, buckets, ln_gain, ln_shift, layer_scale, branch_bias, qkv_weight, qv_bias, out_weight, rel_table, up_weight, up_bias, down_weight, cotangent):

    def forward(inputs, token_vec, gains, shifts, scales, biases, qkv_all, qv_all, out_all, tables, up_all, up_b_all, down_all):
        blocks_in = inputs.reshape(-1, PAGES_DEV, L, D)
        masks_in = page_mask.reshape(-1, PAGES_DEV, L)

        def one_block(carry_in, pieces):
            block_in, block_mask = pieces
            values = jnp.where(block_mask[..., None] == 1, token_vec, block_in)
            for layer_index in range(LAYERS):
                first_half = 2 * layer_index
                second_half = first_half + 1
                values = attention_half(values, gains[first_half], shifts[first_half], scales[first_half], biases[first_half], qkv_all[layer_index], qv_all[layer_index], out_all[layer_index], tables[layer_index], buckets)
                values = mlp_half(values, gains[second_half], shifts[second_half], scales[second_half], biases[second_half], up_all[layer_index], up_b_all[layer_index], down_all[layer_index])
            return (carry_in, values)
        carry_out, outputs = lax.scan(jax.checkpoint(one_block), jnp.zeros((), jnp.float32), (blocks_in, masks_in))
        return outputs.reshape(inputs.shape)
    primals = (patches.astype(jnp.float32), mask_token.astype(jnp.float32), ln_gain.astype(jnp.float32), ln_shift.astype(jnp.float32), layer_scale.astype(jnp.float32), branch_bias.astype(jnp.float32), qkv_weight.astype(jnp.float32), qv_bias.astype(jnp.float32), out_weight.astype(jnp.float32), rel_table.astype(jnp.float32), up_weight.astype(jnp.float32), up_bias.astype(jnp.float32), down_weight.astype(jnp.float32))
    block_out, pullback = jax.vjp(forward, *primals)
    grads = pullback(cotangent.astype(jnp.float32))
    return (block_out.astype(jnp.bfloat16), grads[0], grads[6], grads[8], grads[10], grads[12], grads[7], grads[11], grads[9], grads[2], grads[3], grads[4], grads[5], grads[1])
```

```python
import functools

import jax
import jax.numpy as jnp
from jax import lax
from jax.experimental import pallas as pl
from jax.experimental.pallas import tpu as pltpu
from jax.sharding import PartitionSpec as P

EPS = 1e-06
MESH = pl.DeviceIdType.MESH
NEG = -1e30
LANES = 128
BF = jnp.bfloat16
F32 = jnp.float32


def pad_up(x, m):
    return (x + m - 1) // m * m


def nn(a, b):
    return jnp.dot(a, b, preferred_element_type=F32)


def nt(a, b):
    return lax.dot_general(a, b, (((1,), (1,)), ((), ())), preferred_element_type=F32)


def tn(a, b):
    return lax.dot_general(a, b, (((0,), (0,)), ((), ())), preferred_element_type=F32)


def bias_kernel(rows, buckets_ref, table_ref, out_ref):
    tables, highs, _ = table_ref.shape
    prow, pcol = buckets_ref.shape
    step = 16

    def body(block, carry):
        at = pl.multiple_of(block * step, step)
        for half in range(pcol // LANES):
            ids = buckets_ref[pl.ds(at, step), half * LANES : (half + 1) * LANES]
            low = ids & (LANES - 1)
            high = lax.shift_right_logical(ids, 7)
            column = lax.broadcasted_iota(jnp.int32, (step, LANES), 1) + half * LANES
            inside = column < rows
            picks = [high == number for number in range(highs)]
            for t in range(tables):
                value = jnp.full((step, LANES), NEG, F32)
                for number in range(highs):
                    row = jnp.broadcast_to(table_ref[t, number : number + 1, :], (step, LANES))
                    got = jnp.take_along_axis(row, low, axis=1)
                    value = jnp.where(picks[number], got, value)
                value = jnp.where(inside, value, NEG)
                out_ref[t, pl.ds(at, step), half * LANES : (half + 1) * LANES] = value.astype(BF)
        return carry

    lax.fori_loop(0, prow // step, body, 0)


def position_bias(buckets, tables, rows):
    return pl.pallas_call(
        functools.partial(bias_kernel, rows),
        out_shape=jax.ShapeDtypeStruct((tables.shape[0],) + buckets.shape, BF),
        in_specs=[pl.BlockSpec(memory_space=pltpu.VMEM)] * 2,
        out_specs=pl.BlockSpec(memory_space=pltpu.VMEM),
        name="position_bias",
        cost_estimate=pl.CostEstimate(flops=10**7, bytes_accessed=10**6, transcendentals=0),
    )(buckets, tables)


def bucket_kernel(rows, highs, buckets_ref, grads_ref, out_ref, acc_ref):
    groups = grads_ref.shape[0]
    pcol = grads_ref.shape[2]
    acc_ref[...] = jnp.zeros_like(acc_ref)
    step = 8

    def body(block, carry):
        at = pl.multiple_of(block * step, step)
        ids_all = buckets_ref[pl.ds(at, step), :]
        grads_all = grads_ref[:, pl.ds(at, step), :]
        total = None
        for r in range(step):
            ids = ids_all[r : r + 1, :]
            low = ids & (LANES - 1)
            high = lax.shift_right_logical(ids, 7)
            spots = lax.broadcasted_iota(jnp.int32, (LANES, pcol), 0)
            hot = jnp.where(spots == low, 1.0, 0.0).astype(BF)
            grads = grads_all[:, r, :]
            parts = [jnp.where(high == number, grads, 0.0) for number in range(highs)]
            left = jnp.concatenate(parts, 0).astype(BF)
            got = nt(left, hot)
            total = got if total is None else total + got
        acc_ref[...] += total
        return carry

    lax.fori_loop(0, pad_up(rows, step) // step, body, 0)
    out_ref[...] = acc_ref[...].reshape(out_ref.shape)


def bucket_sums(buckets, grads, rows, highs):
    groups = grads.shape[0]
    return pl.pallas_call(
        functools.partial(bucket_kernel, rows, highs),
        out_shape=jax.ShapeDtypeStruct((highs, groups, LANES), F32),
        in_specs=[pl.BlockSpec(memory_space=pltpu.VMEM)] * 2,
        out_specs=pl.BlockSpec(memory_space=pltpu.VMEM),
        scratch_shapes=[pltpu.VMEM((highs * groups, LANES), F32)],
        name="bucket_sums",
        compiler_params=pltpu.CompilerParams(vmem_limit_bytes=40 * 2**20),
        cost_estimate=pl.CostEstimate(flops=10**9, bytes_accessed=3 * 10**6, transcendentals=0),
    )(buckets, grads)


class Layout:
    def __init__(self, layers, heads, head, rows, prow, width, hidden):
        self.layers, self.heads, self.head = layers, heads, head
        self.rows, self.prow, self.width, self.hidden = rows, prow, width, hidden
        self.own = heads * head
        self.halves = 2 * layers
        h = self.halves
        self.scale_at, self.bias_at, self.gain_at, self.shift_at = 0, h, 2 * h, 3 * h
        self.qv_at, self.up_at, self.token_at = 4 * h, 4 * h + layers, 4 * h + 2 * layers
        self.smalls = pad_up(4 * h + 2 * layers + 1, 8)


def norm_stats(x):
    mean = jnp.mean(x, -1, keepdims=True)
    centered = x - mean
    r = lax.rsqrt(jnp.mean(centered * centered, -1, keepdims=True) + EPS)
    return centered * r, r


def blocks_kernel(
    lay,
    x0_ref, g4_ref, mask_ref, vec_ref, qvb_ref, upb_ref, bias_ref,
    wqkv_ref, wout_ref, wup_ref, wdn_ref,
    v4_ref, g0_ref, small_ref, ds_ref,
    gqkv_ref, gout_ref, gup_ref, gdn_ref,
    v_buf, normed, branch, qkv, probs, ctx, act, gate, bgrad, dqkv, acc, g_buf,
    core_out, core_in, far_out, far_in,
    core_send, core_recv, far_send, far_recv, row_send, row_recv,
):
    section = lax.axis_index("section")
    mate = {"section": section + 1 - 2 * lax.rem(section, 2)}
    far = {"section": lax.rem(section + 2, 4)}
    halves, prow, width = lay.halves, lay.prow, lay.width
    own, hid, hd = lay.own, lay.hidden, lay.head

    barrier = pltpu.get_barrier_semaphore()
    for other in (mate, far):
        pl.semaphore_signal(barrier, inc=1, device_id=other, device_id_type=MESH)
    pl.semaphore_wait(barrier, 2)

    small_ref[...] = jnp.zeros_like(small_ref)

    def add_small(at, row, columns=slice(None)):
        small_ref[at : at + 1, columns] = row

    def column_sum(x):
        return jnp.sum(x, 0, keepdims=True)

    def vec(kind, k):
        return vec_ref[kind * halves + k : kind * halves + k + 1, :]

    def share_rows(ref, step):
        return pltpu.make_async_remote_copy(
            src_ref=ref.at[0], dst_ref=ref.at[1],
            send_sem=row_send.at[step], recv_sem=row_recv.at[step],
            device_id=mate, device_id_type=MESH,
        )

    def to_mate(step):
        return pltpu.make_async_remote_copy(
            src_ref=core_out.at[step], dst_ref=core_in.at[step],
            send_sem=core_send.at[step], recv_sem=core_recv.at[step],
            device_id=mate, device_id_type=MESH,
        )

    def to_far(step):
        return pltpu.make_async_remote_copy(
            src_ref=far_out.at[step], dst_ref=far_in.at[step],
            send_sem=far_send.at[step], recv_sem=far_recv.at[step],
            device_id=far, device_id_type=MESH,
        )

    def sum_up_start(step):
        to_mate(step).wait_recv()
        far_out[step] = (acc[...] + core_in[step].astype(F32)).astype(BF)
        to_far(step).start()

    def sum_up_end(step):
        to_far(step).wait_recv()
        return far_out[step].astype(F32) + far_in[step].astype(F32)

    def finish_sends(step, ref):
        share_rows(ref, step).wait_send()
        to_mate(step).wait_send()
        to_far(step).wait_send()

    scale = hd ** -0.5

    def attention_page(l, k, slot):
        rows = nn(normed[k, slot], wqkv_ref[l])
        rows = rows + qvb_ref[l : l + 1, :]
        qkv[l, slot] = rows.astype(BF)
        for h in range(lay.heads):
            q = qkv[l, slot, :, h * hd : (h + 1) * hd]
            kk = qkv[l, slot, :, own + h * hd : own + (h + 1) * hd]
            vv = qkv[l, slot, :, 2 * own + h * hd : 2 * own + (h + 1) * hd]
            s = nt(q, kk) * scale + bias_ref[l * lay.heads + h, :, :prow].astype(F32)
            e = jnp.exp(s - jnp.max(s, -1, keepdims=True))
            p = (e / jnp.sum(e, -1, keepdims=True)).astype(BF)
            probs[l, slot, h] = p
            ctx[l, slot, :, h * hd : (h + 1) * hd] = nn(p, vv).astype(BF)
        return nn(ctx[l, slot], wout_ref[l])

    def mlp_page(l, k, slot):
        pre = nn(normed[k, slot], wup_ref[l]) + upb_ref[l : l + 1, :]
        c0, c1 = 0.7978845608028654, 0.044715
        square = pre * pre
        t = jnp.tanh(c0 * (pre + c1 * pre * square))
        act[l, slot] = (0.5 * pre * (1.0 + t)).astype(BF)
        slope = 0.5 * (1.0 + t) + 0.5 * pre * (1.0 - t * t) * (c0 * (1.0 + 3.0 * c1 * square))
        gate[l, slot] = slope.astype(BF)
        return nn(act[l, slot], wdn_ref[l])

    v_buf[0] = x0_ref[...]
    for k in range(halves):
        l = k // 2
        x = v_buf[k].astype(F32)
        xhat, _ = norm_stats(x)
        normed[k, 0] = (xhat * vec(0, k) + vec(1, k)).astype(BF)
        share_rows(normed.at[k], k).start()
        page = attention_page if k % 2 == 0 else mlp_page
        acc[...] = page(l, k, 0)
        share_rows(normed.at[k], k).wait_recv()
        core_out[k] = page(l, k, 1).astype(BF)
        to_mate(k).start()
        sum_up_start(k)
        b = sum_up_end(k) + vec(3, k)
        branch[k] = b
        after = (v_buf[k].astype(F32) + vec(2, k) * b).astype(BF)
        if k + 1 < halves:
            v_buf[k + 1] = after
        else:
            v4_ref[...] = after
        finish_sends(k, normed.at[k])

    g_buf[...] = g4_ref[...].astype(F32)
    for k in reversed(range(halves)):
        l = k // 2
        step = halves + (halves - 1 - k)
        g = g_buf[...]
        add_small(lay.scale_at + k, column_sum(g * branch[k]))
        low = (g * vec(2, k)).astype(BF)
        bgrad[k, 0] = low
        share_rows(bgrad.at[k], step).start()
        add_small(lay.bias_at + k, column_sum(low.astype(F32)))

        def attention_back(slot):
            dctx = nt(bgrad[k, slot], wout_ref[l]).astype(BF)
            for h in range(lay.heads):
                q = qkv[l, slot, :, h * hd : (h + 1) * hd]
                kk = qkv[l, slot, :, own + h * hd : own + (h + 1) * hd]
                vv = qkv[l, slot, :, 2 * own + h * hd : 2 * own + (h + 1) * hd]
                dc = dctx[:, h * hd : (h + 1) * hd]
                low_p = probs[l, slot, h]
                p = low_p.astype(F32)
                dp = nt(dc, vv)
                ds = (p * (dp - jnp.sum(p * dp, -1, keepdims=True))).astype(BF)
                where_ds = (l * lay.heads + h) * 2 + slot
                ds_ref[where_ds, :, :prow] = ds.astype(F32)
                dqkv[slot, :, h * hd : (h + 1) * hd] = (nn(ds, kk) * scale).astype(BF)
                dqkv[slot, :, own + h * hd : own + (h + 1) * hd] = (tn(ds, q) * scale).astype(BF)
                dqkv[slot, :, 2 * own + h * hd : 2 * own + (h + 1) * hd] = tn(low_p, dc).astype(BF)
            return nt(dqkv[slot], wqkv_ref[l])

        def mlp_back(slot):
            dact = nt(bgrad[k, slot], wdn_ref[l])
            dqkv_or = (dact * gate[l, slot].astype(F32)).astype(BF)
            gate[l, slot] = dqkv_or
            return nt(dqkv_or, wup_ref[l])

        page = attention_back if k % 2 == 0 else mlp_back
        acc[...] = page(0)
        share_rows(bgrad.at[k], step).wait_recv()
        core_out[step] = page(1).astype(BF)
        to_mate(step).start()
        sum_up_start(step)

        both = 2 * prow
        bg = bgrad[k].reshape(both, width)
        nm = normed[k].reshape(both, width)
        if k % 2 == 0:
            dall = dqkv[...].reshape(both, 3 * own)
            gout_ref[l] = tn(ctx[l].reshape(both, own), bg).astype(BF)
            gqkv_ref[l] = tn(nm, dall).astype(BF)
            sums = column_sum(dall.astype(F32))
            add_small(lay.qv_at + l, sums[:, :own], slice(0, own))
            add_small(lay.qv_at + l, sums[:, 2 * own :], slice(2 * LANES, 2 * LANES + own))
        else:
            dpre = gate[l].reshape(both, hid)
            gdn_ref[l] = tn(act[l].reshape(both, hid), bg).astype(BF)
            gup_ref[l] = tn(nm, dpre).astype(BF)
            add_small(lay.up_at + l, column_sum(dpre.astype(F32)))

        ng = sum_up_end(step)
        xhat, r = norm_stats(v_buf[k].astype(F32))
        add_small(lay.gain_at + k, column_sum(ng * xhat))
        add_small(lay.shift_at + k, column_sum(ng))
        t = ng * vec(0, k)
        inner = t - jnp.mean(t, -1, keepdims=True) - xhat * jnp.mean(t * xhat, -1, keepdims=True)
        g = g_buf[...] + r * inner
        if k > 0:
            g_buf[...] = g.astype(BF).astype(F32)
        else:
            g0_ref[...] = g * (1.0 - mask_ref[...])
            add_small(lay.token_at, column_sum(g * mask_ref[...]))
        finish_sends(step, bgrad.at[k])


def run_blocks(lay, *operands):
    L, prow, width, own, hid = lay.layers, lay.prow, lay.width, lay.own, lay.hidden
    halves, steps = lay.halves, 2 * lay.halves
    pcol = operands[6].shape[2]
    shape = jax.ShapeDtypeStruct
    rows = (prow, width)
    return pl.pallas_call(
        functools.partial(blocks_kernel, lay),
        out_shape=(
            shape(rows, BF), shape(rows, F32), shape((lay.smalls, width), F32),
            shape((2 * L * lay.heads, prow, pcol), F32),
            shape((L, width, 3 * own), BF), shape((L, own, width), BF),
            shape((L, width, hid), BF), shape((L, hid, width), BF),
        ),
        in_specs=[pl.BlockSpec(memory_space=pltpu.VMEM)] * 11,
        out_specs=[pl.BlockSpec(memory_space=pltpu.VMEM)] * 8,
        scratch_shapes=[
            pltpu.VMEM((halves,) + rows, BF),
            pltpu.VMEM((halves, 2) + rows, BF),
            pltpu.VMEM((halves,) + rows, F32),
            pltpu.VMEM((L, 2, prow, 3 * own), BF),
            pltpu.VMEM((L, 2, lay.heads, prow, prow), BF),
            pltpu.VMEM((L, 2, prow, own), BF),
            pltpu.VMEM((L, 2, prow, hid), BF),
            pltpu.VMEM((L, 2, prow, hid), BF),
            pltpu.VMEM((halves, 2) + rows, BF),
            pltpu.VMEM((2, prow, 3 * own), BF),
            pltpu.VMEM(rows, F32),
            pltpu.VMEM(rows, F32),
            pltpu.VMEM((steps,) + rows, BF),
            pltpu.VMEM((steps,) + rows, BF),
            pltpu.VMEM((steps,) + rows, BF),
            pltpu.VMEM((steps,) + rows, BF),
        ] + [pltpu.SemaphoreType.DMA((steps,))] * 6,
        compiler_params=pltpu.CompilerParams(
            collective_id=1, has_side_effects=True, vmem_limit_bytes=60 * 2**20
        ),
        name="blocks",
        cost_estimate=pl.CostEstimate(flops=9 * 10**9, bytes_accessed=2 * 10**7, transcendentals=10**7),
    )(*operands)


def per_device(
    patches, page_mask, mask_token, buckets, ln_gain, ln_shift, layer_scale, branch_bias,
    qkv_weight, qv_bias, out_weight, rel_table, up_weight, up_bias, down_weight, cotangent,
):
    section = lax.axis_index("section")
    sections = lax.axis_size("section")
    dp = lax.axis_index("dp")
    ranks = lax.axis_size("dp")
    core = lax.rem(section, 2)
    layers = qkv_weight.shape[0]
    pages, rows, width = patches.shape
    all_heads = rel_table.shape[1]
    bucket_count = rel_table.shape[2]
    head = width // all_heads
    heads = all_heads // sections
    own = heads * head
    hidden = up_weight.shape[2]
    hid = hidden // sections
    prow, pcol = pad_up(rows, 16), pad_up(rows, LANES)
    highs = pad_up(bucket_count, LANES) // LANES
    lay = Layout(layers, heads, head, rows, prow, width, hid)
    halves = 2 * layers

    unit = down_weight.shape[1] // sections
    shard = qkv_weight.shape[1]

    def pick(x, axis):
        return lax.dynamic_index_in_dim(x, section, axis, keepdims=False)

    qkv_own = pick(qkv_weight.reshape(layers, shard, 3, sections, own), 3).reshape(layers, shard, 3 * own)
    up_own = pick(up_weight.reshape(layers, shard, ranks, sections, unit), 3).reshape(layers, shard, hid)
    dn_own = pick(down_weight.reshape(layers, sections, unit, width), 1)

    def gathered(x):
        return lax.all_gather(x, "dp", axis=1, tiled=True)

    wqkv, wup, wdn = gathered(qkv_own), gathered(up_own), gathered(dn_own)
    wout = pick(gathered(out_weight).reshape(layers, sections, own, width), 1)

    vecs = jnp.concatenate([ln_gain, ln_shift, layer_scale, branch_bias], 0)
    vecs = lax.all_gather(vecs, "section", axis=1, tiled=False).reshape(4 * halves, width).astype(F32)
    qv_own = pick(qv_bias.reshape(layers, 2, sections, own), 2).astype(F32)
    qv_vec = jnp.concatenate([qv_own[:, 0], jnp.zeros_like(qv_own[:, 0]), qv_own[:, 1]], 1)
    upb_own = pick(up_bias.reshape(layers, ranks, sections, unit), 2).reshape(layers, hid).astype(F32)

    tables = pick(rel_table.reshape(layers, sections, heads, bucket_count), 1).astype(F32)
    tables = jnp.pad(tables, ((0, 0), (0, 0), (0, highs * LANES - bucket_count)))
    tables = tables.reshape(layers * heads, highs, LANES)
    ids = jnp.pad(buckets, ((0, prow - rows), (0, pcol - rows)))
    bias = position_bias(ids, tables, rows)

    def page_of(x):
        return lax.dynamic_index_in_dim(x, core, 0, keepdims=False)

    mask_own = page_of(page_mask)[:, None]
    x0 = jnp.where(mask_own == 1, mask_token, page_of(patches))
    x0 = jnp.pad(x0, ((0, prow - rows), (0, 0)))
    g4 = jnp.pad(page_of(cotangent), ((0, prow - rows), (0, 0)))
    mask_f = jnp.pad((mask_own == 1).astype(F32), ((0, prow - rows), (0, 0)))

    v4, g0, small, ds, gqkv, gout, gup, gdn = run_blocks(
        lay, x0, g4, mask_f, vecs, qv_vec, upb_own, bias, wqkv, wout, wup, wdn
    )

    def scattered(x):
        return lax.psum_scatter(x, "dp", scatter_dimension=1, tiled=True)

    sqkv, sup, sdn = scattered(gqkv), scattered(gup), scattered(gdn)

    def everywhere(x, axis):
        return lax.all_gather(x, "section", axis=axis, tiled=False)

    qkv_all = everywhere(sqkv.reshape(layers, shard, 3, own), 3).reshape(layers, shard, 3 * width)
    qkv_cols = 3 * width // sections
    qkv_out = lax.dynamic_slice_in_dim(qkv_all, section * qkv_cols, qkv_cols, 2).astype(F32)
    up_all = everywhere(sup.reshape(layers, shard, ranks, unit), 3).reshape(layers, shard, hidden)
    up_out = lax.dynamic_slice_in_dim(up_all, section * hid, hid, 2).astype(F32)
    cols = width // sections
    dn_all = lax.all_to_all(
        sdn.reshape(layers, unit, sections, cols), "section", split_axis=2, concat_axis=1, tiled=False
    )
    dn_out = dn_all.reshape(layers, sections * unit, cols).astype(F32)
    out_full = everywhere(gout, 1).reshape(layers, width, width)
    out_mine = lax.psum_scatter(out_full, "dp", scatter_dimension=1, tiled=True)
    out_out = lax.dynamic_slice_in_dim(out_mine, section * cols, cols, 2).astype(F32)

    def pages_of(x):
        both = lax.all_gather(x[:rows], "section", axis=0, tiled=False)[:pages]
        return lax.dynamic_slice_in_dim(both, section * cols, cols, 2)

    block_out = pages_of(v4)
    input_out = pages_of(g0)

    sums = bucket_sums(ids, ds, rows, highs)
    sums = sums.reshape(highs, layers, heads, 2, LANES).sum(3)
    table_own = sums.transpose(1, 2, 0, 3).reshape(layers, heads, highs * LANES)[:, :, :bucket_count]

    once = (section < 2).astype(F32)
    replicated = small[: 4 * halves] * once
    token = small[lay.token_at] * once
    qv_rows = small[lay.qv_at : lay.qv_at + layers]
    qv_pair = jnp.stack([qv_rows[:, :own], qv_rows[:, 2 * LANES : 2 * LANES + own]], 1)
    here = (jnp.arange(sections) == section).astype(F32)
    qv_full = (qv_pair[:, :, None, :] * here[None, None, :, None]).reshape(layers, 2 * width)
    up_rows = small[lay.up_at : lay.up_at + layers].reshape(layers, ranks, 1, unit)
    up_full = (up_rows * here[None, None, :, None]).reshape(layers, hidden)
    table_full = (table_own[:, None] * here[None, :, None, None]).reshape(layers, all_heads, bucket_count)
    replicated, token, qv_total, up_total, table_total = lax.psum(
        (replicated, token, qv_full, up_full, table_full), ("section", "dp")
    )

    def own_row(at):
        return lax.dynamic_slice_in_dim(replicated, at + section, 1, 0)

    return (
        block_out, input_out, qkv_out, out_out, up_out, dn_out,
        qv_total, up_total, table_total,
        own_row(lay.gain_at), own_row(lay.shift_at), own_row(lay.scale_at), own_row(lay.bias_at),
        token,
    )


def solution(mesh):
    rows3 = P("dp", None, None)
    part = P("section", None)
    weight = P(None, "dp", None)
    in_specs = (
        rows3, P("dp", None), P(), P(), part, part, part, part,
        weight, P(), weight, P(), weight, P(), weight, rows3,
    )
    cut = P("dp", None, "section")
    grad = P(None, "dp", "section")
    out_specs = (cut, cut, grad, grad, grad, grad, P(), P(), P(), part, part, part, part, P())
    return jax.shard_map(per_device, mesh=mesh, in_specs=in_specs, out_specs=out_specs, check_vma=False)
```

```python
import functools

import jax
import jax.numpy as jnp
from jax import lax
from jax.experimental import pallas as pl
from jax.experimental.pallas import tpu as pltpu
from jax.sharding import PartitionSpec as P

EPS = 1e-06
MESH = pl.DeviceIdType.MESH
NEG = -1e30
LANES = 128
BF = jnp.bfloat16
F32 = jnp.float32


def pad_up(x, m):
    return (x + m - 1) // m * m


def nn(a, b):
    return jnp.dot(a, b, preferred_element_type=F32)


def nt(a, b):
    return lax.dot_general(a, b, (((1,), (1,)), ((), ())), preferred_element_type=F32)


def tn(a, b):
    return lax.dot_general(a, b, (((0,), (0,)), ((), ())), preferred_element_type=F32)


def bias_kernel(rows, buckets_ref, table_ref, out_ref):
    tables, highs, _ = table_ref.shape
    prow, pcol = buckets_ref.shape
    step = 16

    def body(block, carry):
        at = pl.multiple_of(block * step, step)
        for half in range(pcol // LANES):
            ids = buckets_ref[pl.ds(at, step), half * LANES : (half + 1) * LANES]
            low = ids & (LANES - 1)
            high = lax.shift_right_logical(ids, 7)
            column = lax.broadcasted_iota(jnp.int32, (step, LANES), 1) + half * LANES
            inside = column < rows
            picks = [high == number for number in range(highs)]
            for t in range(tables):
                value = jnp.full((step, LANES), NEG, F32)
                for number in range(highs):
                    row = jnp.broadcast_to(table_ref[t, number : number + 1, :], (step, LANES))
                    got = jnp.take_along_axis(row, low, axis=1)
                    value = jnp.where(picks[number], got, value)
                value = jnp.where(inside, value, NEG)
                out_ref[t, pl.ds(at, step), half * LANES : (half + 1) * LANES] = value.astype(BF)
        return carry

    lax.fori_loop(0, prow // step, body, 0)


def position_bias(buckets, tables, rows):
    return pl.pallas_call(
        functools.partial(bias_kernel, rows),
        out_shape=jax.ShapeDtypeStruct((tables.shape[0],) + buckets.shape, BF),
        in_specs=[pl.BlockSpec(memory_space=pltpu.VMEM)] * 2,
        out_specs=pl.BlockSpec(memory_space=pltpu.VMEM),
        name="position_bias",
        cost_estimate=pl.CostEstimate(flops=10**7, bytes_accessed=10**6, transcendentals=0),
    )(buckets, tables)


class Layout:
    def __init__(self, layers, heads, head, rows, prow, width, hidden, shard, highs, fused):
        self.layers, self.heads, self.head = layers, heads, head
        self.rows, self.prow, self.width, self.hidden = rows, prow, width, hidden
        self.shard, self.highs, self.fused = shard, highs, fused
        self.own = heads * head
        self.halves = 2 * layers
        self.scale_at, self.bias_at, self.gain_at, self.shift_at, self.token_at = range(5)
        self.qv_at, self.up_at, self.table_at = 0, layers, 2 * layers
        self.sec_rows = pad_up(2 * layers + layers * heads, 8)


def norm_stats(x):
    mean = jnp.mean(x, -1, keepdims=True)
    centered = x - mean
    r = lax.rsqrt(jnp.mean(centered * centered, -1, keepdims=True) + EPS)
    return centered * r, r


ITEMS = ("qkv", "out", "up", "dn")


def blocks_kernel(lay, names, *refs):
    r = dict(zip(names, refs))
    fused = lay.fused
    section = lax.axis_index("section")
    core = lax.rem(section, 2)
    mate_at = section + 1 - 2 * core
    mate = {"section": mate_at}
    far = {"section": lax.rem(section + 2, 4)}
    layers, halves, prow, width = lay.layers, lay.halves, lay.prow, lay.width
    own, hid, hd, heads, shard = lay.own, lay.hidden, lay.head, lay.heads, lay.shard
    v_buf, normed, branch, qkv, probs = r["v_buf"], r["normed"], r["branch"], r["qkv"], r["probs"]
    ctx, act, gate, bgrad, dqkv = r["ctx"], r["act"], r["gate"], r["bgrad"], r["dqkv"]
    acc, g_buf, ds_ref, bias_ref = r["acc"], r["g_buf"], r["ds"], r["bias"]
    tiles, sec, vec_all = r["tiles"], r["sec"], r["vec_all"]
    core_out, core_in, far_out, far_in = r["core_out"], r["core_in"], r["far_out"], r["far_in"]

    def remote(src, dst, send, recv, device):
        return pltpu.make_async_remote_copy(
            src_ref=src, dst_ref=dst, send_sem=send, recv_sem=recv, device_id=device, device_id_type=MESH
        )

    partners = [mate, far]
    if fused:
        dp = lax.axis_index("dp")
        zi, xi = dp // 2, lax.rem(dp, 2)
        xmate = {"dp": zi * 2 + 1 - xi}
        znext = [lax.rem(zi + o, 4) for o in (1, 2, 3)]
        zprev = [lax.rem(zi + 4 - o, 4) for o in (1, 2, 3)]
        zdev = [{"dp": z * 2 + xi} for z in znext]
        snext = [lax.rem(section + o, 4) for o in (1, 2, 3)]
        sprev = [lax.rem(section + 4 - o, 4) for o in (1, 2, 3)]
        sdev = [{"section": t} for t in snext]
        partners = [xmate] + zdev + sdev

    barrier = pltpu.get_barrier_semaphore()
    for other in partners:
        pl.semaphore_signal(barrier, inc=1, device_id=other, device_id_type=MESH)
    pl.semaphore_wait(barrier, len(partners))

    sends = []

    def sent(copy, when=None):
        sends.append((copy, when))

    if fused:
        zs, zr, xs, xr, ls = r["ag_zs"], r["ag_zr"], r["ag_xs"], r["ag_xr"], r["ag_ls"]
        my_out = zi == section

        def item(n):
            l, kind = n // 4, ITEMS[n % 4]
            return l, kind, r["a_" + kind].at[l], r["w_" + kind]

        def gather_z(n):
            l, kind, src, dst = item(n)
            if kind == "out":
                for o in range(3):
                    copy = remote(src, dst.at[l, xi], zs.at[n, o], zr.at[n, 0], zdev[o])
                    pl.when(my_out)(copy.start)
                    sent(copy, my_out)
                pl.when(my_out)(pltpu.make_async_copy(src, dst.at[l, xi], ls.at[n]).start)
                return
            for o in range(3):
                copy = remote(src, dst.at[l, zi, xi], zs.at[n, o], zr.at[n, o], zdev[o])
                copy.start()
                sent(copy)
            pltpu.make_async_copy(src, dst.at[l, zi, xi], ls.at[n]).start()

        def gather_x_own(n):
            l, kind, src, dst = item(n)
            if kind == "out":
                copy = remote(src, dst.at[l, xi], xs.at[n, 0], xr.at[n, 0], xmate)
                pl.when(my_out)(copy.start)
            else:
                copy = remote(src, dst.at[l, zi, xi], xs.at[n, 3], xr.at[n, 3], xmate)
                copy.start()
                sent(copy)

        def pump(n):
            l, kind, src, dst = item(n)
            if kind == "out":
                away = jnp.logical_not(my_out)
                copy = remote(dst.at[l, xi], dst.at[l, xi], xs.at[n, 0], xr.at[n, 0], xmate)

                @pl.when(away)
                def _():
                    remote(src, dst.at[l, xi], zs.at[n, 0], zr.at[n, 0], zdev[0]).wait_recv()
                    copy.start()

                sent(copy)
            else:
                for o in range(3):
                    block = dst.at[l, zprev[o], xi]
                    remote(src, block, zs.at[n, o], zr.at[n, o], zdev[o]).wait_recv()
                    copy = remote(block, block, xs.at[n, o], xr.at[n, o], xmate)
                    copy.start()
                    sent(copy)

        def need(n):
            l, kind, src, dst = item(n)
            if kind == "out":
                pl.when(my_out)(pltpu.make_async_copy(src, dst.at[l, xi], ls.at[n]).wait)
                remote(src, dst.at[l, 1 - xi], xs.at[n, 0], xr.at[n, 0], xmate).wait_recv()
                return
            pltpu.make_async_copy(src, dst.at[l, zi, xi], ls.at[n]).wait()
            for o in range(3):
                block = dst.at[l, zprev[o], 1 - xi]
                remote(src, block, xs.at[n, o], xr.at[n, o], xmate).wait_recv()
            remote(src, dst.at[l, zi, 1 - xi], xs.at[n, 3], xr.at[n, 3], xmate).wait_recv()

        vec_all[section] = r["vec_own"][...]
        vec_copies = [
            remote(r["vec_own"], vec_all.at[section], r["vec_s"].at[o], r["vec_r"].at[o], sdev[o])
            for o in range(3)
        ]
        for copy in vec_copies:
            copy.start()
            sent(copy)
        count = 4 * layers
        for n in range(count):
            gather_z(n)
        for n in range(3):
            gather_x_own(n)
        pumped = 3

        def pump_next(n):
            pump(n)
            if n + 3 < count:
                gather_x_own(n + 3)

        for o in range(3):
            remote(r["vec_own"], vec_all.at[sprev[o]], r["vec_s"].at[o], r["vec_r"].at[o], sdev[o]).wait_recv()
    else:
        need = pump_next = lambda n: None

    def weight(kind, l):
        w = r["w_" + kind][l]
        return w.reshape(-1, w.shape[-1])

    tiles[...] = jnp.zeros_like(tiles)
    sec[...] = jnp.zeros_like(sec)

    def column_sum(x):
        return jnp.sum(x, 0, keepdims=True)

    def vec(kind, k):
        return vec_all[k, kind : kind + 1, :]

    def share_rows(ref, step):
        return remote(ref.at[0], ref.at[1], r["row_s"].at[step], r["row_r"].at[step], mate)

    def to_mate(step):
        return remote(core_out, core_in.at[step % 2], r["core_s"].at[step], r["core_r"].at[step], mate)

    def to_far(step):
        return remote(far_out, far_in.at[step % 2], r["far_s"].at[step], r["far_r"].at[step], far)

    def sum_up_start(step):
        to_mate(step).wait_recv()
        far_out[...] = (acc[...] + core_in[step % 2].astype(F32)).astype(BF)
        to_far(step).start()

    def sum_up_end(step):
        to_far(step).wait_recv()
        return far_out[...].astype(F32) + far_in[step % 2].astype(F32)

    def finish_sends(step, ref):
        share_rows(ref, step).wait_send()
        to_mate(step).wait_send()
        to_far(step).wait_send()

    scale = hd ** -0.5

    def attention_page(l, k, slot):
        rows = nn(normed[k, slot], weight("qkv", l))
        rows = rows + r["qvb"][l : l + 1, :]
        qkv[l, slot] = rows.astype(BF)
        for h in range(heads):
            q = qkv[l, slot, :, h * hd : (h + 1) * hd]
            kk = qkv[l, slot, :, own + h * hd : own + (h + 1) * hd]
            vv = qkv[l, slot, :, 2 * own + h * hd : 2 * own + (h + 1) * hd]
            s = nt(q, kk) * scale + bias_ref[l * heads + h, :, :prow].astype(F32)
            e = jnp.exp(s - jnp.max(s, -1, keepdims=True))
            p = (e / jnp.sum(e, -1, keepdims=True)).astype(BF)
            probs[l, slot, h] = p
            ctx[l, slot, :, h * hd : (h + 1) * hd] = nn(p, vv).astype(BF)
        if slot == 0:
            need(4 * l + 1)
        return nn(ctx[l, slot], weight("out", l))

    def mlp_page(l, k, slot):
        pre = nn(normed[k, slot], weight("up", l)) + r["upb"][l : l + 1, :]
        c0, c1 = 0.7978845608028654, 0.044715
        square = pre * pre
        t = jnp.tanh(c0 * (pre + c1 * pre * square))
        act[l, slot] = (0.5 * pre * (1.0 + t)).astype(BF)
        slope = 0.5 * (1.0 + t) + 0.5 * pre * (1.0 - t * t) * (c0 * (1.0 + 3.0 * c1 * square))
        gate[l, slot] = slope.astype(BF)
        if slot == 0:
            pump_next(4 * l + 3)
            need(4 * l + 3)
        return nn(act[l, slot], weight("dn", l))

    v_buf[0] = r["x0"][...]
    for k in range(halves):
        l = k // 2
        x = v_buf[k].astype(F32)
        xhat, _ = norm_stats(x)
        normed[k, 0] = (xhat * vec(0, k) + vec(1, k)).astype(BF)
        share_rows(normed.at[k], k).start()
        if k % 2 == 0:
            pump_next(4 * l)
            pump_next(4 * l + 1)
            need(4 * l)
            page = attention_page
        else:
            need(4 * l + 2)
            page = mlp_page
        acc[...] = page(l, k, 0)
        share_rows(normed.at[k], k).wait_recv()
        core_out[...] = page(l, k, 1).astype(BF)
        to_mate(k).start()
        sum_up_start(k)
        if k % 2 == 0:
            pump_next(4 * l + 2)
        b = sum_up_end(k) + vec(3, k)
        branch[k] = b
        after = (v_buf[k].astype(F32) + vec(2, k) * b).astype(BF)
        if k + 1 < halves:
            v_buf[k + 1] = after
        finish_sends(k, normed.at[k])

    if fused:
        cols = own

        def share_page(value, name):
            out = r[name + "_s"]
            for t in range(4):
                out[t] = value[:, t * cols : (t + 1) * cols]
            copy = remote(
                out.at[mate_at], r[name + "_r"], r["page_s"].at[int(name == "pg")], r["page_r"].at[int(name == "pg")], mate
            )
            copy.start()
            sent(copy)
            return copy

        v_copy = share_page(after, "pv")
    else:
        r["v4"][...] = after

    if fused:
        rs_xs, rs_xr, rs_zs, rs_zr = r["rs_xs"], r["rs_xr"], r["rs_zs"], r["rs_zr"]
        rs_ss, rs_sr = r["rs_ss"], r["rs_sr"]

        def reduce_x(n):
            l, kind = n // 4, ITEMS[n % 4]
            part = r["g_" + kind]
            src = part.at[l, 1 - xi] if kind == "out" else part.at[l, :, 1 - xi]
            return remote(src, r["x_" + kind].at[l], rs_xs.at[n], rs_xr.at[n], xmate)

        def reduce_x_start(n):
            copy = reduce_x(n)
            copy.start()
            sent(copy)

        def reduce_z_start(n):
            l, kind = n // 4, ITEMS[n % 4]
            reduce_x(n).wait_recv()
            pair, part = r["x_" + kind], r["g_" + kind]
            mine = part[l, xi] if kind == "out" else part[l, :, xi]
            pair[l] = (mine.astype(F32) + pair[l].astype(F32)).astype(BF)
            if kind == "out":
                for o in range(3):
                    ours = znext[o] == section
                    copy = remote(pair.at[l], r["z_out"].at[l, o], rs_zs.at[n, 0], rs_zr.at[n, o], zdev[o])
                    pl.when(ours)(copy.start)
                    sent(copy, ours)
                return
            for o in range(3):
                copy = remote(pair.at[l, znext[o]], r["z_" + kind].at[l, o], rs_zs.at[n, o], rs_zr.at[n, o], zdev[o])
                copy.start()
                sent(copy)

        def z_arrival(n, o):
            l, kind = n // 4, ITEMS[n % 4]
            src = r["x_out"].at[l] if kind == "out" else r["x_" + kind].at[l, 0]
            remote(src, r["z_" + kind].at[l, o], rs_zs.at[n, o], rs_zr.at[n, o], zdev[o]).wait_recv()

        def to_section(n, o, src, dst, device):
            return remote(src, dst, rs_ss.at[n, o], rs_sr.at[n, o], device)

        def qkv_place(m):
            at = 4 * m + section
            return at // 3, lax.rem(at, 3)

        def finish_item(n):
            l, kind = n // 4, ITEMS[n % 4]
            blocks, got = r["s_" + kind], r["t_" + kind]
            if kind == "out":

                @pl.when(my_out)
                def _():
                    total = r["x_out"][l].astype(F32)
                    for o in range(3):
                        z_arrival(n, o)
                        total = total + r["z_out"][l, o].astype(F32)
                    for t in range(4):
                        blocks[l, t] = total[:, t * cols : (t + 1) * cols].astype(BF)
                    for o in range(3):
                        to_section(n, o, blocks.at[l, snext[o]], got.at[l], sdev[o]).start()
                    got[l] = blocks[l, section]

                for o in range(3):
                    sent(to_section(n, o, blocks.at[l, snext[o]], got.at[l], sdev[o]), my_out)
                return
            total = r["x_" + kind][l, zi].astype(F32)
            for o in range(3):
                z_arrival(n, o)
                total = total + r["z_" + kind][l, o].astype(F32)
            for t in range(3 if kind == "qkv" else 4):
                blocks[l, t] = total[:, t * cols : (t + 1) * cols].astype(BF)
            if kind == "qkv":
                for m in range(3):
                    dest, place = qkv_place(m)
                    away = dest != section
                    copy = remote(
                        blocks.at[l, m], got.at[l, place], rs_ss.at[n, m], rs_sr.at[n, place], {"section": dest}
                    )
                    pl.when(away)(copy.start)
                    sent(copy, away)

                    @pl.when(jnp.logical_not(away))
                    def _():
                        got[l, place] = blocks[l, m]

                return
            for o in range(3):
                copy = to_section(n, o, blocks.at[l, snext[o]], got.at[l, section], sdev[o])
                copy.start()
                sent(copy)
            got[l, section] = blocks[l, section]

        def store_item(n):
            l, kind = n // 4, ITEMS[n % 4]
            blocks, got, out = r["s_" + kind], r["t_" + kind], r["o_" + kind]
            if kind == "out":
                for o in range(3):
                    copy = to_section(n, o, blocks.at[l, 0], got.at[l], sdev[o])
                    pl.when(sprev[o] == zi)(copy.wait_recv)
                out[l] = got[l].astype(F32)
            elif kind == "qkv":
                for place in range(3):
                    source = lax.rem(3 * section + place, 4)
                    copy = to_section(n, place, blocks.at[l, 0], got.at[l, place], mate)
                    pl.when(source != section)(copy.wait_recv)
                out[l] = jnp.concatenate([got[l, place].astype(F32) for place in range(3)], 1)
            else:
                for o in range(3):
                    to_section(n, o, blocks.at[l, 0], got.at[l, sprev[o]], sdev[o]).wait_recv()
                if kind == "dn":
                    out[l] = got[l].astype(F32).reshape(out.shape[1:])
                else:
                    unit = cols // 2
                    out[l] = jnp.concatenate(
                        [got[l, t, :, half * unit : (half + 1) * unit].astype(F32) for half in range(2) for t in range(4)], 1
                    )
    else:
        reduce_x_start = reduce_z_start = finish_item = lambda n: None

    def keep_grad(kind, l, value):
        ref = r["g_" + kind]
        ref[l] = value.astype(BF).reshape(ref.shape[1:])
        reduce_x_start(4 * l + ITEMS.index(kind))

    def table_sums(l):
        groups = 2 * heads
        count = lay.highs * groups
        hist = r["hist"]
        hist[...] = jnp.zeros_like(hist)
        step = 8
        pcol = ds_ref.shape[2]

        def body(block, carry):
            at = pl.multiple_of(block * step, step)
            ids_all = r["ids"][pl.ds(at, step), :]
            grads_all = ds_ref[l * groups : (l + 1) * groups, pl.ds(at, step), :]
            total = None
            for row in range(step):
                ids = ids_all[row : row + 1, :]
                low = ids & (LANES - 1)
                high = lax.shift_right_logical(ids, 7)
                spots = lax.broadcasted_iota(jnp.int32, (LANES, pcol), 0)
                hot = jnp.where(spots == low, 1.0, 0.0).astype(BF)
                grads = grads_all[:, row, :]
                parts = [jnp.where(high == number, grads, 0.0) for number in range(lay.highs)]
                got = nt(jnp.concatenate(parts, 0).astype(BF), hot)
                total = got if total is None else total + got
            hist[...] += total
            return carry

        lax.fori_loop(0, pad_up(lay.rows, step) // step, body, 0)
        for h in range(heads):
            at = lay.table_at + l * heads + h
            for number in range(lay.highs):
                first = number * groups + 2 * h
                row = hist[first : first + 1, :] + hist[first + 1 : first + 2, :]
                sec[at : at + 1, number * LANES : (number + 1) * LANES] = row

    g_buf[...] = r["g4"][...].astype(F32)
    ds_ref[...] = jnp.zeros_like(ds_ref)
    for k in reversed(range(halves)):
        l = k // 2
        step = halves + (halves - 1 - k)
        g = g_buf[...]
        tiles[k, lay.scale_at : lay.scale_at + 1, :] = column_sum(g * branch[k])
        low = (g * vec(2, k)).astype(BF)
        bgrad[k, 0] = low
        share_rows(bgrad.at[k], step).start()
        tiles[k, lay.bias_at : lay.bias_at + 1, :] = column_sum(low.astype(F32))

        def attention_back(slot):
            dctx = nt(bgrad[k, slot], weight("out", l)).astype(BF)
            for h in range(heads):
                q = qkv[l, slot, :, h * hd : (h + 1) * hd]
                kk = qkv[l, slot, :, own + h * hd : own + (h + 1) * hd]
                vv = qkv[l, slot, :, 2 * own + h * hd : 2 * own + (h + 1) * hd]
                dc = dctx[:, h * hd : (h + 1) * hd]
                low_p = probs[l, slot, h]
                p = low_p.astype(F32)
                dp_ = nt(dc, vv)
                ds = (p * (dp_ - jnp.sum(p * dp_, -1, keepdims=True))).astype(BF)
                ds_ref[(l * heads + h) * 2 + slot, :, :prow] = ds.astype(F32)
                dqkv[slot, :, h * hd : (h + 1) * hd] = (nn(ds, kk) * scale).astype(BF)
                dqkv[slot, :, own + h * hd : own + (h + 1) * hd] = (tn(ds, q) * scale).astype(BF)
                dqkv[slot, :, 2 * own + h * hd : 2 * own + (h + 1) * hd] = tn(low_p, dc).astype(BF)
            return nt(dqkv[slot], weight("qkv", l))

        def mlp_back(slot):
            dact = nt(bgrad[k, slot], weight("dn", l))
            dpre = (dact * gate[l, slot].astype(F32)).astype(BF)
            gate[l, slot] = dpre
            return nt(dpre, weight("up", l))

        page = attention_back if k % 2 == 0 else mlp_back
        acc[...] = page(0)
        share_rows(bgrad.at[k], step).wait_recv()
        core_out[...] = page(1).astype(BF)
        to_mate(step).start()
        sum_up_start(step)

        both = 2 * prow
        bg = bgrad[k].reshape(both, width)
        nm = normed[k].reshape(both, width)
        if k % 2 == 0:
            dall = dqkv[...].reshape(both, 3 * own)
            keep_grad("out", l, tn(ctx[l].reshape(both, own), bg))
            keep_grad("qkv", l, tn(nm, dall))
            sums = column_sum(dall.astype(F32))
            sec[lay.qv_at + l : lay.qv_at + l + 1, :own] = sums[:, :own]
            sec[lay.qv_at + l : lay.qv_at + l + 1, 2 * LANES : 2 * LANES + own] = sums[:, 2 * own :]
        else:
            dpre = gate[l].reshape(both, hid)
            keep_grad("dn", l, tn(act[l].reshape(both, hid), bg))
            keep_grad("up", l, tn(nm, dpre))
            sec[lay.up_at + l : lay.up_at + l + 1, :] = column_sum(dpre.astype(F32))
        if k + 1 < halves:
            for n in ((4 * (l + 1) + 1, 4 * (l + 1)) if k % 2 else (4 * l + 3, 4 * l + 2)):
                reduce_z_start(n)
        if k % 2 == 1 and l + 1 < layers:
            table_sums(l + 1)

        ng = sum_up_end(step)
        xhat, rr = norm_stats(v_buf[k].astype(F32))
        tiles[k, lay.gain_at : lay.gain_at + 1, :] = column_sum(ng * xhat)
        tiles[k, lay.shift_at : lay.shift_at + 1, :] = column_sum(ng)
        t = ng * vec(0, k)
        inner = t - jnp.mean(t, -1, keepdims=True) - xhat * jnp.mean(t * xhat, -1, keepdims=True)
        g = g_buf[...] + rr * inner
        if k > 0:
            g_buf[...] = g.astype(BF).astype(F32)
        finish_sends(step, bgrad.at[k])

    masked = r["mask"][...] > 0.5
    kept = jnp.where(masked, 0.0, g)
    token = column_sum(jnp.where(masked, g, 0.0))
    for k in range(halves):
        tiles[k, lay.token_at : lay.token_at + 1, :] = token

    if not fused:
        r["g0"][...] = kept
        table_sums(0)
        return

    g_copy = share_page(kept, "pg")
    table_sums(0)
    order = [n for l in reversed(range(layers)) for n in (4 * l + 3, 4 * l + 2, 4 * l + 1, 4 * l)]
    for n in order[-2:]:
        reduce_z_start(n)

    tile_copy = remote(tiles.at[mate_at], r["tile_in"], r["small_s"].at[0], r["small_r"].at[0], mate)
    tile_copy.start()
    sent(tile_copy)
    for n in order[:-2]:
        finish_item(n)
    tile_copy.wait_recv()
    red, red_in = r["red"], r["red_in"]
    red[0, :8] = tiles[section] + r["tile_in"][...]
    red[0, 8:] = sec[...]
    hops = [xmate, {"dp": (zi + 1 - 2 * lax.rem(zi, 2)) * 2 + xi}, {"dp": (3 - zi) * 2 + xi}]
    for hop in range(3):
        copy = remote(red.at[hop], red_in.at[hop], r["small_s"].at[1 + hop], r["small_r"].at[1 + hop], hops[hop])
        copy.start()
        sent(copy)
        if hop == 1:
            for n in order[-2:]:
                finish_item(n)
        copy.wait_recv()
        red[hop + 1] = red[hop] + red_in[hop]
    r["o_tile"][...] = red[3, :8]
    sec_all = r["o_sec"]
    mine = r["sec_sum"]
    mine[...] = red[3, 8:]
    sec_all[section] = mine[...]
    for o in range(3):
        copy = remote(mine, sec_all.at[section], r["sec_s"].at[o], r["sec_r"].at[o], sdev[o])
        copy.start()
        sent(copy)

    rows = lay.rows
    for name, copy, out in (("pv", v_copy, r["o_block"]), ("pg", g_copy, r["o_input"])):
        copy.wait_recv()
        out[core] = r[name + "_s"][section, :rows, :]
        out[1 - core] = r[name + "_r"][:rows, :]
    for n in order:
        store_item(n)
    for o in range(3):
        remote(mine, sec_all.at[sprev[o]], r["sec_s"].at[o], r["sec_r"].at[o], sdev[o]).wait_recv()
    for copy, when in sends:
        if when is None:
            copy.wait_send()
        else:
            pl.when(when)(copy.wait_send)


def run_blocks(lay, operands):
    L, prow, width, own, hid, shard = lay.layers, lay.prow, lay.width, lay.own, lay.hidden, lay.shard
    halves, steps, heads = lay.halves, 2 * lay.halves, lay.heads
    pcol = operands["bias"].shape[2]
    rows = (prow, width)
    groups = 2 * heads
    dma = pltpu.SemaphoreType.DMA
    outs, scratch = {}, {}
    items = 4 * L
    wide = {"qkv": 3 * own, "up": hid, "dn": width, "out": width}
    if lay.fused:
        outs["o_block"] = ((2, lay.rows, own), BF)
        outs["o_input"] = ((2, lay.rows, own), F32)
        outs["o_qkv"] = ((L, shard, 3 * own), F32)
        outs["o_out"] = ((L, shard, own), F32)
        outs["o_up"] = ((L, shard, hid), F32)
        outs["o_dn"] = ((L, 4 * shard, own), F32)
        outs["o_tile"] = ((8, width), F32)
        outs["o_sec"] = ((4, lay.sec_rows, width), F32)
        scratch["tiles"] = ((halves, 8, width), F32)
        scratch["sec"] = ((lay.sec_rows, width), F32)
        scratch["vec_all"] = ((halves, 8, width), F32)
        for kind, c in wide.items():
            lead = (2,) if kind == "out" else (4, 2)
            scratch["w_" + kind] = ((L,) + lead + (shard, c), BF)
            scratch["g_" + kind] = ((L,) + lead + (shard, c), BF)
            scratch["x_" + kind] = ((L,) + lead[:-1] + (shard, c), BF)
            scratch["z_" + kind] = ((L, 3, shard, c), BF)
            scratch["s_" + kind] = ((L, 3 if kind == "qkv" else 4, shard, own), BF)
            scratch["t_" + kind] = ((L,) + {"qkv": (3,), "out": ()}.get(kind, (4,)) + (shard, own), BF)
        scratch["pv_s"], scratch["pv_r"] = ((4, prow, own), BF), ((prow, own), BF)
        scratch["pg_s"], scratch["pg_r"] = ((4, prow, own), F32), ((prow, own), F32)
        scratch["tile_in"] = ((8, width), F32)
        scratch["red"] = ((4, 8 + lay.sec_rows, width), F32)
        scratch["red_in"] = ((3, 8 + lay.sec_rows, width), F32)
        scratch["sec_sum"] = ((lay.sec_rows, width), F32)
    else:
        outs["v4"] = (rows, BF)
        outs["g0"] = (rows, F32)
        outs["tiles"] = ((halves, 8, width), F32)
        outs["sec"] = ((lay.sec_rows, width), F32)
        outs["g_qkv"], outs["g_out"] = ((L, width, 3 * own), BF), ((L, own, width), BF)
        outs["g_up"], outs["g_dn"] = ((L, width, hid), BF), ((L, hid, width), BF)
    scratch.update(
        v_buf=((halves,) + rows, BF),
        normed=((halves, 2) + rows, BF),
        branch=((halves,) + rows, F32),
        qkv=((L, 2, prow, 3 * own), BF),
        probs=((L, 2, heads, prow, prow), BF),
        ctx=((L, 2, prow, own), BF),
        act=((L, 2, prow, hid), BF),
        gate=((L, 2, prow, hid), BF),
        bgrad=((halves, 2) + rows, BF),
        dqkv=((2, prow, 3 * own), BF),
        acc=(rows, F32),
        g_buf=(rows, F32),
        ds=((L * groups, prow, pcol), F32),
        hist=((lay.highs * groups, LANES), F32),
        core_out=(rows, BF),
        core_in=((2,) + rows, BF),
        far_out=(rows, BF),
        far_in=((2,) + rows, BF),
    )
    sems = {name: (steps,) for name in ("core_s", "core_r", "far_s", "far_r", "row_s", "row_r")}
    if lay.fused:
        sems.update(
            ag_zs=(items, 3), ag_zr=(items, 3), ag_xs=(items, 4), ag_xr=(items, 4), ag_ls=(items,),
            vec_s=(3,), vec_r=(3,), rs_xs=(items,), rs_xr=(items,), rs_zs=(items, 3), rs_zr=(items, 3),
            rs_ss=(items, 3), rs_sr=(items, 3), page_s=(2,), page_r=(2,), small_s=(4,), small_r=(4,),
            sec_s=(3,), sec_r=(3,),
        )
    names = list(operands) + list(outs) + list(scratch) + list(sems)
    results = pl.pallas_call(
        functools.partial(blocks_kernel, lay, names),
        out_shape=tuple(jax.ShapeDtypeStruct(*spec) for spec in outs.values()),
        in_specs=[pl.BlockSpec(memory_space=pltpu.VMEM)] * len(operands),
        out_specs=[pl.BlockSpec(memory_space=pltpu.VMEM)] * len(outs),
        scratch_shapes=[pltpu.VMEM(*spec) for spec in scratch.values()] + [dma(spec) for spec in sems.values()],
        compiler_params=pltpu.CompilerParams(
            collective_id=1, has_side_effects=True, vmem_limit_bytes=60 * 2**20
        ),
        name="blocks",
        cost_estimate=pl.CostEstimate(flops=9 * 10**9, bytes_accessed=2 * 10**7, transcendentals=10**7),
    )(*operands.values())
    return dict(zip(outs, results))


def per_device(
    patches, page_mask, mask_token, buckets, ln_gain, ln_shift, layer_scale, branch_bias,
    qkv_weight, qv_bias, out_weight, rel_table, up_weight, up_bias, down_weight, cotangent,
):
    section = lax.axis_index("section")
    sections = lax.axis_size("section")
    dp = lax.axis_index("dp")
    ranks = lax.axis_size("dp")
    core = lax.rem(section, 2)
    layers = qkv_weight.shape[0]
    pages, rows, width = patches.shape
    all_heads = rel_table.shape[1]
    bucket_count = rel_table.shape[2]
    head = width // all_heads
    heads = all_heads // sections
    own = heads * head
    hidden = up_weight.shape[2]
    hid = hidden // sections
    prow, pcol = pad_up(rows, 16), pad_up(rows, LANES)
    highs = pad_up(bucket_count, LANES) // LANES
    fused = ranks == 8 and sections == 4
    shard = qkv_weight.shape[1]
    lay = Layout(layers, heads, head, rows, prow, width, hid, shard, highs, fused)
    halves = 2 * layers

    unit = down_weight.shape[1] // sections

    def pick(x, axis):
        return lax.dynamic_index_in_dim(x, section, axis, keepdims=False)

    qkv_own = pick(qkv_weight.reshape(layers, shard, 3, sections, own), 3).reshape(layers, shard, 3 * own)
    up_own = pick(up_weight.reshape(layers, shard, ranks, sections, unit), 3).reshape(layers, shard, hid)
    dn_own = pick(down_weight.reshape(layers, sections, unit, width), 1)

    vecs = jnp.concatenate([ln_gain, ln_shift, layer_scale, branch_bias], 0).astype(F32)
    vecs = jnp.pad(vecs, ((0, 4), (0, 0)))
    qv_own = pick(qv_bias.reshape(layers, 2, sections, own), 2).astype(F32)
    qv_vec = jnp.concatenate([qv_own[:, 0], jnp.zeros_like(qv_own[:, 0]), qv_own[:, 1]], 1)
    upb_own = pick(up_bias.reshape(layers, ranks, sections, unit), 2).reshape(layers, hid).astype(F32)

    tables = pick(rel_table.reshape(layers, sections, heads, bucket_count), 1).astype(F32)
    tables = jnp.pad(tables, ((0, 0), (0, 0), (0, highs * LANES - bucket_count)))
    tables = tables.reshape(layers * heads, highs, LANES)
    ids = jnp.pad(buckets, ((0, prow - rows), (0, pcol - rows)))
    bias = position_bias(ids, tables, rows)

    def page_of(x):
        return lax.dynamic_index_in_dim(x, core, 0, keepdims=False)

    mask_own = page_of(page_mask)[:, None]
    x0 = jnp.where(mask_own == 1, mask_token, page_of(patches))
    x0 = jnp.pad(x0, ((0, prow - rows), (0, 0)))
    g4 = jnp.pad(page_of(cotangent), ((0, prow - rows), (0, 0)))
    mask_f = jnp.pad((mask_own == 1).astype(F32), ((0, prow - rows), (0, 0)))

    operands = dict(x0=x0, g4=g4, mask=mask_f, qvb=qv_vec, upb=upb_own, bias=bias, ids=ids)
    cols = width // sections

    def assembled(sec_all):
        qv = sec_all[:, lay.qv_at : lay.qv_at + layers]
        qv = jnp.stack([qv[..., :own], qv[..., 2 * LANES : 2 * LANES + own]], 2)
        qv = qv.transpose(1, 2, 0, 3).reshape(layers, 2 * width)
        up = sec_all[:, lay.up_at : lay.up_at + layers].reshape(sections, layers, ranks, unit)
        up = up.transpose(1, 2, 0, 3).reshape(layers, hidden)
        table = sec_all[:, lay.table_at : lay.table_at + layers * heads, :bucket_count]
        table = table.reshape(sections, layers, heads, bucket_count)
        return qv, up, table.transpose(1, 0, 2, 3).reshape(layers, all_heads, bucket_count)

    if fused:
        operands.update(vec_own=vecs, a_qkv=qkv_own, a_out=out_weight, a_up=up_own, a_dn=dn_own)
        res = run_blocks(lay, operands)
        tile = res["o_tile"]
        return (
            res["o_block"], res["o_input"], res["o_qkv"], res["o_out"], res["o_up"], res["o_dn"],
            *assembled(res["o_sec"]),
            *[tile[at : at + 1] for at in (lay.gain_at, lay.shift_at, lay.scale_at, lay.bias_at)],
            tile[lay.token_at],
        )

    def gathered(x):
        return lax.all_gather(x, "dp", axis=1, tiled=True)

    operands.update(
        vec_all=lax.all_gather(vecs, "section", axis=0, tiled=False),
        w_qkv=gathered(qkv_own),
        w_out=pick(gathered(out_weight).reshape(layers, sections, own, width), 1),
        w_up=gathered(up_own),
        w_dn=gathered(dn_own),
    )
    res = run_blocks(lay, operands)

    def scattered(x):
        return lax.psum_scatter(x, "dp", scatter_dimension=1, tiled=True)

    def everywhere(x, axis):
        return lax.all_gather(x, "section", axis=axis, tiled=False)

    sqkv, sup, sdn = scattered(res["g_qkv"]), scattered(res["g_up"]), scattered(res["g_dn"])
    qkv_all = everywhere(sqkv.reshape(layers, shard, 3, own), 3).reshape(layers, shard, 3 * width)
    qkv_cols = 3 * width // sections
    qkv_out = lax.dynamic_slice_in_dim(qkv_all, section * qkv_cols, qkv_cols, 2).astype(F32)
    up_all = everywhere(sup.reshape(layers, shard, ranks, unit), 3).reshape(layers, shard, hidden)
    up_out = lax.dynamic_slice_in_dim(up_all, section * hid, hid, 2).astype(F32)
    dn_all = lax.all_to_all(
        sdn.reshape(layers, unit, sections, cols), "section", split_axis=2, concat_axis=1, tiled=False
    )
    dn_out = dn_all.reshape(layers, sections * unit, cols).astype(F32)
    out_mine = scattered(everywhere(res["g_out"], 1).reshape(layers, width, width))
    out_out = lax.dynamic_slice_in_dim(out_mine, section * cols, cols, 2).astype(F32)

    def pages_of(x):
        both = lax.all_gather(x[:rows], "section", axis=0, tiled=False)[:pages]
        return lax.dynamic_slice_in_dim(both, section * cols, cols, 2)

    once = (section < 2).astype(F32)
    here = (jnp.arange(sections) == section).astype(F32)
    tiles, sec_all = lax.psum(
        (res["tiles"] * once, res["sec"][None] * here[:, None, None]), ("section", "dp")
    )
    tile = pick(tiles, 0)
    return (
        pages_of(res["v4"]), pages_of(res["g0"]), qkv_out, out_out, up_out, dn_out,
        *assembled(sec_all),
        *[tile[at : at + 1] for at in (lay.gain_at, lay.shift_at, lay.scale_at, lay.bias_at)],
        tile[lay.token_at],
    )


def solution(mesh):
    rows3 = P("dp", None, None)
    part = P("section", None)
    weight = P(None, "dp", None)
    in_specs = (
        rows3, P("dp", None), P(), P(), part, part, part, part,
        weight, P(), weight, P(), weight, P(), weight, rows3,
    )
    cut = P("dp", None, "section")
    grad = P(None, "dp", "section")
    out_specs = (cut, cut, grad, grad, grad, grad, P(), P(), P(), part, part, part, part, P())
    return jax.shard_map(per_device, mesh=mesh, in_specs=in_specs, out_specs=out_specs, check_vma=False)
```

```python
import functools
import types

import jax
import jax.numpy as jnp
from jax import lax
from jax.experimental import pallas as pl
from jax.experimental.pallas import tpu as pltpu
from jax.sharding import PartitionSpec as P

EPS = 1e-06
MESH = pl.DeviceIdType.MESH
NEG = -1e30
LANES = 128
BF = jnp.bfloat16
F32 = jnp.float32


def pad_up(x, m):
    return (x + m - 1) // m * m


def nn(a, b):
    return jnp.dot(a, b, preferred_element_type=F32)


def nt(a, b):
    return lax.dot_general(a, b, (((1,), (1,)), ((), ())), preferred_element_type=F32)


def tn(a, b):
    return lax.dot_general(a, b, (((0,), (0,)), ((), ())), preferred_element_type=F32)


class Layout:
    def __init__(self, layers, heads, head, rows, prow, pcol, width, hidden, shard, highs, fused):
        self.layers, self.heads, self.head = layers, heads, head
        self.rows, self.prow, self.pcol, self.width, self.hidden = rows, prow, pcol, width, hidden
        self.shard, self.highs, self.fused = shard, highs, fused
        self.own = heads * head
        self.halves = 2 * layers
        self.scale_at, self.bias_at, self.gain_at, self.shift_at, self.token_at = range(5)
        self.qv_at, self.up_at, self.table_at = 0, layers, 2 * layers
        self.sec_rows = pad_up(2 * layers + layers * heads, 8)


def norm_stats(x):
    mean = jnp.mean(x, -1, keepdims=True)
    centered = x - mean
    r = lax.rsqrt(jnp.mean(centered * centered, -1, keepdims=True) + EPS)
    return centered * r, r


ITEMS = ("qkv", "out", "up", "dn")
QKV, OUT, UP, DN = range(4)


def blocks_kernel(lay, names, *refs):
    r = types.SimpleNamespace(**dict(zip(names, refs)))
    fused = lay.fused
    section = lax.axis_index("section")
    core = lax.rem(section, 2)
    mate_at = section + 1 - 2 * core
    mate = {"section": mate_at}
    far = {"section": lax.rem(section + 2, 4)}
    layers, halves, prow, width = lay.layers, lay.halves, lay.prow, lay.width
    rows, pcol = lay.rows, lay.pcol
    own, hid, hd, heads, shard = lay.own, lay.hidden, lay.head, lay.heads, lay.shard
    v_buf, normed, branch, qkv, probs = r.v_buf, r.normed, r.branch, r.qkv, r.probs
    ctx, act, gate, bgrad, dqkv = r.ctx, r.act, r.gate, r.bgrad, r.dqkv
    acc, g_buf, g4_buf, ds_ref, bias_ref = r.acc, r.g_buf, r.g4_buf, r.ds, r.bias
    tiles, sec, vec_all = r.tiles, r.sec, r.vec_all
    core_out, core_in, far_out, far_in = r.core_out, r.core_in, r.far_out, r.far_in

    def remote(src, dst, send, recv, device):
        return pltpu.make_async_remote_copy(
            src_ref=src, dst_ref=dst, send_sem=send, recv_sem=recv, device_id=device, device_id_type=MESH
        )

    loads = {}

    def load(name, src, dst):
        loads[name] = pltpu.make_async_copy(src, dst, r.load_s.at[len(loads)])
        loads[name].start()

    def loaded(*wanted):
        for name in wanted:
            loads[name].wait()

    if fused:
        load("qkv", r.qkv_weight, r.raw_qkv)
        for n, name in enumerate(("ln_gain", "ln_shift", "layer_scale", "branch_bias")):
            load(name, getattr(r, name), r.raw_vec.at[n])
        load("up", r.up_weight, r.raw_up)
        load("qv_bias", r.qv_bias, r.raw_qvb)
        load("up_bias", r.up_bias, r.raw_upb)
    load("patches", r.patches, r.raw_x)
    load("mask", r.page_mask, r.raw_mask)
    load("token", r.mask_token, r.raw_token)
    load("buckets", r.buckets, r.raw_ids)
    load("table", r.rel_table, r.raw_table)
    load("cotangent", r.cotangent, r.raw_g)

    partners = [mate, far]
    if fused:
        dp = lax.axis_index("dp")
        zi, xi = dp // 2, lax.rem(dp, 2)
        xmate = {"dp": zi * 2 + 1 - xi}
        hi, par = zi // 2, lax.rem(zi, 2)
        znear = {"dp": (zi + 1 - 2 * par) * 2 + xi}
        zfar = {"dp": lax.rem(zi + 2, 4) * 2 + xi}
        snext = [lax.rem(section + o, 4) for o in (1, 2, 3)]
        sprev = [lax.rem(section + 4 - o, 4) for o in (1, 2, 3)]
        sdev = [{"section": t} for t in snext]
        partners = [xmate, znear, zfar] + sdev

    barrier = pltpu.get_barrier_semaphore()
    for other in partners:
        pl.semaphore_signal(barrier, inc=1, device_id=other, device_id_type=MESH)

    sends = []

    def sent(copy, when=None):
        sends.append((copy, when))

    def each_section(body):
        for t in range(4):
            pl.when(section == t)(functools.partial(body, t))

    if fused:
        zfs, zfr, zns, znr = r.ag_zfs, r.ag_zfr, r.ag_zns, r.ag_znr
        xs, xr, ls = r.ag_xs, r.ag_xr, r.ag_ls
        my_out = zi == section
        out_far = lax.rem(section + 2, 4) == zi
        out_even = lax.rem(section + zi, 2) == 0
        out_odd = jnp.logical_not(out_even)

        def item(n):
            l, kind = n // 4, ITEMS[n % 4]
            if kind == "out":
                src = r.out_weight.at[l]
            elif kind == "dn":
                src = r.down_weight.at[l, pl.ds(pl.multiple_of(section * shard, shard), shard)]
            else:
                src = getattr(r, "a_" + kind).at[l]
            return l, kind, src, getattr(r, "w_" + kind)

        def own_copy(n):
            l, kind, src, dst = item(n)
            place = dst.at[l, xi] if kind == "out" else dst.at[l, hi, par, xi]
            return pltpu.make_async_copy(src, place, ls.at[n])

        def far_copy(n):
            l, kind, src, dst = item(n)
            place = dst.at[l, xi] if kind == "out" else dst.at[l, hi, par, xi]
            return remote(src, place, zfs.at[n], zfr.at[n], zfar)

        def near_copy(n):
            l, kind, src, dst = item(n)
            place = dst.at[l, xi] if kind == "out" else dst.at[l, :, par, xi]
            return remote(place, place, zns.at[n], znr.at[n], znear)

        def across(n, stage):
            l, kind, src, dst = item(n)
            if kind == "out":
                place = dst.at[l, xi]
                return remote(src if stage == 0 else place, place, xs.at[n, 0], xr.at[n, 0], xmate)
            place = dst.at[l, :, 1 - par, xi] if stage == 2 else dst.at[l, hi if stage == 0 else 1 - hi, par, xi]
            return remote(src if stage == 0 else place, place, xs.at[n, stage], xr.at[n, stage], xmate)

        def begin(copy, when=None):
            if when is None:
                copy.start()
            else:
                pl.when(when)(copy.start)

        def both_ends(copy, when=None):
            begin(copy, when)
            sent(copy, when)

        def gather_start(n):
            if n >= 4 * layers:
                return
            when = my_out if n % 4 == OUT else None
            both_ends(far_copy(n), when)
            begin(own_copy(n), when)

        def gather_across(n):
            if n >= 4 * layers:
                return
            if n % 4 == OUT:
                begin(across(n, 0), my_out)
                sent(across(n, 0))
            else:
                both_ends(across(n, 0))

        def pump_far(n):
            if n % 4 == OUT:

                @pl.when(out_far)
                def _():
                    far_copy(n).wait_recv()
                    across(n, 1).start()

                pl.when(my_out)(own_copy(n).wait)
                both_ends(near_copy(n), out_even)
                return
            own_copy(n).wait()
            far_copy(n).wait_recv()
            both_ends(near_copy(n))
            both_ends(across(n, 1))

        def pump_near(n):
            if n % 4 == OUT:

                @pl.when(out_odd)
                def _():
                    near_copy(n).wait_recv()
                    across(n, 2).start()

                return
            near_copy(n).wait_recv()
            both_ends(across(n, 2))

        def need(n):
            for stage in range(1 if n % 4 == OUT else 3):
                across(n, stage).wait_recv()

        loaded("qkv")

        def slice_qkv(t):
            for l in range(layers):
                parts = [r.raw_qkv[l, :, m * width + t * own : m * width + (t + 1) * own] for m in range(3)]
                r.a_qkv[l] = jnp.concatenate(parts, 1)

        each_section(slice_qkv)
        loaded("ln_gain", "ln_shift", "layer_scale", "branch_bias")
        vec_own = r.vec_own
        vec_own[...] = jnp.zeros_like(vec_own)
        for n in range(4):
            vec_own[n : n + 1, :] = r.raw_vec[n].astype(F32)
        vec_all[section] = vec_own[...]

        pl.semaphore_wait(barrier, len(partners))

        gather_start(QKV)
        gather_across(QKV)
        for o in range(3):
            copy = remote(vec_own, vec_all.at[section], r.vec_s.at[o], r.vec_r.at[o], sdev[o])
            copy.start()
            sent(copy)
        gather_start(OUT)
        gather_across(OUT)
        loaded("up", "up_bias", "qv_bias")
        unit = own // 2

        def slice_up(t):
            for l in range(layers):
                at = [d * 4 * unit + t * unit for d in range(hid // unit)]
                r.a_up[l] = jnp.concatenate([r.raw_up[l, :, a : a + unit] for a in at], 1)
            r.upb[...] = jnp.concatenate([r.raw_upb[:, a : a + unit].astype(F32) for a in at], 1)
            q = r.raw_qvb[:, t * own : (t + 1) * own].astype(F32)
            v = r.raw_qvb[:, width + t * own : width + (t + 1) * own].astype(F32)
            r.qvb[...] = jnp.concatenate([q, jnp.zeros_like(q), v], 1)

        each_section(slice_up)
        gather_start(UP)
        gather_across(UP)
        gather_across(DN)
    else:
        need = pump_far = pump_near = gather_start = gather_across = lambda n: None
        pl.semaphore_wait(barrier, len(partners))

    def weight(kind, l):
        w = getattr(r, "w_" + kind)[l]
        return w.reshape(-1, w.shape[-1])

    tiles[...] = jnp.zeros_like(tiles)
    sec[...] = jnp.zeros_like(sec)
    loaded("patches", "mask", "token")
    mask_row = (r.raw_mask[0:1, :] * (1 - core) + r.raw_mask[1:2, :] * core).astype(F32)
    at_row = lax.broadcasted_iota(jnp.int32, (prow, rows), 0)
    at_column = lax.broadcasted_iota(jnp.int32, (prow, rows), 1)
    mask = jnp.sum(jnp.where(at_row == at_column, mask_row, 0.0), 1, keepdims=True)
    masked = mask > 0.5
    v_buf[0, prow - 16 :, :] = jnp.zeros((16, width), BF)
    token = r.raw_token[...].reshape(1, width).astype(F32)

    def own_page(ref):
        return jnp.where(core == 0, ref[:, 0, :].astype(F32), ref[:, 1, :].astype(F32))

    v_buf[0, :rows, :] = jnp.where(masked[:rows], token, own_page(r.raw_x)).astype(BF)

    def column_sum(x):
        return jnp.sum(x, 0, keepdims=True)

    def vec(kind, k):
        return vec_all[k, kind : kind + 1, :]

    def share_rows(ref, step):
        return remote(ref.at[0], ref.at[1], r.row_s.at[step], r.row_r.at[step], mate)

    def to_mate(step):
        slot = step % 3
        return remote(core_out.at[slot], core_in.at[slot], r.core_s.at[step], r.core_r.at[step], mate)

    def to_far(step):
        slot = step % 3
        return remote(far_out.at[slot], far_in.at[slot], r.far_s.at[step], r.far_r.at[step], far)

    def sum_up_start(step, part):
        core_out[step % 3] = part(1).astype(BF)
        to_mate(step).start()
        acc[...] = part(0)
        to_mate(step).wait_recv()
        far_out[step % 3] = (acc[...] + core_in[step % 3].astype(F32)).astype(BF)
        to_far(step).start()

    def sum_up_end(step):
        to_far(step).wait_recv()
        total = far_out[step % 3].astype(F32) + far_in[step % 3].astype(F32)
        to_mate(step).wait_send()
        to_far(step).wait_send()
        return total

    def norm_row(k):
        xhat, _ = norm_stats(v_buf[k].astype(F32))
        normed[k, 0] = (xhat * vec(0, k) + vec(1, k)).astype(BF)
        share_rows(normed.at[k], k).start()

    def rows_here(ref, step):
        share_rows(ref, step).wait_recv()

    scale = hd ** -0.5

    def attention_page(l, k, slot):
        fresh = nn(normed[k, slot], weight("qkv", l)) + r.qvb[l : l + 1, :]
        qkv[l, slot] = fresh.astype(BF)
        for h in range(heads):
            q = qkv[l, slot, :, h * hd : (h + 1) * hd]
            kk = qkv[l, slot, :, own + h * hd : own + (h + 1) * hd]
            vv = qkv[l, slot, :, 2 * own + h * hd : 2 * own + (h + 1) * hd]
            s = nt(q, kk) * scale + bias_ref[l * heads + h, :, :prow].astype(F32)
            e = jnp.exp(s - jnp.max(s, -1, keepdims=True))
            p = (e / jnp.sum(e, -1, keepdims=True)).astype(BF)
            probs[l, slot, h] = p
            ctx[l, slot, :, h * hd : (h + 1) * hd] = nn(p, vv).astype(BF)

    def mlp_page(l, k, slot):
        pre = nn(normed[k, slot], weight("up", l)) + r.upb[l : l + 1, :]
        c0, c1 = 0.7978845608028654, 0.044715
        square = pre * pre
        t = jnp.tanh(c0 * (pre + c1 * pre * square))
        act[l, slot] = (0.5 * pre * (1.0 + t)).astype(BF)
        slope = 0.5 * (1.0 + t) + 0.5 * pre * (1.0 - t * t) * (c0 * (1.0 + 3.0 * c1 * square))
        gate[l, slot] = slope.astype(BF)

    def end_forward(k, step):
        b = sum_up_end(step) + vec(3, k)
        branch[k] = b
        return (v_buf[k].astype(F32) + vec(2, k) * b).astype(BF)

    def context_part(l):
        return lambda slot: nn(ctx[l, slot], weight("out", l))

    def hidden_part(l):
        return lambda slot: nn(act[l, slot], weight("dn", l))

    cols = own
    if fused:
        def z_first(n):
            return n in (OUT, 4 + DN)

        def first_copy(n):
            l, kind = n // 4, ITEMS[n % 4]
            part, place = getattr(r, "g_" + kind), getattr(r, "x_" + kind)
            if kind == "out":
                src, dst = (part.at[l], place.at[l]) if z_first(n) else (part.at[l, 1 - xi], place.at[l, 0])
            else:
                src, dst = part.at[l, :, 1 - par] if z_first(n) else part.at[l, :, :, 1 - xi], place.at[l]
            return remote(src, dst, r.rs_xs.at[n], r.rs_xr.at[n], znear if z_first(n) else xmate)

        def second_copy(n):
            l, kind = n // 4, ITEMS[n % 4]
            pair, place = getattr(r, "x_" + kind), getattr(r, "n_" + kind)
            if kind == "out":
                src = pair.at[l, 1 - xi] if z_first(n) else pair.at[l, 0]
            else:
                src = pair.at[l, :, 1 - xi] if z_first(n) else pair.at[l, :, 1 - par]
            return remote(src, place.at[l], r.rs_ns.at[n], r.rs_nr.at[n], xmate if z_first(n) else znear)

        def far_sum_copy(n):
            l, kind = n // 4, ITEMS[n % 4]
            four = getattr(r, "n_" + kind)
            src = four.at[l] if kind == "out" else four.at[l, 1 - hi]
            return remote(src, getattr(r, "f_" + kind).at[l], r.rs_fs.at[n], r.rs_fr.at[n], zfar)

        def added(a, b):
            return (a.astype(F32) + b.astype(F32)).astype(BF)

        def sum_start(n):
            both_ends(first_copy(n), out_odd if n % 4 == OUT and z_first(n) else None)

        def sum_first(n):
            l, kind = n // 4, ITEMS[n % 4]
            pair, part = getattr(r, "x_" + kind), getattr(r, "g_" + kind)
            if kind != "out":
                first_copy(n).wait_recv()
                mine = part[l, :, par] if z_first(n) else part[l, :, :, xi]
                pair[l] = added(mine, pair[l])
                both_ends(second_copy(n))
            elif z_first(n):

                @pl.when(out_even)
                def _():
                    first_copy(n).wait_recv()
                    pair[l] = added(part[l], pair[l])

                both_ends(second_copy(n), out_even)
            else:
                first_copy(n).wait_recv()
                pair[l, 0] = added(part[l, xi], pair[l, 0])
                both_ends(second_copy(n), out_odd)

        def sum_second(n):
            l, kind = n // 4, ITEMS[n % 4]
            four, pair = getattr(r, "n_" + kind), getattr(r, "x_" + kind)
            if kind == "out":

                @pl.when(out_even)
                def _():
                    second_copy(n).wait_recv()
                    four[l] = added(pair[l, xi if z_first(n) else 0], four[l])

                both_ends(far_sum_copy(n), out_far)
                return
            second_copy(n).wait_recv()
            four[l] = added(pair[l, :, xi] if z_first(n) else pair[l, :, par], four[l])
            both_ends(far_sum_copy(n))

        def to_section(n, o, src, dst, device):
            return remote(src, dst, r.rs_ss.at[n, o], r.rs_sr.at[n, o], device)

        def finish_item(n):
            l, kind = n // 4, ITEMS[n % 4]
            blocks, got = getattr(r, "s_" + kind), getattr(r, "t_" + kind)
            if kind == "out":

                @pl.when(my_out)
                def _():
                    far_sum_copy(n).wait_recv()
                    total = r.n_out[l].astype(F32) + r.f_out[l].astype(F32)
                    for t in range(4):
                        blocks[l, t] = total[:, t * cols : (t + 1) * cols].astype(BF)
                    for o in range(3):
                        to_section(n, o, blocks.at[l, snext[o]], got.at[l], sdev[o]).start()
                    got[l] = blocks[l, section]

                for o in range(3):
                    sent(to_section(n, o, blocks.at[l, snext[o]], got.at[l], sdev[o]), my_out)
                return
            far_sum_copy(n).wait_recv()
            total = getattr(r, "n_" + kind)[l, hi].astype(F32) + getattr(r, "f_" + kind)[l].astype(F32)
            for t in range(3 if kind == "qkv" else 4):
                blocks[l, t] = total[:, t * cols : (t + 1) * cols].astype(BF)
            if kind == "qkv":
                for m in range(3):
                    at = 4 * m + section
                    dest, place = at // 3, lax.rem(at, 3)
                    away = dest != section
                    copy = remote(
                        blocks.at[l, m], got.at[l, place], r.rs_ss.at[n, m], r.rs_sr.at[n, place], {"section": dest}
                    )
                    pl.when(away)(copy.start)
                    sent(copy, away)

                    @pl.when(jnp.logical_not(away))
                    def _():
                        got[l, place] = blocks[l, m]

                return
            for o in range(3):
                copy = to_section(n, o, blocks.at[l, snext[o]], got.at[l, section], sdev[o])
                copy.start()
                sent(copy)
            got[l, section] = blocks[l, section]

        def item_here(n):
            l, kind = n // 4, ITEMS[n % 4]
            blocks, got = getattr(r, "s_" + kind), getattr(r, "t_" + kind)
            if kind == "out":
                for o in range(3):
                    copy = to_section(n, o, blocks.at[l, 0], got.at[l], sdev[o])
                    pl.when(sprev[o] == zi)(copy.wait_recv)
            elif kind == "qkv":
                for place in range(3):
                    source = lax.rem(3 * section + place, 4)
                    copy = to_section(n, place, blocks.at[l, 0], got.at[l, place], mate)
                    pl.when(source != section)(copy.wait_recv)
            else:
                for o in range(3):
                    to_section(n, o, blocks.at[l, 0], got.at[l, sprev[o]], sdev[o]).wait_recv()

        def share_page(value, name):
            out, place = getattr(r, name), getattr(r, name + "_s")
            for t in range(4):
                place[t] = value[:, t * cols : (t + 1) * cols]
            out[core] = place[section]
            at = int(name == "o_input")
            copy = remote(place.at[mate_at], out.at[core], r.page_s.at[at], r.page_r.at[at], mate)
            copy.start()
            sent(copy)

        def page_here(name):
            at = int(name == "o_input")
            remote(getattr(r, name + "_s").at[0], getattr(r, name).at[1 - core], r.page_s.at[at], r.page_r.at[at], mate).wait_recv()
    else:
        sum_start = sum_first = sum_second = finish_item = lambda n: None

    def keep_grad(n, value):
        ref = getattr(r, "g_" + ITEMS[n % 4])
        ref[n // 4] = value.astype(BF).reshape(ref.shape[1:])

    def table_sums(l, part, parts):
        groups = 2 * heads
        hist = r.hist
        if part == 0:
            hist[...] = jnp.zeros_like(hist)
        step = 8

        def body(block, carry):
            at = pl.multiple_of(block * step, step)
            ids_all = r.ids[pl.ds(at, step), :]
            grads_all = ds_ref[l * groups : (l + 1) * groups, pl.ds(at, step), :]
            total = None
            for row in range(step):
                ids = ids_all[row : row + 1, :]
                low = ids & (LANES - 1)
                high = lax.shift_right_logical(ids, 7)
                spots = lax.broadcasted_iota(jnp.int32, (LANES, pcol), 0)
                hot = jnp.where(spots == low, 1.0, 0.0).astype(BF)
                grads = grads_all[:, row, :]
                parts = [jnp.where(high == number, grads, 0.0) for number in range(lay.highs)]
                got = nt(jnp.concatenate(parts, 0).astype(BF), hot)
                total = got if total is None else total + got
            hist[...] += total
            return carry

        count = pad_up(rows, step) // step
        lax.fori_loop(count * part // parts, count * (part + 1) // parts, body, 0)
        if part + 1 < parts:
            return
        for h in range(heads):
            at = lay.table_at + l * heads + h
            for number in range(lay.highs):
                first = number * groups + 2 * h
                row = hist[first : first + 1, :] + hist[first + 1 : first + 2, :]
                sec[at : at + 1, number * LANES : (number + 1) * LANES] = row

    def make_bias():
        table = r.table
        table[...] = jnp.zeros_like(table)
        count = r.raw_table.shape[2]

        def own_tables(t):
            for l in range(layers):
                for h in range(heads):
                    at = l * heads + h
                    row = r.raw_table[t * heads + h, l : l + 1, :]
                    table[at : at + 1, :count] = row.astype(F32)

        each_section(own_tables)
        ids_ref = r.ids
        ids_ref[...] = jnp.zeros_like(ids_ref)
        ids_ref[:rows, :rows] = r.raw_ids[...]
        step = 16

        def body(block, carry):
            at = pl.multiple_of(block * step, step)
            for half in range(pcol // LANES):
                lanes = slice(half * LANES, (half + 1) * LANES)
                ids = ids_ref[pl.ds(at, step), lanes]
                low = ids & (LANES - 1)
                high = lax.shift_right_logical(ids, 7)
                column = lax.broadcasted_iota(jnp.int32, (step, LANES), 1) + half * LANES
                inside = column < rows
                picks = [high == number for number in range(lay.highs)]
                for t in range(layers * heads):
                    value = jnp.full((step, LANES), NEG, F32)
                    for number in range(lay.highs):
                        row = table[t : t + 1, number * LANES : (number + 1) * LANES]
                        got = jnp.take_along_axis(jnp.broadcast_to(row, (step, LANES)), low, axis=1)
                        value = jnp.where(picks[number], got, value)
                    value = jnp.where(inside, value, NEG)
                    bias_ref[t, pl.ds(at, step), lanes] = value.astype(BF)
            return carry

        lax.fori_loop(0, prow // step, body, 0)

    loaded("buckets", "table", "cotangent")
    make_bias()
    if fused:
        for o in range(3):
            remote(r.vec_own, vec_all.at[sprev[o]], r.vec_s.at[o], r.vec_r.at[o], sdev[o]).wait_recv()

    last = halves - 1

    def branch_grad(k, g):
        step = halves + k
        low = (g * vec(2, k)).astype(BF)
        bgrad[k, 0] = low
        share_rows(bgrad.at[k], step).start()
        tiles[k, lay.bias_at : lay.bias_at + 1, :] = column_sum(low.astype(F32))

    norm_row(0)
    g4_buf[prow - 16 :, :] = jnp.zeros((16, width), F32)
    g4_buf[:rows, :] = own_page(r.raw_g)
    branch_grad(last, g4_buf[...])
    ds_ref[...] = jnp.zeros_like(ds_ref)

    pump_far(QKV)
    gather_across(4 + QKV)
    pump_far(OUT)
    pump_near(QKV)
    gather_across(4 + UP)
    gather_start(DN)
    pump_near(OUT)
    gather_across(4 + OUT)
    gather_across(4 + DN)
    pump_far(UP)
    for l in range(layers):
        k = 2 * l
        first = 4 * l
        need(first + QKV)
        attention_page(l, k, 0)
        rows_here(normed.at[k], k)
        if l == 0:
            attention_page(l, k, 1)
            need(OUT)
            sum_up_start(k, context_part(l))
            gather_start(4 + QKV)
            pump_near(UP)
            pump_far(DN)
        else:
            pump_near(4 + OUT)
            attention_page(l, k, 1)
            pump_near(4 + UP)
            pump_far(4 + DN)
            need(4 + OUT)
            sum_up_start(k, context_part(l))
            pump_near(4 + DN)
        v_buf[k + 1] = end_forward(k, k)
        norm_row(k + 1)
        k = k + 1
        if l == 0:
            pump_near(DN)
            pump_far(4 + QKV)
            gather_start(4 + OUT)
            gather_start(4 + UP)
        need(first + UP)
        mlp_page(l, k, 0)
        rows_here(normed.at[k], k)
        mlp_page(l, k, 1)
        if l == 0:
            need(DN)
            sum_up_start(k, hidden_part(l))
            pump_near(4 + QKV)
            pump_far(4 + OUT)
            pump_far(4 + UP)
            gather_start(4 + DN)
            v_buf[k + 1] = end_forward(k, k)
            norm_row(k + 1)

    both = 2 * prow

    def whole(ref):
        return ref.reshape(both, ref.shape[-1])

    def back_through_norm(k, g, ng):
        xhat, rr = norm_stats(v_buf[k].astype(F32))
        tiles[k, lay.gain_at : lay.gain_at + 1, :] = column_sum(ng * xhat)
        tiles[k, lay.shift_at : lay.shift_at + 1, :] = column_sum(ng)
        t = ng * vec(0, k)
        inner = t - jnp.mean(t, -1, keepdims=True) - xhat * jnp.mean(t * xhat, -1, keepdims=True)
        return g + rr * inner

    def scale_sum(k, g):
        tiles[k, lay.scale_at : lay.scale_at + 1, :] = column_sum(g * branch[k])

    def mlp_back(l, k, slot):
        dact = nt(bgrad[k, slot], weight("dn", l))
        gate[l, slot] = (dact * gate[l, slot].astype(F32)).astype(BF)

    def mlp_back_part(l):
        return lambda slot: nt(gate[l, slot], weight("up", l))

    def up_grads(l, k):
        dpre = whole(gate[l])
        keep_grad(4 * l + UP, tn(whole(normed[k]), dpre))
        sum_start(4 * l + UP)
        sec[lay.up_at + l : lay.up_at + l + 1, :] = column_sum(dpre.astype(F32))

    l, k = layers - 1, last
    rows_here(bgrad.at[k], halves + k)
    keep_grad(4 * l + DN, tn(whole(act[l]), whole(bgrad[k])))
    sum_start(4 * l + DN)
    need(4 * l + DN)
    mlp_back(l, k, 1)
    mlp_back(l, k, 0)
    sum_up_start(k, mlp_back_part(l))
    up_grads(l, k)
    sum_up_start(k + 1, hidden_part(l))
    g = back_through_norm(k, g4_buf[...], sum_up_end(k))
    g_buf[...] = g.astype(BF).astype(F32)

    def end_of_forward():
        after = end_forward(last, last + 1)
        scale_sum(last, g4_buf[...])
        if fused:
            share_page(after, "o_block")
        else:
            r.v4[...] = after

    for k in reversed(range(last)):
        l = k // 2
        step = 2 * halves - 1 - k
        g = g_buf[...]
        branch_grad(k, g)
        scale_sum(k, g)
        if k == last - 1:
            sum_first(4 * l + DN)
        if k % 2 == 0:

            def attention_back(slot):
                dctx = nt(bgrad[k, slot], weight("out", l)).astype(BF)
                for h in range(heads):
                    q = qkv[l, slot, :, h * hd : (h + 1) * hd]
                    kk = qkv[l, slot, :, own + h * hd : own + (h + 1) * hd]
                    vv = qkv[l, slot, :, 2 * own + h * hd : 2 * own + (h + 1) * hd]
                    dc = dctx[:, h * hd : (h + 1) * hd]
                    low_p = probs[l, slot, h]
                    p = low_p.astype(F32)
                    dp_ = nt(dc, vv)
                    ds = (p * (dp_ - jnp.sum(p * dp_, -1, keepdims=True))).astype(BF)
                    ds_ref[(l * heads + h) * 2 + slot, :, :prow] = ds.astype(F32)
                    dqkv[slot, :, h * hd : (h + 1) * hd] = (nn(ds, kk) * scale).astype(BF)
                    dqkv[slot, :, own + h * hd : own + (h + 1) * hd] = (tn(ds, q) * scale).astype(BF)
                    dqkv[slot, :, 2 * own + h * hd : 2 * own + (h + 1) * hd] = tn(low_p, dc).astype(BF)

            if l == 0:
                rows_here(bgrad.at[k], halves + k)
                keep_grad(OUT, tn(whole(ctx[l]), whole(bgrad[k])))
                sum_start(OUT)
                attention_back(0)
            else:
                attention_back(0)
                rows_here(bgrad.at[k], halves + k)
            attention_back(1)
            if l == 0:
                sum_second(4 + QKV)
                sum_second(4 + OUT)
            sum_up_start(step, lambda slot: nt(dqkv[slot], weight("qkv", l)))
            sum_first(4 * l + (UP if l > 0 else DN))
            dall = whole(dqkv[...])
            keep_grad(4 * l + QKV, tn(whole(normed[k]), dall))
            sum_start(4 * l + QKV)
            sums = column_sum(dall.astype(F32))
            sec[lay.qv_at + l : lay.qv_at + l + 1, :own] = sums[:, :own]
            sec[lay.qv_at + l : lay.qv_at + l + 1, 2 * LANES : 2 * LANES + own] = sums[:, 2 * own :]
            if l > 0:
                keep_grad(4 * l + OUT, tn(whole(ctx[l]), whole(bgrad[k])))
                sum_start(4 * l + OUT)
                end_of_forward()
                table_sums(l, 0, 2)
            else:
                sum_first(OUT)
                table_sums(l, 0, 2)
                sum_second(DN)
                table_sums(l, 1, 2)
        else:
            rows_here(bgrad.at[k], halves + k)
            keep_grad(4 * l + DN, tn(whole(act[l]), whole(bgrad[k])))
            sum_start(4 * l + DN)
            sum_second(4 * (l + 1) + DN)
            mlp_back(l, k, 1)
            mlp_back(l, k, 0)
            sum_up_start(step, mlp_back_part(l))
            up_grads(l, k)
            sum_second(4 * (l + 1) + UP)
            sum_first(4 * (l + 1) + QKV)
            table_sums(l + 1, 1, 2)
            sum_first(4 * (l + 1) + OUT)
        g = back_through_norm(k, g, sum_up_end(step))
        if k > 0:
            g_buf[...] = g.astype(BF).astype(F32)
    sum_first(UP)

    kept = jnp.where(masked, 0.0, g)
    token_sum = column_sum(jnp.where(masked, g, 0.0))
    for k in range(halves):
        tiles[k, lay.token_at : lay.token_at + 1, :] = token_sum
    for k in range(halves):
        share_rows(normed.at[k], k).wait_send()
        share_rows(bgrad.at[k], halves + k).wait_send()

    if not fused:
        r.g0[...] = kept
        return

    tile_copy = remote(tiles.at[mate_at], r.tile_in, r.small_s.at[0], r.small_r.at[0], mate)
    tile_copy.start()
    sent(tile_copy)
    red, red_in = r.red, r.red_in
    hops = [znear, zfar, xmate]

    def hop_copy(hop):
        return remote(red.at[hop], red_in.at[hop], r.small_s.at[1 + hop], r.small_r.at[1 + hop], hops[hop])

    def hop_start(hop):
        hop_copy(hop).start()
        sent(hop_copy(hop))

    def hop_end(hop):
        hop_copy(hop).wait_recv()
        red[hop + 1] = red[hop] + red_in[hop]

    share_page(kept, "o_input")
    finish_item(4 + DN)
    finish_item(4 + UP)
    tile_copy.wait_recv()
    red[0, :8] = tiles[section] + r.tile_in[...]
    red[0, 8:] = sec[...]
    hop_start(0)
    finish_item(4 + QKV)
    finish_item(4 + OUT)
    finish_item(DN)
    hop_end(0)
    hop_start(1)
    sum_second(UP)
    sum_first(QKV)
    sum_second(OUT)
    hop_end(1)
    hop_start(2)
    sum_second(QKV)
    finish_item(UP)
    hop_end(2)
    r.o_tile[...] = red[3, :8]
    sec_all, sec_sum = r.o_sec, r.sec_sum
    sec_sum[...] = red[3, 8:]
    sec_all[section] = sec_sum[...]
    for o in range(3):
        copy = remote(sec_sum, sec_all.at[section], r.sec_s.at[o], r.sec_r.at[o], sdev[o])
        copy.start()
        sent(copy)
    finish_item(OUT)
    finish_item(QKV)
    page_here("o_block")
    page_here("o_input")
    for n in reversed(range(4 * layers)):
        item_here(n)
    for o in range(3):
        remote(sec_sum, sec_all.at[sprev[o]], r.sec_s.at[o], r.sec_r.at[o], sdev[o]).wait_recv()
    for copy, when in sends:
        if when is None:
            copy.wait_send()
        else:
            pl.when(when)(copy.wait_send)


def run_blocks(lay, operands):
    L, prow, width, own, hid, shard = lay.layers, lay.prow, lay.width, lay.own, lay.hidden, lay.shard
    halves, steps, heads, pcol, page = lay.halves, 2 * lay.halves, lay.heads, lay.pcol, lay.rows
    rows = (prow, width)
    groups = 2 * heads
    dma = pltpu.SemaphoreType.DMA
    outs, scratch = {}, {}
    items = 4 * L
    wide = {"qkv": 3 * own, "up": hid, "dn": width, "out": width}
    raw = types.SimpleNamespace(**{name: (x.shape, x.dtype) for name, x in operands.items()})
    if lay.fused:
        outs.update(o_block=((2, prow, own), BF))
        outs.update(o_input=((2, prow, own), F32))
        outs.update(t_qkv=((L, 3, shard, own), BF))
        outs.update(t_out=((L, shard, own), BF))
        outs.update(t_up=((L, 4, shard, own), BF))
        outs.update(t_dn=((L, 4, shard, own), BF))
        outs.update(o_tile=((8, width), F32))
        outs.update(o_sec=((4, lay.sec_rows, width), F32))
        scratch.update(tiles=((halves, 8, width), F32))
        scratch.update(sec=((lay.sec_rows, width), F32))
        scratch.update(vec_all=((halves, 8, width), F32))
        scratch.update(vec_own=((8, width), F32))
        for kind, c in wide.items():
            lead = (2,) if kind == "out" else (2, 2, 2)
            scratch["w_" + kind] = ((L,) + lead + (shard, c), BF)
            scratch["g_" + kind] = ((L,) + lead + (shard, c), BF)
            scratch["x_" + kind] = ((L,) + (lead if kind == "out" else lead[:-1]) + (shard, c), BF)
            scratch["n_" + kind] = ((L,) + lead[:-2] + (shard, c), BF)
            scratch["f_" + kind] = ((L, shard, c), BF)
            scratch["s_" + kind] = ((L, 3 if kind == "qkv" else 4, shard, own), BF)
        scratch.update(a_qkv=((L, shard, 3 * own), BF))
        scratch.update(a_up=((L, shard, hid), BF))
        scratch.update(raw_qkv=(raw.qkv_weight, raw.up_weight)[0], raw_up=(raw.qkv_weight, raw.up_weight)[1])
        scratch.update(raw_qvb=(raw.qv_bias, raw.up_bias)[0], raw_upb=(raw.qv_bias, raw.up_bias)[1])
        scratch.update(raw_vec=((4,) + raw.ln_gain[0], BF))
        scratch.update(qvb=(((L, 3 * own), F32), ((L, hid), F32))[0], upb=(((L, 3 * own), F32), ((L, hid), F32))[1])
        scratch.update(o_block_s=(((4, prow, own), BF), ((4, prow, own), F32))[0], o_input_s=(((4, prow, own), BF), ((4, prow, own), F32))[1])
        scratch.update(tile_in=((8, width), F32))
        scratch.update(red=((4, 8 + lay.sec_rows, width), F32))
        scratch.update(red_in=((3, 8 + lay.sec_rows, width), F32))
        scratch.update(sec_sum=((lay.sec_rows, width), F32))
    else:
        outs.update(v4=(rows, BF))
        outs.update(g0=(rows, F32))
        outs.update(tiles=((halves, 8, width), F32))
        outs.update(sec=((lay.sec_rows, width), F32))
        outs.update(g_qkv=(((L, width, 3 * own), BF), ((L, own, width), BF))[0], g_out=(((L, width, 3 * own), BF), ((L, own, width), BF))[1])
        outs.update(g_up=(((L, width, hid), BF), ((L, hid, width), BF))[0], g_dn=(((L, width, hid), BF), ((L, hid, width), BF))[1])
    scratch.update(
        raw_x=raw.patches,
        raw_g=raw.cotangent,
        raw_mask=raw.page_mask,
        raw_token=raw.mask_token,
        raw_ids=raw.buckets,
        raw_table=raw.rel_table,
        ids=((prow, pcol), jnp.int32),
        table=((pad_up(L * heads, 8), lay.highs * LANES), F32),
        bias=((L * heads, prow, pcol), BF),
        v_buf=((halves,) + rows, BF),
        normed=((halves, 2) + rows, BF),
        branch=((halves,) + rows, F32),
        qkv=((L, 2, prow, 3 * own), BF),
        probs=((L, 2, heads, prow, prow), BF),
        ctx=((L, 2, prow, own), BF),
        act=((L, 2, prow, hid), BF),
        gate=((L, 2, prow, hid), BF),
        bgrad=((halves, 2) + rows, BF),
        dqkv=((2, prow, 3 * own), BF),
        acc=(rows, F32),
        g_buf=(rows, F32),
        g4_buf=(rows, F32),
        ds=((L * groups, prow, pcol), F32),
        hist=((lay.highs * groups, LANES), F32),
        core_out=((3,) + rows, BF),
        core_in=((3,) + rows, BF),
        far_out=((3,) + rows, BF),
        far_in=((3,) + rows, BF),
    )
    each = (steps,)
    sems = dict(core_s=each, core_r=each, far_s=each, far_r=each, row_s=each, row_r=each, load_s=(16,))
    if lay.fused:
        sems.update(
            ag_zfs=(items,), ag_zfr=(items,), ag_zns=(items,), ag_znr=(items,),
            ag_xs=(items, 3), ag_xr=(items, 3), ag_ls=(items,), vec_s=(3,), vec_r=(3,),
            rs_xs=(items,), rs_xr=(items,), rs_ns=(items,), rs_nr=(items,), rs_fs=(items,), rs_fr=(items,),
            rs_ss=(items, 3), rs_sr=(items, 3), page_s=(2,), page_r=(2,), small_s=(4,), small_r=(4,),
            sec_s=(3,), sec_r=(3,),
        )
    names = list(operands) + list(outs) + list(scratch) + list(sems)
    in_vmem = ("w_qkv", "w_out", "w_up", "w_dn", "vec_all", "qvb", "upb")
    spaces = [pltpu.VMEM if name in in_vmem else pl.ANY for name in operands]
    results = pl.pallas_call(
        functools.partial(blocks_kernel, lay, names),
        out_shape=tuple(jax.ShapeDtypeStruct(*spec) for spec in outs.values()),
        in_specs=[pl.BlockSpec(memory_space=space) for space in spaces],
        out_specs=[pl.BlockSpec(memory_space=pltpu.VMEM)] * len(outs),
        scratch_shapes=[pltpu.VMEM(*spec) for spec in scratch.values()] + [dma(spec) for spec in sems.values()],
        compiler_params=pltpu.CompilerParams(
            collective_id=1, has_side_effects=True, vmem_limit_bytes=61 * 2**20
        ),
        name="blocks",
        cost_estimate=pl.CostEstimate(flops=9 * 10**9, bytes_accessed=2 * 10**7, transcendentals=10**7),
    )(*operands.values())
    return dict(zip(outs, results))


def assemble_kernel(
    lay, block_ref, input_ref, qkv_ref, out_ref, up_ref, dn_ref, tile_ref, sec_ref,
    o_block, o_input, o_qkv, o_out, o_up, o_dn, o_qv, o_upb, o_table,
    o_gain, o_shift, o_scale, o_bias, o_token,
):
    rows, own, layers, heads = lay.rows, lay.own, lay.layers, lay.heads
    unit = own // 2
    for page in range(2):
        o_block[page] = block_ref[page].astype(F32).T[:, :rows].astype(BF)
        o_input[page] = input_ref[page].T[:, :rows]
    for l in range(layers):
        o_qkv[l] = jnp.concatenate([qkv_ref[l, place] for place in range(3)], 1).astype(F32)
        o_out[l] = out_ref[l].astype(F32)
        pieces = [up_ref[l, t, :, half * unit : (half + 1) * unit] for half in range(2) for t in range(4)]
        o_up[l] = jnp.concatenate(pieces, 1).astype(F32)
        o_dn[l] = dn_ref[l].reshape(4 * lay.shard, own).astype(F32).T
    q = [sec_ref[t, lay.qv_at : lay.qv_at + layers, :own] for t in range(4)]
    v = [sec_ref[t, lay.qv_at : lay.qv_at + layers, 2 * LANES : 2 * LANES + own] for t in range(4)]
    o_qv[...] = jnp.concatenate(q + v, 1)
    up = [sec_ref[t, lay.up_at : lay.up_at + layers, :] for t in range(4)]
    count = lay.hidden // unit
    o_upb[...] = jnp.concatenate([up[t][:, d * unit : (d + 1) * unit] for d in range(count) for t in range(4)], 1)
    buckets = o_table.shape[2]
    for l in range(layers):
        for t in range(4):
            at = lay.table_at + l * heads
            for h in range(heads):
                o_table[t * heads + h, l : l + 1, :] = sec_ref[t, at + h : at + h + 1, :buckets]
    for out, at in ((o_gain, lay.gain_at), (o_shift, lay.shift_at), (o_scale, lay.scale_at), (o_bias, lay.bias_at)):
        out[...] = tile_ref[at : at + 1, :]
    o_token[...] = tile_ref[lay.token_at, :]


def assemble(lay, bucket_count, res):
    L, own, width, hid, shard = lay.layers, lay.own, lay.width, lay.hidden, lay.shard
    row = ((1, width), F32)
    outs = [
        ((2, own, lay.rows), BF), ((2, own, lay.rows), F32),
        ((L, shard, 3 * own), F32), ((L, shard, own), F32), ((L, shard, hid), F32), ((L, own, 4 * shard), F32),
        ((L, 2 * width), F32), ((L, 4 * hid), F32), ((4 * lay.heads, L, bucket_count), F32),
        row, row, row, row, ((width,), F32),
    ]
    return pl.pallas_call(
        functools.partial(assemble_kernel, lay),
        out_shape=tuple(jax.ShapeDtypeStruct(*spec) for spec in outs),
        in_specs=[pl.BlockSpec(memory_space=pltpu.VMEM)] * len(res),
        name="assemble",
        cost_estimate=pl.CostEstimate(flops=10**6, bytes_accessed=4 * 10**6, transcendentals=0),
    )(*res.values())


def per_device(
    patches, page_mask, mask_token, buckets, ln_gain, ln_shift, layer_scale, branch_bias,
    qkv_weight, qv_bias, out_weight, rel_table, up_weight, up_bias, down_weight, cotangent,
):
    section = lax.axis_index("section")
    sections = lax.axis_size("section")
    ranks = lax.axis_size("dp")
    layers = qkv_weight.shape[0]
    pages, rows, width = patches.shape
    all_heads = rel_table.shape[1]
    bucket_count = rel_table.shape[2]
    head = width // all_heads
    heads = all_heads // sections
    own = heads * head
    hidden = up_weight.shape[2]
    hid = hidden // sections
    prow, pcol = pad_up(rows, 16), pad_up(rows, LANES)
    highs = pad_up(bucket_count, LANES) // LANES
    fused = ranks == 8 and sections == 4
    shard = qkv_weight.shape[1]
    lay = Layout(layers, heads, head, rows, prow, pcol, width, hid, shard, highs, fused)

    operands = dict(
        patches=patches.transpose(1, 0, 2), page_mask=page_mask, mask_token=mask_token,
        buckets=buckets, rel_table=rel_table.transpose(1, 0, 2), cotangent=cotangent.transpose(1, 0, 2),
    )
    if fused:
        operands.update(
            ln_gain=ln_gain, ln_shift=ln_shift, layer_scale=layer_scale, branch_bias=branch_bias,
            qkv_weight=qkv_weight, out_weight=out_weight, up_weight=up_weight, down_weight=down_weight,
            qv_bias=qv_bias, up_bias=up_bias,
        )
        out = list(assemble(lay, bucket_count, run_blocks(lay, operands)))
        for at in (0, 1, 5):
            out[at] = out[at].transpose(0, 2, 1)
        out[8] = out[8].transpose(1, 0, 2)
        return tuple(out)

    unit = down_weight.shape[1] // sections
    cols = width // sections

    def pick(x, axis):
        return lax.dynamic_index_in_dim(x, section, axis, keepdims=False)

    qkv_own = pick(qkv_weight.reshape(layers, shard, 3, sections, own), 3).reshape(layers, shard, 3 * own)
    up_own = pick(up_weight.reshape(layers, shard, ranks, sections, unit), 3).reshape(layers, shard, hid)
    dn_own = pick(down_weight.reshape(layers, sections, unit, width), 1)

    vecs = jnp.concatenate([ln_gain, ln_shift, layer_scale, branch_bias], 0).astype(F32)
    vecs = jnp.pad(vecs, ((0, 4), (0, 0)))
    qv_own = pick(qv_bias.reshape(layers, 2, sections, own), 2).astype(F32)
    qv_vec = jnp.concatenate([qv_own[:, 0], jnp.zeros_like(qv_own[:, 0]), qv_own[:, 1]], 1)
    upb_own = pick(up_bias.reshape(layers, ranks, sections, unit), 2).reshape(layers, hid).astype(F32)
    operands.update(qvb=qv_vec, upb=upb_own)

    def assembled(sec_all):
        qv = sec_all[:, lay.qv_at : lay.qv_at + layers]
        qv = jnp.stack([qv[..., :own], qv[..., 2 * LANES : 2 * LANES + own]], 2)
        qv = qv.transpose(1, 2, 0, 3).reshape(layers, 2 * width)
        up = sec_all[:, lay.up_at : lay.up_at + layers].reshape(sections, layers, ranks, unit)
        up = up.transpose(1, 2, 0, 3).reshape(layers, hidden)
        table = sec_all[:, lay.table_at : lay.table_at + layers * heads, :bucket_count]
        table = table.reshape(sections, layers, heads, bucket_count)
        return qv, up, table.transpose(1, 0, 2, 3).reshape(layers, all_heads, bucket_count)

    def gathered(x):
        return lax.all_gather(x, "dp", axis=1, tiled=True)

    operands.update(
        vec_all=lax.all_gather(vecs, "section", axis=0, tiled=False),
        w_qkv=gathered(qkv_own),
        w_out=pick(gathered(out_weight).reshape(layers, sections, own, width), 1),
        w_up=gathered(up_own),
        w_dn=gathered(dn_own),
    )
    res = run_blocks(lay, operands)

    def scattered(x):
        return lax.psum_scatter(x, "dp", scatter_dimension=1, tiled=True)

    def everywhere(x, axis):
        return lax.all_gather(x, "section", axis=axis, tiled=False)

    sqkv, sup, sdn = scattered(res["g_qkv"]), scattered(res["g_up"]), scattered(res["g_dn"])
    qkv_all = everywhere(sqkv.reshape(layers, shard, 3, own), 3).reshape(layers, shard, 3 * width)
    qkv_cols = 3 * width // sections
    qkv_out = lax.dynamic_slice_in_dim(qkv_all, section * qkv_cols, qkv_cols, 2).astype(F32)
    up_all = everywhere(sup.reshape(layers, shard, ranks, unit), 3).reshape(layers, shard, hidden)
    up_out = lax.dynamic_slice_in_dim(up_all, section * hid, hid, 2).astype(F32)
    dn_all = lax.all_to_all(
        sdn.reshape(layers, unit, sections, cols), "section", split_axis=2, concat_axis=1, tiled=False
    )
    dn_out = dn_all.reshape(layers, sections * unit, cols).astype(F32)
    out_mine = scattered(everywhere(res["g_out"], 1).reshape(layers, width, width))
    out_out = lax.dynamic_slice_in_dim(out_mine, section * cols, cols, 2).astype(F32)

    def pages_of(x):
        both = lax.all_gather(x[:rows], "section", axis=0, tiled=False)[:pages]
        return lax.dynamic_slice_in_dim(both, section * cols, cols, 2)

    once = (section < 2).astype(F32)
    here = (jnp.arange(sections) == section).astype(F32)
    tiles, sec_all = lax.psum(
        (res["tiles"] * once, res["sec"][None] * here[:, None, None]), ("section", "dp")
    )
    tile = pick(tiles, 0)
    return (
        pages_of(res["v4"]), pages_of(res["g0"]), qkv_out, out_out, up_out, dn_out,
        *assembled(sec_all),
        *[tile[at : at + 1] for at in (lay.gain_at, lay.shift_at, lay.scale_at, lay.bias_at)],
        tile[lay.token_at],
    )


def solution(mesh):
    rows3 = P("dp", None, None)
    part = P("section", None)
    weight = P(None, "dp", None)
    in_specs = (
        rows3, P("dp", None), P(), P(), part, part, part, part,
        weight, P(), weight, P(), weight, P(), weight, rows3,
    )
    cut = P("dp", None, "section")
    grad = P(None, "dp", "section")
    out_specs = (cut, cut, grad, grad, grad, grad, P(), P(), P(), part, part, part, part, P())
    return jax.shard_map(per_device, mesh=mesh, in_specs=in_specs, out_specs=out_specs, check_vma=False)
```

```python
import functools
import types

import jax
import jax.numpy as jnp
from jax import lax
from jax.experimental import pallas as pl
from jax.experimental.pallas import tpu as pltpu
from jax.sharding import PartitionSpec as P

EPS = 1e-06
MESH = pl.DeviceIdType.MESH
NEG = -1e30
LANES = 128
BF = jnp.bfloat16
F32 = jnp.float32


def pad_up(x, m):
    return (x + m - 1) // m * m


def nn(a, b):
    return jnp.dot(a, b, preferred_element_type=F32)


def nt(a, b):
    return lax.dot_general(a, b, (((1,), (1,)), ((), ())), preferred_element_type=F32)


def tn(a, b):
    return lax.dot_general(a, b, (((0,), (0,)), ((), ())), preferred_element_type=F32)


class Layout:
    def __init__(self, layers, heads, head, rows, prow, pcol, width, hidden, shard, highs, fused):
        self.layers, self.heads, self.head = layers, heads, head
        self.rows, self.prow, self.pcol, self.width, self.hidden = rows, prow, pcol, width, hidden
        self.shard, self.highs, self.fused = shard, highs, fused
        self.own = heads * head
        self.halves = 2 * layers
        self.scale_at, self.bias_at, self.gain_at, self.shift_at, self.token_at = range(5)
        self.qv_at, self.up_at, self.table_at = 0, layers, 2 * layers
        self.sec_rows = pad_up(2 * layers + layers * heads, 8)


def norm_stats(x):
    mean = jnp.mean(x, -1, keepdims=True)
    centered = x - mean
    r = lax.rsqrt(jnp.mean(centered * centered, -1, keepdims=True) + EPS)
    return centered * r, r


ITEMS = ("qkv", "out", "up", "dn")
QKV, OUT, UP, DN = range(4)


def blocks_kernel(lay, names, *refs):
    r = types.SimpleNamespace(**dict(zip(names, refs)))
    fused = lay.fused
    section = lax.axis_index("section")
    core = lax.rem(section, 2)
    mate_at = section + 1 - 2 * core
    mate = {"section": mate_at}
    far = {"section": lax.rem(section + 2, 4)}
    layers, halves, prow, width = lay.layers, lay.halves, lay.prow, lay.width
    rows, pcol = lay.rows, lay.pcol
    own, hid, hd, heads, shard = lay.own, lay.hidden, lay.head, lay.heads, lay.shard
    v_buf, normed, branch, qkv, probs = r.v_buf, r.normed, r.branch, r.qkv, r.probs
    ctx, act, gate, bgrad, dqkv = r.ctx, r.act, r.gate, r.bgrad, r.dqkv
    acc, g_buf, g4_buf, ds_ref, bias_ref = r.acc, r.g_buf, r.g4_buf, r.ds, r.bias
    tiles, sec, vec_all = r.tiles, r.sec, r.vec_all
    core_out, core_in, far_out, far_in = r.core_out, r.core_in, r.far_out, r.far_in

    def remote(src, dst, send, recv, device):
        return pltpu.make_async_remote_copy(
            src_ref=src, dst_ref=dst, send_sem=send, recv_sem=recv, device_id=device, device_id_type=MESH
        )

    loads = {}

    def load(name, src, dst):
        loads[name] = pltpu.make_async_copy(src, dst, r.load_s.at[len(loads)])
        loads[name].start()

    def loaded(*wanted):
        for name in wanted:
            loads[name].wait()

    if fused:
        load("qkv", r.qkv_weight, r.raw_qkv)
        for n, name in enumerate(("ln_gain", "ln_shift", "layer_scale", "branch_bias")):
            load(name, getattr(r, name), r.raw_vec.at[n])
        load("up", r.up_weight, r.raw_up)
        load("qv_bias", r.qv_bias, r.raw_qvb)
        load("up_bias", r.up_bias, r.raw_upb)
    load("patches", r.patches, r.raw_x)
    load("mask", r.page_mask, r.raw_mask)
    load("token", r.mask_token, r.raw_token)
    load("buckets", r.buckets, r.raw_ids)
    load("table", r.rel_table, r.raw_table)
    load("cotangent", r.cotangent, r.raw_g)

    partners = [mate, far]
    if fused:
        dp = lax.axis_index("dp")
        zi, xi = dp // 2, lax.rem(dp, 2)
        xmate = {"dp": zi * 2 + 1 - xi}
        hi, par = zi // 2, lax.rem(zi, 2)
        znear = {"dp": (zi + 1 - 2 * par) * 2 + xi}
        zfar = {"dp": lax.rem(zi + 2, 4) * 2 + xi}
        snext = [lax.rem(section + o, 4) for o in (1, 2, 3)]
        sprev = [lax.rem(section + 4 - o, 4) for o in (1, 2, 3)]
        sdev = [{"section": t} for t in snext]
        partners = [xmate, znear, zfar] + sdev

    barrier = pltpu.get_barrier_semaphore()
    for other in partners:
        pl.semaphore_signal(barrier, inc=1, device_id=other, device_id_type=MESH)

    sends = []

    def sent(copy, when=None):
        sends.append((copy, when))

    def each_section(body):
        for t in range(4):
            pl.when(section == t)(functools.partial(body, t))

    if fused:
        zfs, zfr, zns, znr = r.ag_zfs, r.ag_zfr, r.ag_zns, r.ag_znr
        xs, xr, ls = r.ag_xs, r.ag_xr, r.ag_ls
        my_out = zi == section
        out_far = lax.rem(section + 2, 4) == zi
        out_even = lax.rem(section + zi, 2) == 0
        out_odd = jnp.logical_not(out_even)

        def item(n):
            l, kind = n // 4, ITEMS[n % 4]
            if kind == "out":
                src = r.out_weight.at[l]
            elif kind == "dn":
                src = r.down_weight.at[l, pl.ds(pl.multiple_of(section * shard, shard), shard)]
            else:
                src = getattr(r, "a_" + kind).at[l]
            return l, kind, src, getattr(r, "w_" + kind)

        def own_copy(n):
            l, kind, src, dst = item(n)
            place = dst.at[l, xi] if kind == "out" else dst.at[l, hi, par, xi]
            return pltpu.make_async_copy(src, place, ls.at[n])

        def far_copy(n):
            l, kind, src, dst = item(n)
            place = dst.at[l, xi] if kind == "out" else dst.at[l, hi, par, xi]
            return remote(src, place, zfs.at[n], zfr.at[n], zfar)

        def near_copy(n):
            l, kind, src, dst = item(n)
            place = dst.at[l, xi] if kind == "out" else dst.at[l, :, par, xi]
            return remote(place, place, zns.at[n], znr.at[n], znear)

        def across(n, stage):
            l, kind, src, dst = item(n)
            if kind == "out":
                place = dst.at[l, xi]
                return remote(src if stage == 0 else place, place, xs.at[n, 0], xr.at[n, 0], xmate)
            place = dst.at[l, :, 1 - par, xi] if stage == 2 else dst.at[l, hi if stage == 0 else 1 - hi, par, xi]
            return remote(src if stage == 0 else place, place, xs.at[n, stage], xr.at[n, stage], xmate)

        def begin(copy, when=None):
            if when is None:
                copy.start()
            else:
                pl.when(when)(copy.start)

        def both_ends(copy, when=None):
            begin(copy, when)
            sent(copy, when)

        def gather_start(n):
            if n >= 4 * layers:
                return
            when = my_out if n % 4 == OUT else None
            both_ends(far_copy(n), when)
            begin(own_copy(n), when)

        def gather_across(n):
            if n >= 4 * layers:
                return
            if n % 4 == OUT:
                begin(across(n, 0), my_out)
                sent(across(n, 0))
            else:
                both_ends(across(n, 0))

        def pump_far(n):
            if n % 4 == OUT:

                @pl.when(out_far)
                def _():
                    far_copy(n).wait_recv()
                    across(n, 1).start()

                pl.when(my_out)(own_copy(n).wait)
                both_ends(near_copy(n), out_even)
                return
            own_copy(n).wait()
            far_copy(n).wait_recv()
            both_ends(near_copy(n))
            both_ends(across(n, 1))

        def pump_near(n):
            if n % 4 == OUT:

                @pl.when(out_odd)
                def _():
                    near_copy(n).wait_recv()
                    across(n, 2).start()

                return
            near_copy(n).wait_recv()
            both_ends(across(n, 2))

        def need(n):
            for stage in range(1 if n % 4 == OUT else 3):
                across(n, stage).wait_recv()

        loaded("qkv")

        def slice_qkv(t):
            for l in range(layers):
                parts = [r.raw_qkv[l, :, m * width + t * own : m * width + (t + 1) * own] for m in range(3)]
                r.a_qkv[l] = jnp.concatenate(parts, 1)

        each_section(slice_qkv)
        loaded("ln_gain", "ln_shift", "layer_scale", "branch_bias")
        vec_own = r.vec_own
        vec_own[...] = jnp.zeros_like(vec_own)
        for n in range(4):
            vec_own[n : n + 1, :] = r.raw_vec[n].astype(F32)
        vec_all[section] = vec_own[...]

        pl.semaphore_wait(barrier, len(partners))

        gather_start(QKV)
        gather_across(QKV)
        for o in range(3):
            copy = remote(vec_own, vec_all.at[section], r.vec_s.at[o], r.vec_r.at[o], sdev[o])
            copy.start()
            sent(copy)
        gather_start(OUT)
        gather_across(OUT)
        loaded("up", "up_bias", "qv_bias")
        unit = own // 2

        def slice_up(t):
            for l in range(layers):
                at = [d * 4 * unit + t * unit for d in range(hid // unit)]
                r.a_up[l] = jnp.concatenate([r.raw_up[l, :, a : a + unit] for a in at], 1)
            r.upb[...] = jnp.concatenate([r.raw_upb[:, a : a + unit].astype(F32) for a in at], 1)
            q = r.raw_qvb[:, t * own : (t + 1) * own].astype(F32)
            v = r.raw_qvb[:, width + t * own : width + (t + 1) * own].astype(F32)
            r.qvb[...] = jnp.concatenate([q, jnp.zeros_like(q), v], 1)

        each_section(slice_up)
        gather_start(UP)
        gather_across(UP)
        gather_across(DN)
    else:
        need = pump_far = pump_near = gather_start = gather_across = lambda n: None
        pl.semaphore_wait(barrier, len(partners))

    def weight(kind, l):
        w = getattr(r, "w_" + kind)[l]
        return w.reshape(-1, w.shape[-1])

    tiles[...] = jnp.zeros_like(tiles)
    sec[...] = jnp.zeros_like(sec)
    loaded("patches", "mask", "token")
    mask_row = (r.raw_mask[0:1, :] * (1 - core) + r.raw_mask[1:2, :] * core).astype(F32)
    at_row = lax.broadcasted_iota(jnp.int32, (prow, rows), 0)
    at_column = lax.broadcasted_iota(jnp.int32, (prow, rows), 1)
    mask = jnp.sum(jnp.where(at_row == at_column, mask_row, 0.0), 1, keepdims=True)
    masked = mask > 0.5
    v_buf[0, prow - 16 :, :] = jnp.zeros((16, width), BF)
    token = r.raw_token[...].reshape(1, width).astype(F32)

    def own_page(ref):
        return jnp.where(core == 0, ref[:, 0, :].astype(F32), ref[:, 1, :].astype(F32))

    v_buf[0, :rows, :] = jnp.where(masked[:rows], token, own_page(r.raw_x)).astype(BF)

    def column_sum(x):
        return jnp.sum(x, 0, keepdims=True)

    def vec(kind, k):
        return vec_all[k, kind : kind + 1, :]

    def share_rows(ref, step):
        return remote(ref.at[0], ref.at[1], r.row_s.at[step], r.row_r.at[step], mate)

    def to_mate(step):
        slot = step % 3
        return remote(core_out.at[slot], core_in.at[slot], r.core_s.at[step], r.core_r.at[step], mate)

    def to_far(step):
        slot = step % 3
        return remote(far_out.at[slot], far_in.at[slot], r.far_s.at[step], r.far_r.at[step], far)

    def sum_up_start(step, part):
        core_out[step % 3] = part(1).astype(BF)
        to_mate(step).start()
        acc[...] = part(0)
        to_mate(step).wait_recv()
        far_out[step % 3] = (acc[...] + core_in[step % 3].astype(F32)).astype(BF)
        to_far(step).start()

    def sum_up_end(step):
        to_far(step).wait_recv()
        total = far_out[step % 3].astype(F32) + far_in[step % 3].astype(F32)
        to_mate(step).wait_send()
        to_far(step).wait_send()
        return total

    def norm_row(k):
        xhat, _ = norm_stats(v_buf[k].astype(F32))
        normed[k, 0] = (xhat * vec(0, k) + vec(1, k)).astype(BF)
        share_rows(normed.at[k], k).start()

    def rows_here(ref, step):
        share_rows(ref, step).wait_recv()

    scale = hd ** -0.5

    def attention_page(l, k, slot):
        fresh = nn(normed[k, slot], weight("qkv", l)) + r.qvb[l : l + 1, :]
        qkv[l, slot] = fresh.astype(BF)
        for h in range(heads):
            q = qkv[l, slot, :, h * hd : (h + 1) * hd]
            kk = qkv[l, slot, :, own + h * hd : own + (h + 1) * hd]
            vv = qkv[l, slot, :, 2 * own + h * hd : 2 * own + (h + 1) * hd]
            s = nt(q, kk) * scale + bias_ref[l * heads + h, :, :prow].astype(F32)
            e = jnp.exp(s - jnp.max(s, -1, keepdims=True))
            p = (e / jnp.sum(e, -1, keepdims=True)).astype(BF)
            probs[l, slot, h] = p
            ctx[l, slot, :, h * hd : (h + 1) * hd] = nn(p, vv).astype(BF)

    def mlp_page(l, k, slot):
        pre = nn(normed[k, slot], weight("up", l)) + r.upb[l : l + 1, :]
        c0, c1 = 0.7978845608028654, 0.044715
        square = pre * pre
        t = jnp.tanh(c0 * (pre + c1 * pre * square))
        act[l, slot] = (0.5 * pre * (1.0 + t)).astype(BF)
        slope = 0.5 * (1.0 + t) + 0.5 * pre * (1.0 - t * t) * (c0 * (1.0 + 3.0 * c1 * square))
        gate[l, slot] = slope.astype(BF)

    def end_forward(k, step):
        b = sum_up_end(step) + vec(3, k)
        branch[k] = b
        return (v_buf[k].astype(F32) + vec(2, k) * b).astype(BF)

    def context_part(l):
        return lambda slot: nn(ctx[l, slot], weight("out", l))

    def hidden_part(l):
        return lambda slot: nn(act[l, slot], weight("dn", l))

    cols = own
    if fused:
        def z_first(n):
            return n in (OUT, 4 + DN)

        def first_copy(n):
            l, kind = n // 4, ITEMS[n % 4]
            part, place = getattr(r, "g_" + kind), getattr(r, "x_" + kind)
            if kind == "out":
                src, dst = (part.at[l], place.at[l]) if z_first(n) else (part.at[l, 1 - xi], place.at[l, 0])
            else:
                src, dst = part.at[l, :, 1 - par] if z_first(n) else part.at[l, :, :, 1 - xi], place.at[l]
            return remote(src, dst, r.rs_xs.at[n], r.rs_xr.at[n], znear if z_first(n) else xmate)

        def second_copy(n):
            l, kind = n // 4, ITEMS[n % 4]
            pair, place = getattr(r, "x_" + kind), getattr(r, "n_" + kind)
            if kind == "out":
                src = pair.at[l, 1 - xi] if z_first(n) else pair.at[l, 0]
            else:
                src = pair.at[l, :, 1 - xi] if z_first(n) else pair.at[l, :, 1 - par]
            return remote(src, place.at[l], r.rs_ns.at[n], r.rs_nr.at[n], xmate if z_first(n) else znear)

        def far_sum_copy(n):
            l, kind = n // 4, ITEMS[n % 4]
            four = getattr(r, "n_" + kind)
            src = four.at[l] if kind == "out" else four.at[l, 1 - hi]
            return remote(src, getattr(r, "f_" + kind).at[l], r.rs_fs.at[n], r.rs_fr.at[n], zfar)

        def added(a, b):
            return (a.astype(F32) + b.astype(F32)).astype(BF)

        def sum_start(n):
            both_ends(first_copy(n), out_odd if n % 4 == OUT and z_first(n) else None)

        def sum_first(n):
            l, kind = n // 4, ITEMS[n % 4]
            pair, part = getattr(r, "x_" + kind), getattr(r, "g_" + kind)
            if kind != "out":
                first_copy(n).wait_recv()
                mine = part[l, :, par] if z_first(n) else part[l, :, :, xi]
                pair[l] = added(mine, pair[l])
                both_ends(second_copy(n))
            elif z_first(n):

                @pl.when(out_even)
                def _():
                    first_copy(n).wait_recv()
                    pair[l] = added(part[l], pair[l])

                both_ends(second_copy(n), out_even)
            else:
                first_copy(n).wait_recv()
                pair[l, 0] = added(part[l, xi], pair[l, 0])
                both_ends(second_copy(n), out_odd)

        def sum_second(n):
            l, kind = n // 4, ITEMS[n % 4]
            four, pair = getattr(r, "n_" + kind), getattr(r, "x_" + kind)
            if kind == "out":

                @pl.when(out_even)
                def _():
                    second_copy(n).wait_recv()
                    four[l] = added(pair[l, xi if z_first(n) else 0], four[l])

                both_ends(far_sum_copy(n), out_far)
                return
            second_copy(n).wait_recv()
            four[l] = added(pair[l, :, xi] if z_first(n) else pair[l, :, par], four[l])
            both_ends(far_sum_copy(n))

        def to_section(n, o, src, dst, device):
            return remote(src, dst, r.rs_ss.at[n, o], r.rs_sr.at[n, o], device)

        def finish_item(n):
            l, kind = n // 4, ITEMS[n % 4]
            blocks, got = getattr(r, "s_" + kind), getattr(r, "t_" + kind)
            if kind == "out":

                @pl.when(my_out)
                def _():
                    far_sum_copy(n).wait_recv()
                    total = r.n_out[l].astype(F32) + r.f_out[l].astype(F32)
                    for t in range(4):
                        blocks[l, t] = total[:, t * cols : (t + 1) * cols].astype(BF)
                    for o in range(3):
                        to_section(n, o, blocks.at[l, snext[o]], got.at[l], sdev[o]).start()
                    got[l] = blocks[l, section]

                for o in range(3):
                    sent(to_section(n, o, blocks.at[l, snext[o]], got.at[l], sdev[o]), my_out)
                return
            far_sum_copy(n).wait_recv()
            total = getattr(r, "n_" + kind)[l, hi].astype(F32) + getattr(r, "f_" + kind)[l].astype(F32)
            for t in range(3 if kind == "qkv" else 4):
                blocks[l, t] = total[:, t * cols : (t + 1) * cols].astype(BF)
            if kind == "qkv":
                for m in range(3):
                    at = 4 * m + section
                    dest, place = at // 3, lax.rem(at, 3)
                    away = dest != section
                    copy = remote(
                        blocks.at[l, m], got.at[l, place], r.rs_ss.at[n, m], r.rs_sr.at[n, place], {"section": dest}
                    )
                    pl.when(away)(copy.start)
                    sent(copy, away)

                    @pl.when(jnp.logical_not(away))
                    def _():
                        got[l, place] = blocks[l, m]

                return
            for o in range(3):
                copy = to_section(n, o, blocks.at[l, snext[o]], got.at[l, section], sdev[o])
                copy.start()
                sent(copy)
            got[l, section] = blocks[l, section]

        def item_here(n):
            l, kind = n // 4, ITEMS[n % 4]
            blocks, got = getattr(r, "s_" + kind), getattr(r, "t_" + kind)
            if kind == "out":
                for o in range(3):
                    copy = to_section(n, o, blocks.at[l, 0], got.at[l], sdev[o])
                    pl.when(sprev[o] == zi)(copy.wait_recv)
            elif kind == "qkv":
                for place in range(3):
                    source = lax.rem(3 * section + place, 4)
                    copy = to_section(n, place, blocks.at[l, 0], got.at[l, place], mate)
                    pl.when(source != section)(copy.wait_recv)
            else:
                for o in range(3):
                    to_section(n, o, blocks.at[l, 0], got.at[l, sprev[o]], sdev[o]).wait_recv()

        def share_page(value, name):
            out, place = getattr(r, name), getattr(r, name + "_s")
            for t in range(4):
                place[t] = value[:, t * cols : (t + 1) * cols]
            out[core] = place[section]
            at = int(name == "o_input")
            copy = remote(place.at[mate_at], out.at[core], r.page_s.at[at], r.page_r.at[at], mate)
            copy.start()
            sent(copy)

        def page_here(name):
            at = int(name == "o_input")
            remote(getattr(r, name + "_s").at[0], getattr(r, name).at[1 - core], r.page_s.at[at], r.page_r.at[at], mate).wait_recv()
    else:
        sum_start = sum_first = sum_second = finish_item = lambda n: None

    def keep_grad(n, value):
        ref = getattr(r, "g_" + ITEMS[n % 4])
        ref[n // 4] = value.astype(BF).reshape(ref.shape[1:])

    def table_sums(l, part, parts):
        groups = 2 * heads
        hist = r.hist
        if part == 0:
            hist[...] = jnp.zeros_like(hist)
        step = 8

        def body(block, carry):
            at = pl.multiple_of(block * step, step)
            ids_all = r.ids[pl.ds(at, step), :]
            grads_all = ds_ref[l * groups : (l + 1) * groups, pl.ds(at, step), :]
            total = None
            for row in range(step):
                ids = ids_all[row : row + 1, :]
                low = ids & (LANES - 1)
                high = lax.shift_right_logical(ids, 7)
                spots = lax.broadcasted_iota(jnp.int32, (LANES, pcol), 0)
                hot = jnp.where(spots == low, 1.0, 0.0).astype(BF)
                grads = grads_all[:, row, :]
                parts = [jnp.where(high == number, grads, 0.0) for number in range(lay.highs)]
                got = nt(jnp.concatenate(parts, 0).astype(BF), hot)
                total = got if total is None else total + got
            hist[...] += total
            return carry

        count = pad_up(rows, step) // step
        lax.fori_loop(count * part // parts, count * (part + 1) // parts, body, 0)
        if part + 1 < parts:
            return
        for h in range(heads):
            at = lay.table_at + l * heads + h
            for number in range(lay.highs):
                first = number * groups + 2 * h
                row = hist[first : first + 1, :] + hist[first + 1 : first + 2, :]
                sec[at : at + 1, number * LANES : (number + 1) * LANES] = row

    def make_bias():
        table = r.table
        table[...] = jnp.zeros_like(table)
        count = r.raw_table.shape[2]

        def own_tables(t):
            for l in range(layers):
                for h in range(heads):
                    at = l * heads + h
                    row = r.raw_table[t * heads + h, l : l + 1, :]
                    table[at : at + 1, :count] = row.astype(F32)

        each_section(own_tables)
        ids_ref = r.ids
        ids_ref[...] = jnp.zeros_like(ids_ref)
        ids_ref[:rows, :rows] = r.raw_ids[...]
        step = 16

        def body(block, carry):
            at = pl.multiple_of(block * step, step)
            for half in range(pcol // LANES):
                lanes = slice(half * LANES, (half + 1) * LANES)
                ids = ids_ref[pl.ds(at, step), lanes]
                low = ids & (LANES - 1)
                high = lax.shift_right_logical(ids, 7)
                column = lax.broadcasted_iota(jnp.int32, (step, LANES), 1) + half * LANES
                inside = column < rows
                picks = [high == number for number in range(lay.highs)]
                for t in range(layers * heads):
                    value = jnp.full((step, LANES), NEG, F32)
                    for number in range(lay.highs):
                        row = table[t : t + 1, number * LANES : (number + 1) * LANES]
                        got = jnp.take_along_axis(jnp.broadcast_to(row, (step, LANES)), low, axis=1)
                        value = jnp.where(picks[number], got, value)
                    value = jnp.where(inside, value, NEG)
                    bias_ref[t, pl.ds(at, step), lanes] = value.astype(BF)
            return carry

        lax.fori_loop(0, prow // step, body, 0)

    loaded("buckets", "table", "cotangent")
    make_bias()
    if fused:
        for o in range(3):
            remote(r.vec_own, vec_all.at[sprev[o]], r.vec_s.at[o], r.vec_r.at[o], sdev[o]).wait_recv()

    last = halves - 1

    def branch_grad(k, g):
        step = halves + k
        low = (g * vec(2, k)).astype(BF)
        bgrad[k, 0] = low
        share_rows(bgrad.at[k], step).start()
        tiles[k, lay.bias_at : lay.bias_at + 1, :] = column_sum(low.astype(F32))

    norm_row(0)
    g4_buf[prow - 16 :, :] = jnp.zeros((16, width), F32)
    g4_buf[:rows, :] = own_page(r.raw_g)
    branch_grad(last, g4_buf[...])
    ds_ref[...] = jnp.zeros_like(ds_ref)

    pump_far(QKV)
    gather_across(4 + QKV)
    pump_far(OUT)
    pump_near(QKV)
    gather_across(4 + UP)
    gather_start(DN)
    pump_near(OUT)
    gather_across(4 + OUT)
    gather_across(4 + DN)
    pump_far(UP)
    for l in range(layers):
        k = 2 * l
        first = 4 * l
        need(first + QKV)
        attention_page(l, k, 0)
        rows_here(normed.at[k], k)
        if l == 0:
            attention_page(l, k, 1)
            gather_start(4 + QKV)
            need(OUT)
            sum_up_start(k, context_part(l))
            pump_near(UP)
            pump_far(DN)
            gather_start(4 + OUT)
            gather_start(4 + UP)
        else:
            attention_page(l, k, 1)
            pump_near(4 + DN)
            need(4 + OUT)
            sum_up_start(k, context_part(l))
        v_buf[k + 1] = end_forward(k, k)
        norm_row(k + 1)
        k = k + 1
        if l == 0:
            pump_near(DN)
            pump_far(4 + QKV)
            gather_start(4 + DN)
        need(first + UP)
        mlp_page(l, k, 0)
        rows_here(normed.at[k], k)
        mlp_page(l, k, 1)
        if l == 0:
            pump_far(4 + OUT)
            pump_far(4 + UP)
            need(DN)
            sum_up_start(k, hidden_part(l))
            pump_near(4 + QKV)
            pump_near(4 + OUT)
            pump_far(4 + DN)
            pump_near(4 + UP)
            v_buf[k + 1] = end_forward(k, k)
            norm_row(k + 1)

    both = 2 * prow

    def whole(ref):
        return ref.reshape(both, ref.shape[-1])

    def back_through_norm(k, g, ng):
        xhat, rr = norm_stats(v_buf[k].astype(F32))
        tiles[k, lay.gain_at : lay.gain_at + 1, :] = column_sum(ng * xhat)
        tiles[k, lay.shift_at : lay.shift_at + 1, :] = column_sum(ng)
        t = ng * vec(0, k)
        inner = t - jnp.mean(t, -1, keepdims=True) - xhat * jnp.mean(t * xhat, -1, keepdims=True)
        return g + rr * inner

    def scale_sum(k, g):
        tiles[k, lay.scale_at : lay.scale_at + 1, :] = column_sum(g * branch[k])

    def mlp_back(l, k, slot):
        dact = nt(bgrad[k, slot], weight("dn", l))
        gate[l, slot] = (dact * gate[l, slot].astype(F32)).astype(BF)

    def mlp_back_part(l):
        return lambda slot: nt(gate[l, slot], weight("up", l))

    def up_grads(l, k):
        dpre = whole(gate[l])
        keep_grad(4 * l + UP, tn(whole(normed[k]), dpre))
        sum_start(4 * l + UP)
        sec[lay.up_at + l : lay.up_at + l + 1, :] = column_sum(dpre.astype(F32))

    l, k = layers - 1, last
    rows_here(bgrad.at[k], halves + k)
    keep_grad(4 * l + DN, tn(whole(act[l]), whole(bgrad[k])))
    sum_start(4 * l + DN)
    need(4 * l + DN)
    mlp_back(l, k, 1)
    mlp_back(l, k, 0)
    sum_up_start(k, mlp_back_part(l))
    up_grads(l, k)
    sum_up_start(k + 1, hidden_part(l))
    g = back_through_norm(k, g4_buf[...], sum_up_end(k))
    g_buf[...] = g.astype(BF).astype(F32)

    def end_of_forward():
        after = end_forward(last, last + 1)
        scale_sum(last, g4_buf[...])
        if fused:
            share_page(after, "o_block")
        else:
            r.v4[...] = after

    forward_sends = len(sends)

    def drain(count):
        for copy, when in sends[:count]:
            if when is None:
                copy.wait_send()
            else:
                pl.when(when)(copy.wait_send)
        del sends[:count]

    for k in reversed(range(last)):
        l = k // 2
        step = 2 * halves - 1 - k
        g = g_buf[...]
        branch_grad(k, g)
        scale_sum(k, g)
        if k == last - 1:
            sum_first(4 * l + DN)
        if k % 2 == 0:

            def attention_back(slot):
                dctx = nt(bgrad[k, slot], weight("out", l)).astype(BF)
                for h in range(heads):
                    q = qkv[l, slot, :, h * hd : (h + 1) * hd]
                    kk = qkv[l, slot, :, own + h * hd : own + (h + 1) * hd]
                    vv = qkv[l, slot, :, 2 * own + h * hd : 2 * own + (h + 1) * hd]
                    dc = dctx[:, h * hd : (h + 1) * hd]
                    low_p = probs[l, slot, h]
                    p = low_p.astype(F32)
                    dp_ = nt(dc, vv)
                    ds = (p * (dp_ - jnp.sum(p * dp_, -1, keepdims=True))).astype(BF)
                    ds_ref[(l * heads + h) * 2 + slot, :, :prow] = ds.astype(F32)
                    dqkv[slot, :, h * hd : (h + 1) * hd] = (nn(ds, kk) * scale).astype(BF)
                    dqkv[slot, :, own + h * hd : own + (h + 1) * hd] = (tn(ds, q) * scale).astype(BF)
                    dqkv[slot, :, 2 * own + h * hd : 2 * own + (h + 1) * hd] = tn(low_p, dc).astype(BF)

            if l == 0:
                rows_here(bgrad.at[k], halves + k)
                keep_grad(OUT, tn(whole(ctx[l]), whole(bgrad[k])))
                sum_start(OUT)
                attention_back(0)
            else:
                attention_back(0)
                rows_here(bgrad.at[k], halves + k)
            attention_back(1)
            if l == 0:
                sum_second(4 + QKV)
                sum_second(4 + OUT)
            sum_up_start(step, lambda slot: nt(dqkv[slot], weight("qkv", l)))
            sum_first(4 * l + (UP if l > 0 else DN))
            dall = whole(dqkv[...])
            keep_grad(4 * l + QKV, tn(whole(normed[k]), dall))
            sum_start(4 * l + QKV)
            sums = column_sum(dall.astype(F32))
            sec[lay.qv_at + l : lay.qv_at + l + 1, :own] = sums[:, :own]
            sec[lay.qv_at + l : lay.qv_at + l + 1, 2 * LANES : 2 * LANES + own] = sums[:, 2 * own :]
            if l > 0:
                keep_grad(4 * l + OUT, tn(whole(ctx[l]), whole(bgrad[k])))
                sum_start(4 * l + OUT)
                end_of_forward()
                table_sums(l, 0, 2)
            else:
                sum_first(OUT)
                table_sums(l, 0, 1)
        else:
            rows_here(bgrad.at[k], halves + k)
            keep_grad(4 * l + DN, tn(whole(act[l]), whole(bgrad[k])))
            sum_start(4 * l + DN)
            sum_second(4 * (l + 1) + DN)
            mlp_back(l, k, 1)
            mlp_back(l, k, 0)
            sum_up_start(step, mlp_back_part(l))
            up_grads(l, k)
            sum_second(4 * (l + 1) + UP)
            sum_first(4 * (l + 1) + QKV)
            table_sums(l + 1, 1, 2)
            drain(forward_sends)
            early_sends = len(sends)
            sum_first(4 * (l + 1) + OUT)
        g = back_through_norm(k, g, sum_up_end(step))
        if k > 0:
            g_buf[...] = g.astype(BF).astype(F32)
    sum_first(UP)

    kept = jnp.where(masked, 0.0, g)
    token_sum = column_sum(jnp.where(masked, g, 0.0))
    for k in range(halves):
        tiles[k, lay.token_at : lay.token_at + 1, :] = token_sum
    for k in range(halves):
        share_rows(normed.at[k], k).wait_send()
        share_rows(bgrad.at[k], halves + k).wait_send()

    if not fused:
        r.g0[...] = kept
        return

    tile_copy = remote(tiles.at[mate_at], r.tile_in, r.small_s.at[0], r.small_r.at[0], mate)
    tile_copy.start()
    sent(tile_copy)
    red, red_in = r.red, r.red_in
    hops = [znear, zfar, xmate]

    def hop_copy(hop):
        return remote(red.at[hop], red_in.at[hop], r.small_s.at[1 + hop], r.small_r.at[1 + hop], hops[hop])

    def hop_start(hop):
        hop_copy(hop).start()
        sent(hop_copy(hop))

    def hop_end(hop):
        hop_copy(hop).wait_recv()
        red[hop + 1] = red[hop] + red_in[hop]

    share_page(kept, "o_input")
    finish_item(4 + DN)
    finish_item(4 + UP)
    tile_copy.wait_recv()
    red[0, :8] = tiles[section] + r.tile_in[...]
    red[0, 8:] = sec[...]
    hop_start(0)
    sum_second(DN)
    finish_item(4 + QKV)
    finish_item(4 + OUT)
    sum_first(QKV)
    hop_end(0)
    hop_start(1)
    sum_second(UP)
    finish_item(DN)
    sum_second(OUT)
    sum_second(QKV)
    hop_end(1)
    hop_start(2)
    finish_item(UP)
    drain(early_sends)
    hop_end(2)
    r.o_tile[...] = red[3, :8]
    sec_all, sec_sum = r.o_sec, r.sec_sum
    sec_sum[...] = red[3, 8:]
    sec_all[section] = sec_sum[...]
    for o in range(3):
        copy = remote(sec_sum, sec_all.at[section], r.sec_s.at[o], r.sec_r.at[o], sdev[o])
        copy.start()
        sent(copy)
    finish_item(OUT)
    finish_item(QKV)
    page_here("o_block")
    page_here("o_input")
    for n in reversed(range(4 * layers)):
        item_here(n)
    for o in range(3):
        remote(sec_sum, sec_all.at[sprev[o]], r.sec_s.at[o], r.sec_r.at[o], sdev[o]).wait_recv()
    drain(len(sends))


def run_blocks(lay, operands):
    L, prow, width, own, hid, shard = lay.layers, lay.prow, lay.width, lay.own, lay.hidden, lay.shard
    halves, steps, heads, pcol, page = lay.halves, 2 * lay.halves, lay.heads, lay.pcol, lay.rows
    rows = (prow, width)
    groups = 2 * heads
    dma = pltpu.SemaphoreType.DMA
    outs, scratch = {}, {}
    items = 4 * L
    wide = {"qkv": 3 * own, "up": hid, "dn": width, "out": width}
    raw = types.SimpleNamespace(**{name: (x.shape, x.dtype) for name, x in operands.items()})
    if lay.fused:
        outs.update(o_block=((2, prow, own), BF))
        outs.update(o_input=((2, prow, own), F32))
        outs.update(t_qkv=((L, 3, shard, own), BF))
        outs.update(t_out=((L, shard, own), BF))
        outs.update(t_up=((L, 4, shard, own), BF))
        outs.update(t_dn=((L, 4, shard, own), BF))
        outs.update(o_tile=((8, width), F32))
        outs.update(o_sec=((4, lay.sec_rows, width), F32))
        scratch.update(tiles=((halves, 8, width), F32))
        scratch.update(sec=((lay.sec_rows, width), F32))
        scratch.update(vec_all=((halves, 8, width), F32))
        scratch.update(vec_own=((8, width), F32))
        for kind, c in wide.items():
            lead = (2,) if kind == "out" else (2, 2, 2)
            scratch["w_" + kind] = ((L,) + lead + (shard, c), BF)
            scratch["g_" + kind] = ((L,) + lead + (shard, c), BF)
            scratch["x_" + kind] = ((L,) + (lead if kind == "out" else lead[:-1]) + (shard, c), BF)
            scratch["n_" + kind] = ((L,) + lead[:-2] + (shard, c), BF)
            scratch["f_" + kind] = ((L, shard, c), BF)
            scratch["s_" + kind] = ((L, 3 if kind == "qkv" else 4, shard, own), BF)
        scratch.update(a_qkv=((L, shard, 3 * own), BF))
        scratch.update(a_up=((L, shard, hid), BF))
        scratch.update(raw_qkv=(raw.qkv_weight, raw.up_weight)[0], raw_up=(raw.qkv_weight, raw.up_weight)[1])
        scratch.update(raw_qvb=(raw.qv_bias, raw.up_bias)[0], raw_upb=(raw.qv_bias, raw.up_bias)[1])
        scratch.update(raw_vec=((4,) + raw.ln_gain[0], BF))
        scratch.update(qvb=(((L, 3 * own), F32), ((L, hid), F32))[0], upb=(((L, 3 * own), F32), ((L, hid), F32))[1])
        scratch.update(o_block_s=(((4, prow, own), BF), ((4, prow, own), F32))[0], o_input_s=(((4, prow, own), BF), ((4, prow, own), F32))[1])
        scratch.update(tile_in=((8, width), F32))
        scratch.update(red=((4, 8 + lay.sec_rows, width), F32))
        scratch.update(red_in=((3, 8 + lay.sec_rows, width), F32))
        scratch.update(sec_sum=((lay.sec_rows, width), F32))
    else:
        outs.update(v4=(rows, BF))
        outs.update(g0=(rows, F32))
        outs.update(tiles=((halves, 8, width), F32))
        outs.update(sec=((lay.sec_rows, width), F32))
        outs.update(g_qkv=(((L, width, 3 * own), BF), ((L, own, width), BF))[0], g_out=(((L, width, 3 * own), BF), ((L, own, width), BF))[1])
        outs.update(g_up=(((L, width, hid), BF), ((L, hid, width), BF))[0], g_dn=(((L, width, hid), BF), ((L, hid, width), BF))[1])
    scratch.update(
        raw_x=raw.patches,
        raw_g=raw.cotangent,
        raw_mask=raw.page_mask,
        raw_token=raw.mask_token,
        raw_ids=raw.buckets,
        raw_table=raw.rel_table,
        ids=((prow, pcol), jnp.int32),
        table=((pad_up(L * heads, 8), lay.highs * LANES), F32),
        bias=((L * heads, prow, pcol), BF),
        v_buf=((halves,) + rows, BF),
        normed=((halves, 2) + rows, BF),
        branch=((halves,) + rows, F32),
        qkv=((L, 2, prow, 3 * own), BF),
        probs=((L, 2, heads, prow, prow), BF),
        ctx=((L, 2, prow, own), BF),
        act=((L, 2, prow, hid), BF),
        gate=((L, 2, prow, hid), BF),
        bgrad=((halves, 2) + rows, BF),
        dqkv=((2, prow, 3 * own), BF),
        acc=(rows, F32),
        g_buf=(rows, F32),
        g4_buf=(rows, F32),
        ds=((L * groups, prow, pcol), F32),
        hist=((lay.highs * groups, LANES), F32),
        core_out=((3,) + rows, BF),
        core_in=((3,) + rows, BF),
        far_out=((3,) + rows, BF),
        far_in=((3,) + rows, BF),
    )
    each = (steps,)
    sems = dict(core_s=each, core_r=each, far_s=each, far_r=each, row_s=each, row_r=each, load_s=(16,))
    if lay.fused:
        sems.update(
            ag_zfs=(items,), ag_zfr=(items,), ag_zns=(items,), ag_znr=(items,),
            ag_xs=(items, 3), ag_xr=(items, 3), ag_ls=(items,), vec_s=(3,), vec_r=(3,),
            rs_xs=(items,), rs_xr=(items,), rs_ns=(items,), rs_nr=(items,), rs_fs=(items,), rs_fr=(items,),
            rs_ss=(items, 3), rs_sr=(items, 3), page_s=(2,), page_r=(2,), small_s=(4,), small_r=(4,),
            sec_s=(3,), sec_r=(3,),
        )
    names = list(operands) + list(outs) + list(scratch) + list(sems)
    in_vmem = ("w_qkv", "w_out", "w_up", "w_dn", "vec_all", "qvb", "upb")
    spaces = [pltpu.VMEM if name in in_vmem else pl.ANY for name in operands]
    results = pl.pallas_call(
        functools.partial(blocks_kernel, lay, names),
        out_shape=tuple(jax.ShapeDtypeStruct(*spec) for spec in outs.values()),
        in_specs=[pl.BlockSpec(memory_space=space) for space in spaces],
        out_specs=[pl.BlockSpec(memory_space=pltpu.VMEM)] * len(outs),
        scratch_shapes=[pltpu.VMEM(*spec) for spec in scratch.values()] + [dma(spec) for spec in sems.values()],
        compiler_params=pltpu.CompilerParams(
            collective_id=1, has_side_effects=True, vmem_limit_bytes=61 * 2**20
        ),
        name="blocks",
        cost_estimate=pl.CostEstimate(flops=9 * 10**9, bytes_accessed=2 * 10**7, transcendentals=10**7),
    )(*operands.values())
    return dict(zip(outs, results))


def assemble_kernel(
    lay, block_ref, input_ref, qkv_ref, out_ref, up_ref, dn_ref, tile_ref, sec_ref,
    o_block, o_input, o_qkv, o_out, o_up, o_dn, o_qv, o_upb, o_table,
    o_gain, o_shift, o_scale, o_bias, o_token,
):
    rows, own, layers, heads = lay.rows, lay.own, lay.layers, lay.heads
    unit = own // 2
    for page in range(2):
        o_block[page] = block_ref[page].astype(F32).T[:, :rows].astype(BF)
        o_input[page] = input_ref[page].T[:, :rows]
    for l in range(layers):
        o_qkv[l] = jnp.concatenate([qkv_ref[l, place] for place in range(3)], 1).astype(F32)
        o_out[l] = out_ref[l].astype(F32)
        pieces = [up_ref[l, t, :, half * unit : (half + 1) * unit] for half in range(2) for t in range(4)]
        o_up[l] = jnp.concatenate(pieces, 1).astype(F32)
        o_dn[l] = dn_ref[l].reshape(4 * lay.shard, own).astype(F32).T
    q = [sec_ref[t, lay.qv_at : lay.qv_at + layers, :own] for t in range(4)]
    v = [sec_ref[t, lay.qv_at : lay.qv_at + layers, 2 * LANES : 2 * LANES + own] for t in range(4)]
    o_qv[...] = jnp.concatenate(q + v, 1)
    up = [sec_ref[t, lay.up_at : lay.up_at + layers, :] for t in range(4)]
    count = lay.hidden // unit
    o_upb[...] = jnp.concatenate([up[t][:, d * unit : (d + 1) * unit] for d in range(count) for t in range(4)], 1)
    buckets = o_table.shape[2]
    for l in range(layers):
        for t in range(4):
            at = lay.table_at + l * heads
            for h in range(heads):
                o_table[t * heads + h, l : l + 1, :] = sec_ref[t, at + h : at + h + 1, :buckets]
    for out, at in ((o_gain, lay.gain_at), (o_shift, lay.shift_at), (o_scale, lay.scale_at), (o_bias, lay.bias_at)):
        out[...] = tile_ref[at : at + 1, :]
    o_token[...] = tile_ref[lay.token_at, :]


def assemble(lay, bucket_count, res):
    L, own, width, hid, shard = lay.layers, lay.own, lay.width, lay.hidden, lay.shard
    row = ((1, width), F32)
    outs = [
        ((2, own, lay.rows), BF), ((2, own, lay.rows), F32),
        ((L, shard, 3 * own), F32), ((L, shard, own), F32), ((L, shard, hid), F32), ((L, own, 4 * shard), F32),
        ((L, 2 * width), F32), ((L, 4 * hid), F32), ((4 * lay.heads, L, bucket_count), F32),
        row, row, row, row, ((width,), F32),
    ]
    return pl.pallas_call(
        functools.partial(assemble_kernel, lay),
        out_shape=tuple(jax.ShapeDtypeStruct(*spec) for spec in outs),
        in_specs=[pl.BlockSpec(memory_space=pltpu.VMEM)] * len(res),
        name="assemble",
        cost_estimate=pl.CostEstimate(flops=10**6, bytes_accessed=4 * 10**6, transcendentals=0),
    )(*res.values())


def per_device(
    patches, page_mask, mask_token, buckets, ln_gain, ln_shift, layer_scale, branch_bias,
    qkv_weight, qv_bias, out_weight, rel_table, up_weight, up_bias, down_weight, cotangent,
):
    section = lax.axis_index("section")
    sections = lax.axis_size("section")
    ranks = lax.axis_size("dp")
    layers = qkv_weight.shape[0]
    pages, rows, width = patches.shape
    all_heads = rel_table.shape[1]
    bucket_count = rel_table.shape[2]
    head = width // all_heads
    heads = all_heads // sections
    own = heads * head
    hidden = up_weight.shape[2]
    hid = hidden // sections
    prow, pcol = pad_up(rows, 16), pad_up(rows, LANES)
    highs = pad_up(bucket_count, LANES) // LANES
    fused = ranks == 8 and sections == 4
    shard = qkv_weight.shape[1]
    lay = Layout(layers, heads, head, rows, prow, pcol, width, hid, shard, highs, fused)

    operands = dict(
        patches=patches.transpose(1, 0, 2), page_mask=page_mask, mask_token=mask_token,
        buckets=buckets, rel_table=rel_table.transpose(1, 0, 2), cotangent=cotangent.transpose(1, 0, 2),
    )
    if fused:
        operands.update(
            ln_gain=ln_gain, ln_shift=ln_shift, layer_scale=layer_scale, branch_bias=branch_bias,
            qkv_weight=qkv_weight, out_weight=out_weight, up_weight=up_weight, down_weight=down_weight,
            qv_bias=qv_bias, up_bias=up_bias,
        )
        out = list(assemble(lay, bucket_count, run_blocks(lay, operands)))
        for at in (0, 1, 5):
            out[at] = out[at].transpose(0, 2, 1)
        out[8] = out[8].transpose(1, 0, 2)
        return tuple(out)

    unit = down_weight.shape[1] // sections
    cols = width // sections

    def pick(x, axis):
        return lax.dynamic_index_in_dim(x, section, axis, keepdims=False)

    qkv_own = pick(qkv_weight.reshape(layers, shard, 3, sections, own), 3).reshape(layers, shard, 3 * own)
    up_own = pick(up_weight.reshape(layers, shard, ranks, sections, unit), 3).reshape(layers, shard, hid)
    dn_own = pick(down_weight.reshape(layers, sections, unit, width), 1)

    vecs = jnp.concatenate([ln_gain, ln_shift, layer_scale, branch_bias], 0).astype(F32)
    vecs = jnp.pad(vecs, ((0, 4), (0, 0)))
    qv_own = pick(qv_bias.reshape(layers, 2, sections, own), 2).astype(F32)
    qv_vec = jnp.concatenate([qv_own[:, 0], jnp.zeros_like(qv_own[:, 0]), qv_own[:, 1]], 1)
    upb_own = pick(up_bias.reshape(layers, ranks, sections, unit), 2).reshape(layers, hid).astype(F32)
    operands.update(qvb=qv_vec, upb=upb_own)

    def assembled(sec_all):
        qv = sec_all[:, lay.qv_at : lay.qv_at + layers]
        qv = jnp.stack([qv[..., :own], qv[..., 2 * LANES : 2 * LANES + own]], 2)
        qv = qv.transpose(1, 2, 0, 3).reshape(layers, 2 * width)
        up = sec_all[:, lay.up_at : lay.up_at + layers].reshape(sections, layers, ranks, unit)
        up = up.transpose(1, 2, 0, 3).reshape(layers, hidden)
        table = sec_all[:, lay.table_at : lay.table_at + layers * heads, :bucket_count]
        table = table.reshape(sections, layers, heads, bucket_count)
        return qv, up, table.transpose(1, 0, 2, 3).reshape(layers, all_heads, bucket_count)

    def gathered(x):
        return lax.all_gather(x, "dp", axis=1, tiled=True)

    operands.update(
        vec_all=lax.all_gather(vecs, "section", axis=0, tiled=False),
        w_qkv=gathered(qkv_own),
        w_out=pick(gathered(out_weight).reshape(layers, sections, own, width), 1),
        w_up=gathered(up_own),
        w_dn=gathered(dn_own),
    )
    res = run_blocks(lay, operands)

    def scattered(x):
        return lax.psum_scatter(x, "dp", scatter_dimension=1, tiled=True)

    def everywhere(x, axis):
        return lax.all_gather(x, "section", axis=axis, tiled=False)

    sqkv, sup, sdn = scattered(res["g_qkv"]), scattered(res["g_up"]), scattered(res["g_dn"])
    qkv_all = everywhere(sqkv.reshape(layers, shard, 3, own), 3).reshape(layers, shard, 3 * width)
    qkv_cols = 3 * width // sections
    qkv_out = lax.dynamic_slice_in_dim(qkv_all, section * qkv_cols, qkv_cols, 2).astype(F32)
    up_all = everywhere(sup.reshape(layers, shard, ranks, unit), 3).reshape(layers, shard, hidden)
    up_out = lax.dynamic_slice_in_dim(up_all, section * hid, hid, 2).astype(F32)
    dn_all = lax.all_to_all(
        sdn.reshape(layers, unit, sections, cols), "section", split_axis=2, concat_axis=1, tiled=False
    )
    dn_out = dn_all.reshape(layers, sections * unit, cols).astype(F32)
    out_mine = scattered(everywhere(res["g_out"], 1).reshape(layers, width, width))
    out_out = lax.dynamic_slice_in_dim(out_mine, section * cols, cols, 2).astype(F32)

    def pages_of(x):
        both = lax.all_gather(x[:rows], "section", axis=0, tiled=False)[:pages]
        return lax.dynamic_slice_in_dim(both, section * cols, cols, 2)

    once = (section < 2).astype(F32)
    here = (jnp.arange(sections) == section).astype(F32)
    tiles, sec_all = lax.psum(
        (res["tiles"] * once, res["sec"][None] * here[:, None, None]), ("section", "dp")
    )
    tile = pick(tiles, 0)
    return (
        pages_of(res["v4"]), pages_of(res["g0"]), qkv_out, out_out, up_out, dn_out,
        *assembled(sec_all),
        *[tile[at : at + 1] for at in (lay.gain_at, lay.shift_at, lay.scale_at, lay.bias_at)],
        tile[lay.token_at],
    )


def solution(mesh):
    rows3 = P("dp", None, None)
    part = P("section", None)
    weight = P(None, "dp", None)
    in_specs = (
        rows3, P("dp", None), P(), P(), part, part, part, part,
        weight, P(), weight, P(), weight, P(), weight, rows3,
    )
    cut = P("dp", None, "section")
    grad = P(None, "dp", "section")
    out_specs = (cut, cut, grad, grad, grad, grad, P(), P(), P(), part, part, part, part, P())
    return jax.shard_map(per_device, mesh=mesh, in_specs=in_specs, out_specs=out_specs, check_vma=False)
```

```python
import functools
import types

import jax
import jax.numpy as jnp
from jax import lax
from jax.experimental import pallas as pl
from jax.experimental.pallas import tpu as pltpu
from jax.sharding import PartitionSpec as P

EPS = 1e-06
MESH = pl.DeviceIdType.MESH
NEG = -1e30
LANES = 128
BF = jnp.bfloat16
F32 = jnp.float32


def pad_up(x, m):
    return (x + m - 1) // m * m


def nn(a, b):
    return jnp.dot(a, b, preferred_element_type=F32)


def nt(a, b):
    return lax.dot_general(a, b, (((1,), (1,)), ((), ())), preferred_element_type=F32)


def tn(a, b):
    return lax.dot_general(a, b, (((0,), (0,)), ((), ())), preferred_element_type=F32)


class Layout:
    def __init__(self, layers, heads, head, rows, prow, pcol, width, hidden, shard, highs, fused):
        self.layers, self.heads, self.head = layers, heads, head
        self.rows, self.prow, self.pcol, self.width, self.hidden = rows, prow, pcol, width, hidden
        self.shard, self.highs, self.fused = shard, highs, fused
        self.own = heads * head
        self.halves = 2 * layers
        self.scale_at, self.bias_at, self.gain_at, self.shift_at, self.token_at = range(5)
        self.qv_at, self.up_at, self.table_at = 0, layers, 2 * layers
        self.sec_rows = pad_up(2 * layers + layers * heads, 8)


def norm_stats(x):
    mean = jnp.mean(x, -1, keepdims=True)
    centered = x - mean
    r = lax.rsqrt(jnp.mean(centered * centered, -1, keepdims=True) + EPS)
    return centered * r, r


ITEMS = ("qkv", "out", "up", "dn")
QKV, OUT, UP, DN = range(4)
UPB = 8


def blocks_kernel(lay, names, *refs):
    r = types.SimpleNamespace(**dict(zip(names, refs)))
    fused = lay.fused
    section = lax.axis_index("section")
    core = lax.rem(section, 2)
    mate_at = section + 1 - 2 * core
    mate = {"section": mate_at}
    far = {"section": lax.rem(section + 2, 4)}
    layers, halves, prow, width = lay.layers, lay.halves, lay.prow, lay.width
    rows, pcol = lay.rows, lay.pcol
    own, hid, hd, heads, shard = lay.own, lay.hidden, lay.head, lay.heads, lay.shard
    v_buf, normed, branch, qkv, probs = r.v_buf, r.normed, r.branch, r.qkv, r.probs
    ctx, act, gate, bgrad, dqkv = r.ctx, r.act, r.gate, r.bgrad, r.dqkv
    acc, g_buf, g4_buf, ds_ref, bias_ref = r.acc, r.g_buf, r.g4_buf, r.ds, r.bias
    tiles, sec, vec_all = r.tiles, r.sec, r.vec_all
    core_out, core_in, far_out, far_in = r.core_out, r.core_in, r.far_out, r.far_in

    def remote(src, dst, send, recv, device):
        return pltpu.make_async_remote_copy(
            src_ref=src, dst_ref=dst, send_sem=send, recv_sem=recv, device_id=device, device_id_type=MESH
        )

    loads = {}

    def load(name, src, dst):
        loads[name] = pltpu.make_async_copy(src, dst, r.load_s.at[len(loads)])
        loads[name].start()

    def loaded(*wanted):
        for name in wanted:
            loads[name].wait()

    if fused:
        load("qkv", r.qkv_weight, r.raw_qkv)
        for n, name in enumerate(("ln_gain", "ln_shift", "layer_scale", "branch_bias")):
            load(name, getattr(r, name), r.raw_vec.at[n])
        load("up", r.up_weight, r.raw_up)
        load("qv_bias", r.qv_bias, r.raw_qvb)
        load("up_bias", r.up_bias, r.raw_upb)
    load("patches", r.patches, r.raw_x)
    load("mask", r.page_mask, r.raw_mask)
    load("token", r.mask_token, r.raw_token)
    load("buckets", r.buckets, r.raw_ids)
    load("table", r.rel_table, r.raw_table)
    load("cotangent", r.cotangent, r.raw_g)

    partners = [mate, far]
    if fused:
        dp = lax.axis_index("dp")
        zi, xi = dp // 2, lax.rem(dp, 2)
        xmate = {"dp": zi * 2 + 1 - xi}
        hi, par = zi // 2, lax.rem(zi, 2)
        znear = {"dp": (zi + 1 - 2 * par) * 2 + xi}
        zfar = {"dp": lax.rem(zi + 2, 4) * 2 + xi}
        snext = [lax.rem(section + o, 4) for o in (1, 2, 3)]
        sprev = [lax.rem(section + 4 - o, 4) for o in (1, 2, 3)]
        sdev = [{"section": t} for t in snext]
        partners = [xmate, znear, zfar] + sdev

    barrier = pltpu.get_barrier_semaphore()
    for other in partners:
        pl.semaphore_signal(barrier, inc=1, device_id=other, device_id_type=MESH)

    sends = []

    def sent(copy, when=None):
        sends.append((copy, when))

    def each_section(body):
        for t in range(4):
            pl.when(section == t)(functools.partial(body, t))

    if fused:
        zfs, zfr, zns, znr = r.ag_zfs, r.ag_zfr, r.ag_zns, r.ag_znr
        xs, xr, ls = r.ag_xs, r.ag_xr, r.ag_ls
        my_out = zi == section
        out_far = lax.rem(section + 2, 4) == zi
        out_even = lax.rem(section + zi, 2) == 0
        out_odd = jnp.logical_not(out_even)

        def item(n):
            l, kind = n // 4, ITEMS[n % 4]
            if kind == "out":
                src = r.out_weight.at[l]
            elif kind == "dn":
                src = r.down_weight.at[l, pl.ds(pl.multiple_of(section * shard, shard), shard)]
            else:
                src = getattr(r, "a_" + kind).at[l]
            return l, kind, src, getattr(r, "w_" + kind)

        def own_copy(n):
            l, kind, src, dst = item(n)
            place = dst.at[l, xi] if kind == "out" else dst.at[l, hi, par, xi]
            return pltpu.make_async_copy(src, place, ls.at[n])

        def far_copy(n):
            l, kind, src, dst = item(n)
            place = dst.at[l, xi] if kind == "out" else dst.at[l, hi, par, xi]
            return remote(src, place, zfs.at[n], zfr.at[n], zfar)

        def near_copy(n):
            l, kind, src, dst = item(n)
            place = dst.at[l, xi] if kind == "out" else dst.at[l, :, par, xi]
            return remote(place, place, zns.at[n], znr.at[n], znear)

        def across(n, stage):
            l, kind, src, dst = item(n)
            if kind == "out":
                place = dst.at[l, xi]
                return remote(src if stage == 0 else place, place, xs.at[n, 0], xr.at[n, 0], xmate)
            place = dst.at[l, :, 1 - par, xi] if stage == 2 else dst.at[l, hi if stage == 0 else 1 - hi, par, xi]
            return remote(src if stage == 0 else place, place, xs.at[n, stage], xr.at[n, stage], xmate)

        def begin(copy, when=None):
            if when is None:
                copy.start()
            else:
                pl.when(when)(copy.start)

        def both_ends(copy, when=None):
            begin(copy, when)
            sent(copy, when)

        def gather_start(n):
            if n >= 4 * layers:
                return
            when = my_out if n % 4 == OUT else None
            both_ends(far_copy(n), when)
            begin(own_copy(n), when)

        def gather_across(n):
            if n >= 4 * layers:
                return
            if n % 4 == OUT:
                begin(across(n, 0), my_out)
                sent(across(n, 0))
            else:
                both_ends(across(n, 0))

        def pump_far(n):
            if n % 4 == OUT:

                @pl.when(out_far)
                def _():
                    far_copy(n).wait_recv()
                    across(n, 1).start()

                pl.when(my_out)(own_copy(n).wait)
                both_ends(near_copy(n), out_even)
                return
            own_copy(n).wait()
            far_copy(n).wait_recv()
            both_ends(near_copy(n))
            both_ends(across(n, 1))

        def pump_near(n):
            if n % 4 == OUT:

                @pl.when(out_odd)
                def _():
                    near_copy(n).wait_recv()
                    across(n, 2).start()

                return
            near_copy(n).wait_recv()
            both_ends(across(n, 2))

        def need(n):
            for stage in range(1 if n % 4 == OUT else 3):
                across(n, stage).wait_recv()

        loaded("qkv")

        def slice_qkv(t):
            for l in range(layers):
                parts = [r.raw_qkv[l, :, m * width + t * own : m * width + (t + 1) * own] for m in range(3)]
                r.a_qkv[l] = jnp.concatenate(parts, 1)

        each_section(slice_qkv)
        loaded("ln_gain", "ln_shift", "layer_scale", "branch_bias")
        vec_own = r.vec_own
        vec_own[...] = jnp.zeros_like(vec_own)
        for n in range(4):
            vec_own[n : n + 1, :] = r.raw_vec[n].astype(F32)
        vec_all[section] = vec_own[...]

        pl.semaphore_wait(barrier, len(partners))

        gather_start(QKV)
        gather_across(QKV)
        for o in range(3):
            copy = remote(vec_own, vec_all.at[section], r.vec_s.at[o], r.vec_r.at[o], sdev[o])
            copy.start()
            sent(copy)
        gather_start(OUT)
        gather_across(OUT)
        loaded("up", "up_bias", "qv_bias")
        unit = own // 2

        def slice_up(t):
            for l in range(layers):
                at = [d * 4 * unit + t * unit for d in range(hid // unit)]
                r.a_up[l] = jnp.concatenate([r.raw_up[l, :, a : a + unit] for a in at], 1)
            r.upb[...] = jnp.concatenate([r.raw_upb[:, a : a + unit].astype(F32) for a in at], 1)
            q = r.raw_qvb[:, t * own : (t + 1) * own].astype(F32)
            v = r.raw_qvb[:, width + t * own : width + (t + 1) * own].astype(F32)
            r.qvb[...] = jnp.concatenate([q, jnp.zeros_like(q), v], 1)

        each_section(slice_up)
        gather_start(UP)
        gather_across(UP)
        gather_across(DN)
    else:
        need = pump_far = pump_near = gather_start = gather_across = lambda n: None
        pl.semaphore_wait(barrier, len(partners))

    def weight(kind, l):
        w = getattr(r, "w_" + kind)[l]
        return w.reshape(-1, w.shape[-1])

    tiles[...] = jnp.zeros_like(tiles)
    sec[...] = jnp.zeros_like(sec)
    loaded("patches", "mask", "token")
    mask_row = (r.raw_mask[0:1, :] * (1 - core) + r.raw_mask[1:2, :] * core).astype(F32)
    at_row = lax.broadcasted_iota(jnp.int32, (prow, rows), 0)
    at_column = lax.broadcasted_iota(jnp.int32, (prow, rows), 1)
    mask = jnp.sum(jnp.where(at_row == at_column, mask_row, 0.0), 1, keepdims=True)
    masked = mask > 0.5
    v_buf[0, prow - 16 :, :] = jnp.zeros((16, width), BF)
    token = r.raw_token[...].reshape(1, width).astype(F32)

    def own_page(ref):
        return jnp.where(core == 0, ref[:, 0, :].astype(F32), ref[:, 1, :].astype(F32))

    v_buf[0, :rows, :] = jnp.where(masked[:rows], token, own_page(r.raw_x)).astype(BF)

    def column_sum(x):
        return jnp.sum(x, 0, keepdims=True)

    def vec(kind, k):
        return vec_all[k, kind : kind + 1, :]

    def share_rows(ref, step):
        return remote(ref.at[0], ref.at[1], r.row_s.at[step], r.row_r.at[step], mate)

    cut = prow // 32 * 16
    parts = (slice(0, cut), slice(cut, prow))

    def to_mate(step, part):
        slot = step % 3
        rows_of = pl.ds(parts[part].start, parts[part].stop - parts[part].start)
        return remote(
            core_out.at[slot, rows_of], core_in.at[slot, rows_of],
            r.core_s.at[step, part], r.core_r.at[step, part], mate,
        )

    def to_far(step, part):
        slot = step % 3
        rows_of = pl.ds(parts[part].start, parts[part].stop - parts[part].start)
        return remote(
            far_out.at[slot, rows_of], far_in.at[slot, rows_of],
            r.far_s.at[step, part], r.far_r.at[step, part], far,
        )

    def sum_up_start(step, part):
        slot = step % 3
        for n, rows_of in enumerate(parts):
            core_out[slot, rows_of] = part(1, rows_of).astype(BF)
            to_mate(step, n).start()
        for n, rows_of in enumerate(parts):
            acc[rows_of] = part(0, rows_of)
            to_mate(step, n).wait_recv()
            far_out[slot, rows_of] = (acc[rows_of] + core_in[slot, rows_of].astype(F32)).astype(BF)
            to_far(step, n).start()

    def sum_up_end(step):
        slot = step % 3
        for n in range(2):
            to_far(step, n).wait_recv()
        total = far_out[slot].astype(F32) + far_in[slot].astype(F32)
        for n in range(2):
            to_mate(step, n).wait_send()
            to_far(step, n).wait_send()
        return total

    def norm_row(k):
        xhat, _ = norm_stats(v_buf[k].astype(F32))
        normed[k, 0] = (xhat * vec(0, k) + vec(1, k)).astype(BF)
        share_rows(normed.at[k], k).start()

    def rows_here(ref, step):
        share_rows(ref, step).wait_recv()

    scale = hd ** -0.5

    def attention_page(l, k, slot):
        fresh = nn(normed[k, slot], weight("qkv", l)) + r.qvb[l : l + 1, :]
        qkv[l, slot] = fresh.astype(BF)
        for h in range(heads):
            q = qkv[l, slot, :, h * hd : (h + 1) * hd]
            kk = qkv[l, slot, :, own + h * hd : own + (h + 1) * hd]
            vv = qkv[l, slot, :, 2 * own + h * hd : 2 * own + (h + 1) * hd]
            s = nt(q, kk) * scale + bias_ref[l * heads + h, :, :prow].astype(F32)
            e = jnp.exp(s - jnp.max(s, -1, keepdims=True))
            p = (e / jnp.sum(e, -1, keepdims=True)).astype(BF)
            probs[l, slot, h] = p
            ctx[l, slot, :, h * hd : (h + 1) * hd] = nn(p, vv).astype(BF)

    def mlp_page(l, k, slot):
        pre = nn(normed[k, slot], weight("up", l)) + r.upb[l : l + 1, :]
        c0, c1 = 0.7978845608028654, 0.044715
        square = pre * pre
        t = jnp.tanh(c0 * (pre + c1 * pre * square))
        act[l, slot] = (0.5 * pre * (1.0 + t)).astype(BF)
        slope = 0.5 * (1.0 + t) + 0.5 * pre * (1.0 - t * t) * (c0 * (1.0 + 3.0 * c1 * square))
        gate[l, slot] = slope.astype(BF)

    def end_forward(k, step):
        b = sum_up_end(step) + vec(3, k)
        branch[k] = b
        return (v_buf[k].astype(F32) + vec(2, k) * b).astype(BF)

    def context_part(l):
        return lambda slot, at: nn(ctx[l, slot, at], weight("out", l))

    def hidden_part(l):
        return lambda slot, at: nn(act[l, slot, at], weight("dn", l))

    cols = own
    if fused:
        def z_first(n):
            return n in (OUT, 4 + DN)

        def parts_of(n):
            if n == UPB:
                return 0, "up", slice(hid // 2, hid)
            return n // 4, ITEMS[n % 4], slice(0, hid // 2) if n == UP else slice(None)

        def first_copy(n):
            l, kind, at = parts_of(n)
            part, place = getattr(r, "g_" + kind), getattr(r, "x_" + kind)
            if kind == "out":
                src, dst = (part.at[l], place.at[l]) if z_first(n) else (part.at[l, 1 - xi], place.at[l, 0])
            else:
                src = part.at[l, :, 1 - par, :, :, at] if z_first(n) else part.at[l, :, :, 1 - xi, :, at]
                dst = place.at[l, :, :, :, at]
            return remote(src, dst, r.rs_xs.at[n], r.rs_xr.at[n], znear if z_first(n) else xmate)

        def second_copy(n):
            l, kind, at = parts_of(n)
            pair, place = getattr(r, "x_" + kind), getattr(r, "n_" + kind)
            if kind == "out":
                src, dst = pair.at[l, 1 - xi] if z_first(n) else pair.at[l, 0], place.at[l]
            else:
                src = pair.at[l, :, 1 - xi, :, at] if z_first(n) else pair.at[l, :, 1 - par, :, at]
                dst = place.at[l, :, :, at]
            return remote(src, dst, r.rs_ns.at[n], r.rs_nr.at[n], xmate if z_first(n) else znear)

        def far_sum_copy(n):
            l, kind, at = parts_of(n)
            four, place = getattr(r, "n_" + kind), getattr(r, "f_" + kind)
            src, dst = (four.at[l], place.at[l]) if kind == "out" else (four.at[l, 1 - hi, :, at], place.at[l, :, at])
            return remote(src, dst, r.rs_fs.at[n], r.rs_fr.at[n], zfar)

        def added(a, b):
            return (a.astype(F32) + b.astype(F32)).astype(BF)

        def sum_start(n):
            both_ends(first_copy(n), out_odd if n % 4 == OUT and z_first(n) else None)

        def sum_first(n):
            l, kind, at = parts_of(n)
            pair, part = getattr(r, "x_" + kind), getattr(r, "g_" + kind)
            if kind != "out":
                first_copy(n).wait_recv()
                mine = part[l, :, par, :, :, at] if z_first(n) else part[l, :, :, xi, :, at]
                pair[l, :, :, :, at] = added(mine, pair[l, :, :, :, at])
                both_ends(second_copy(n))
            elif z_first(n):

                @pl.when(out_even)
                def _():
                    first_copy(n).wait_recv()
                    pair[l] = added(part[l], pair[l])

                both_ends(second_copy(n), out_even)
            else:
                first_copy(n).wait_recv()
                pair[l, 0] = added(part[l, xi], pair[l, 0])
                both_ends(second_copy(n), out_odd)

        def sum_second(n):
            l, kind, at = parts_of(n)
            four, pair = getattr(r, "n_" + kind), getattr(r, "x_" + kind)
            if kind == "out":

                @pl.when(out_even)
                def _():
                    second_copy(n).wait_recv()
                    four[l] = added(pair[l, xi if z_first(n) else 0], four[l])

                both_ends(far_sum_copy(n), out_far)
                return
            second_copy(n).wait_recv()
            mine = pair[l, :, xi, :, at] if z_first(n) else pair[l, :, par, :, at]
            four[l, :, :, at] = added(mine, four[l, :, :, at])
            both_ends(far_sum_copy(n))

        def to_section(n, o, src, dst, device):
            return remote(src, dst, r.rs_ss.at[n, o], r.rs_sr.at[n, o], device)

        def finish_item(n):
            l, kind, at = parts_of(n)
            blocks, got = getattr(r, "s_" + kind), getattr(r, "t_" + kind)
            if kind == "out":

                @pl.when(my_out)
                def _():
                    far_sum_copy(n).wait_recv()
                    total = r.n_out[l].astype(F32) + r.f_out[l].astype(F32)
                    for t in range(4):
                        blocks[l, t] = total[:, t * cols : (t + 1) * cols].astype(BF)
                    for o in range(3):
                        to_section(n, o, blocks.at[l, snext[o]], got.at[l], sdev[o]).start()
                    got[l] = blocks[l, section]

                for o in range(3):
                    sent(to_section(n, o, blocks.at[l, snext[o]], got.at[l], sdev[o]), my_out)
                return
            far_sum_copy(n).wait_recv()
            total = getattr(r, "n_" + kind)[l, hi, :, at].astype(F32) + getattr(r, "f_" + kind)[l, :, at].astype(F32)
            if n in (UP, UPB):
                half = int(n == UPB)
                for t in range(2):
                    blocks[l, 2 * half + t] = total[:, t * cols : (t + 1) * cols].astype(BF)
                for o in range(3):
                    copy = to_section(UP, o, blocks.at[l, snext[o]], got.at[l, section], sdev[o])
                    both_ends(copy, snext[o] // 2 == half)

                @pl.when(section // 2 == half)
                def _():
                    got[l, section] = blocks[l, section]

                return
            for t in range(3 if kind == "qkv" else 4):
                blocks[l, t] = total[:, t * cols : (t + 1) * cols].astype(BF)
            if kind == "qkv":
                for m in range(3):
                    at = 4 * m + section
                    dest, place = at // 3, lax.rem(at, 3)
                    away = dest != section
                    copy = remote(
                        blocks.at[l, m], got.at[l, place], r.rs_ss.at[n, m], r.rs_sr.at[n, place], {"section": dest}
                    )
                    pl.when(away)(copy.start)
                    sent(copy, away)

                    @pl.when(jnp.logical_not(away))
                    def _():
                        got[l, place] = blocks[l, m]

                return
            for o in range(3):
                copy = to_section(n, o, blocks.at[l, snext[o]], got.at[l, section], sdev[o])
                copy.start()
                sent(copy)
            got[l, section] = blocks[l, section]

        def item_here(n):
            l, kind = n // 4, ITEMS[n % 4]
            blocks, got = getattr(r, "s_" + kind), getattr(r, "t_" + kind)
            if kind == "out":
                for o in range(3):
                    copy = to_section(n, o, blocks.at[l, 0], got.at[l], sdev[o])
                    pl.when(sprev[o] == zi)(copy.wait_recv)
            elif kind == "qkv":
                for place in range(3):
                    source = lax.rem(3 * section + place, 4)
                    copy = to_section(n, place, blocks.at[l, 0], got.at[l, place], mate)
                    pl.when(source != section)(copy.wait_recv)
            else:
                for o in range(3):
                    to_section(n, o, blocks.at[l, 0], got.at[l, sprev[o]], sdev[o]).wait_recv()

        def share_page(value, name):
            out, place = getattr(r, name), getattr(r, name + "_s")
            for t in range(4):
                place[t] = value[:, t * cols : (t + 1) * cols]
            out[core] = place[section]
            at = int(name == "o_input")
            copy = remote(place.at[mate_at], out.at[core], r.page_s.at[at], r.page_r.at[at], mate)
            copy.start()
            sent(copy)

        def page_here(name):
            at = int(name == "o_input")
            remote(getattr(r, name + "_s").at[0], getattr(r, name).at[1 - core], r.page_s.at[at], r.page_r.at[at], mate).wait_recv()
    else:
        sum_start = sum_first = sum_second = finish_item = lambda n: None

    def keep_grad(n, value):
        ref = getattr(r, "g_" + ITEMS[n % 4])
        ref[n // 4] = value.astype(BF).reshape(ref.shape[1:])

    def table_sums(l, part, parts):
        groups = 2 * heads
        hist = r.hist
        if part == 0:
            hist[...] = jnp.zeros_like(hist)
        step = 8

        def body(block, carry):
            at = pl.multiple_of(block * step, step)
            ids_all = r.ids[pl.ds(at, step), :]
            grads_all = ds_ref[l * groups : (l + 1) * groups, pl.ds(at, step), :]
            total = None
            for row in range(step):
                ids = ids_all[row : row + 1, :]
                low = ids & (LANES - 1)
                high = lax.shift_right_logical(ids, 7)
                spots = lax.broadcasted_iota(jnp.int32, (LANES, pcol), 0)
                hot = jnp.where(spots == low, 1.0, 0.0).astype(BF)
                grads = grads_all[:, row, :]
                parts = [jnp.where(high == number, grads, 0.0) for number in range(lay.highs)]
                got = nt(jnp.concatenate(parts, 0).astype(BF), hot)
                total = got if total is None else total + got
            hist[...] += total
            return carry

        count = pad_up(rows, step) // step
        lax.fori_loop(count * part // parts, count * (part + 1) // parts, body, 0)
        if part + 1 < parts:
            return
        for h in range(heads):
            at = lay.table_at + l * heads + h
            for number in range(lay.highs):
                first = number * groups + 2 * h
                row = hist[first : first + 1, :] + hist[first + 1 : first + 2, :]
                sec[at : at + 1, number * LANES : (number + 1) * LANES] = row

    def make_bias():
        table = r.table
        table[...] = jnp.zeros_like(table)
        count = r.raw_table.shape[2]

        def own_tables(t):
            for l in range(layers):
                for h in range(heads):
                    at = l * heads + h
                    row = r.raw_table[t * heads + h, l : l + 1, :]
                    table[at : at + 1, :count] = row.astype(F32)

        each_section(own_tables)
        ids_ref = r.ids
        ids_ref[...] = jnp.zeros_like(ids_ref)
        ids_ref[:rows, :rows] = r.raw_ids[...]
        step = 16

        def body(block, carry):
            at = pl.multiple_of(block * step, step)
            for half in range(pcol // LANES):
                lanes = slice(half * LANES, (half + 1) * LANES)
                ids = ids_ref[pl.ds(at, step), lanes]
                low = ids & (LANES - 1)
                high = lax.shift_right_logical(ids, 7)
                column = lax.broadcasted_iota(jnp.int32, (step, LANES), 1) + half * LANES
                inside = column < rows
                picks = [high == number for number in range(lay.highs)]
                for t in range(layers * heads):
                    value = jnp.full((step, LANES), NEG, F32)
                    for number in range(lay.highs):
                        row = table[t : t + 1, number * LANES : (number + 1) * LANES]
                        got = jnp.take_along_axis(jnp.broadcast_to(row, (step, LANES)), low, axis=1)
                        value = jnp.where(picks[number], got, value)
                    value = jnp.where(inside, value, NEG)
                    bias_ref[t, pl.ds(at, step), lanes] = value.astype(BF)
            return carry

        lax.fori_loop(0, prow // step, body, 0)

    loaded("buckets", "table", "cotangent")
    make_bias()
    if fused:
        for o in range(3):
            remote(r.vec_own, vec_all.at[sprev[o]], r.vec_s.at[o], r.vec_r.at[o], sdev[o]).wait_recv()

    last = halves - 1

    def branch_grad(k, g):
        step = halves + k
        low = (g * vec(2, k)).astype(BF)
        bgrad[k, 0] = low
        share_rows(bgrad.at[k], step).start()
        tiles[k, lay.bias_at : lay.bias_at + 1, :] = column_sum(low.astype(F32))

    norm_row(0)
    g4_buf[prow - 16 :, :] = jnp.zeros((16, width), F32)
    g4_buf[:rows, :] = own_page(r.raw_g)
    branch_grad(last, g4_buf[...])
    ds_ref[...] = jnp.zeros_like(ds_ref)

    pump_far(QKV)
    gather_across(4 + QKV)
    pump_far(OUT)
    pump_near(QKV)
    gather_across(4 + UP)
    gather_start(DN)
    pump_near(OUT)
    gather_across(4 + OUT)
    gather_across(4 + DN)
    pump_far(UP)
    for l in range(layers):
        k = 2 * l
        first = 4 * l
        need(first + QKV)
        attention_page(l, k, 0)
        rows_here(normed.at[k], k)
        if l == 0:
            attention_page(l, k, 1)
            gather_start(4 + QKV)
            need(OUT)
            sum_up_start(k, context_part(l))
            pump_near(UP)
            pump_far(DN)
            gather_start(4 + OUT)
            gather_start(4 + UP)
        else:
            attention_page(l, k, 1)
            pump_near(4 + DN)
            need(4 + OUT)
            sum_up_start(k, context_part(l))
        v_buf[k + 1] = end_forward(k, k)
        norm_row(k + 1)
        k = k + 1
        if l == 0:
            pump_near(DN)
            pump_far(4 + QKV)
            gather_start(4 + DN)
        need(first + UP)
        mlp_page(l, k, 0)
        rows_here(normed.at[k], k)
        mlp_page(l, k, 1)
        if l == 0:
            pump_far(4 + OUT)
            pump_far(4 + UP)
            need(DN)
            sum_up_start(k, hidden_part(l))
            pump_near(4 + QKV)
            pump_near(4 + OUT)
            pump_far(4 + DN)
            pump_near(4 + UP)
            v_buf[k + 1] = end_forward(k, k)
            norm_row(k + 1)

    both = 2 * prow

    def whole(ref):
        return ref.reshape(both, ref.shape[-1])

    def back_through_norm(k, g, ng):
        xhat, rr = norm_stats(v_buf[k].astype(F32))
        tiles[k, lay.gain_at : lay.gain_at + 1, :] = column_sum(ng * xhat)
        tiles[k, lay.shift_at : lay.shift_at + 1, :] = column_sum(ng)
        t = ng * vec(0, k)
        inner = t - jnp.mean(t, -1, keepdims=True) - xhat * jnp.mean(t * xhat, -1, keepdims=True)
        return g + rr * inner

    def scale_sum(k, g):
        tiles[k, lay.scale_at : lay.scale_at + 1, :] = column_sum(g * branch[k])

    def mlp_back(l, k, slot):
        dact = nt(bgrad[k, slot], weight("dn", l))
        gate[l, slot] = (dact * gate[l, slot].astype(F32)).astype(BF)

    def mlp_back_part(l):
        return lambda slot, at: nt(gate[l, slot, at], weight("up", l))

    def up_grads(l, k):
        dpre = whole(gate[l])
        keep_grad(4 * l + UP, tn(whole(normed[k]), dpre))
        sum_start(4 * l + UP)
        sec[lay.up_at + l : lay.up_at + l + 1, :] = column_sum(dpre.astype(F32))

    l, k = layers - 1, last
    rows_here(bgrad.at[k], halves + k)
    keep_grad(4 * l + DN, tn(whole(act[l]), whole(bgrad[k])))
    sum_start(4 * l + DN)
    need(4 * l + DN)
    mlp_back(l, k, 1)
    mlp_back(l, k, 0)
    sum_up_start(k, mlp_back_part(l))
    up_grads(l, k)
    sum_up_start(k + 1, hidden_part(l))
    g = back_through_norm(k, g4_buf[...], sum_up_end(k))
    g_buf[...] = g.astype(BF).astype(F32)

    def end_of_forward():
        after = end_forward(last, last + 1)
        scale_sum(last, g4_buf[...])
        if fused:
            share_page(after, "o_block")
        else:
            r.v4[...] = after

    forward_sends = len(sends)

    def drain(count):
        for copy, when in sends[:count]:
            if when is None:
                copy.wait_send()
            else:
                pl.when(when)(copy.wait_send)
        del sends[:count]

    for k in reversed(range(last)):
        l = k // 2
        step = 2 * halves - 1 - k
        g = g_buf[...]
        branch_grad(k, g)
        scale_sum(k, g)
        if k == last - 1:
            sum_first(4 * l + DN)
        if k % 2 == 0:

            def attention_back(slot):
                dctx = nt(bgrad[k, slot], weight("out", l)).astype(BF)
                for h in range(heads):
                    q = qkv[l, slot, :, h * hd : (h + 1) * hd]
                    kk = qkv[l, slot, :, own + h * hd : own + (h + 1) * hd]
                    vv = qkv[l, slot, :, 2 * own + h * hd : 2 * own + (h + 1) * hd]
                    dc = dctx[:, h * hd : (h + 1) * hd]
                    low_p = probs[l, slot, h]
                    p = low_p.astype(F32)
                    dp_ = nt(dc, vv)
                    ds = (p * (dp_ - jnp.sum(p * dp_, -1, keepdims=True))).astype(BF)
                    ds_ref[(l * heads + h) * 2 + slot, :, :prow] = ds.astype(F32)
                    dqkv[slot, :, h * hd : (h + 1) * hd] = (nn(ds, kk) * scale).astype(BF)
                    dqkv[slot, :, own + h * hd : own + (h + 1) * hd] = (tn(ds, q) * scale).astype(BF)
                    dqkv[slot, :, 2 * own + h * hd : 2 * own + (h + 1) * hd] = tn(low_p, dc).astype(BF)

            if l == 0:
                rows_here(bgrad.at[k], halves + k)
                keep_grad(OUT, tn(whole(ctx[l]), whole(bgrad[k])))
                sum_start(OUT)
                attention_back(0)
            else:
                attention_back(0)
                rows_here(bgrad.at[k], halves + k)
            attention_back(1)
            if l == 0:
                sum_second(4 + QKV)
                sum_second(4 + OUT)
            sum_up_start(step, lambda slot, at: nt(dqkv[slot, at], weight("qkv", l)))
            sum_first(4 * l + (UP if l > 0 else DN))
            dall = whole(dqkv[...])
            keep_grad(4 * l + QKV, tn(whole(normed[k]), dall))
            sum_start(4 * l + QKV)
            sums = column_sum(dall.astype(F32))
            sec[lay.qv_at + l : lay.qv_at + l + 1, :own] = sums[:, :own]
            sec[lay.qv_at + l : lay.qv_at + l + 1, 2 * LANES : 2 * LANES + own] = sums[:, 2 * own :]
            if l > 0:
                keep_grad(4 * l + OUT, tn(whole(ctx[l]), whole(bgrad[k])))
                sum_start(4 * l + OUT)
                end_of_forward()
                table_sums(l, 0, 2)
            else:
                sum_first(OUT)
                sum_start(UPB)
                table_sums(l, 0, 2)
                sum_first(UP)
                table_sums(l, 1, 2)
        else:
            rows_here(bgrad.at[k], halves + k)
            keep_grad(4 * l + DN, tn(whole(act[l]), whole(bgrad[k])))
            sum_start(4 * l + DN)
            sum_second(4 * (l + 1) + DN)
            mlp_back(l, k, 1)
            mlp_back(l, k, 0)
            sum_up_start(step, mlp_back_part(l))
            up_grads(l, k)
            sum_second(4 * (l + 1) + UP)
            sum_first(4 * (l + 1) + QKV)
            table_sums(l + 1, 1, 2)
            drain(forward_sends)
            early_sends = len(sends)
            sum_first(4 * (l + 1) + OUT)
        g = back_through_norm(k, g, sum_up_end(step))
        if k > 0:
            g_buf[...] = g.astype(BF).astype(F32)

    kept = jnp.where(masked, 0.0, g)
    token_sum = column_sum(jnp.where(masked, g, 0.0))
    for k in range(halves):
        tiles[k, lay.token_at : lay.token_at + 1, :] = token_sum
    for k in range(halves):
        share_rows(normed.at[k], k).wait_send()
        share_rows(bgrad.at[k], halves + k).wait_send()

    if not fused:
        r.g0[...] = kept
        return

    tile_copy = remote(tiles.at[mate_at], r.tile_in, r.small_s.at[0], r.small_r.at[0], mate)
    tile_copy.start()
    sent(tile_copy)
    red, red_in = r.red, r.red_in
    hops = [znear, zfar, xmate]

    def hop_copy(hop):
        return remote(red.at[hop], red_in.at[hop], r.small_s.at[1 + hop], r.small_r.at[1 + hop], hops[hop])

    def hop_start(hop):
        hop_copy(hop).start()
        sent(hop_copy(hop))

    def hop_end(hop):
        hop_copy(hop).wait_recv()
        red[hop + 1] = red[hop] + red_in[hop]

    share_page(kept, "o_input")
    finish_item(4 + DN)
    finish_item(4 + UP)
    tile_copy.wait_recv()
    red[0, :8] = tiles[section] + r.tile_in[...]
    red[0, 8:] = sec[...]
    hop_start(0)
    sum_second(DN)
    finish_item(4 + QKV)
    finish_item(4 + OUT)
    sum_first(QKV)
    sum_second(UP)
    hop_end(0)
    hop_start(1)
    finish_item(DN)
    sum_second(OUT)
    sum_second(QKV)
    sum_first(UPB)
    hop_end(1)
    hop_start(2)
    finish_item(UP)
    drain(early_sends)
    sum_second(UPB)
    hop_end(2)
    r.o_tile[...] = red[3, :8]
    sec_all, sec_sum = r.o_sec, r.sec_sum
    sec_sum[...] = red[3, 8:]
    sec_all[section] = sec_sum[...]
    for o in range(3):
        copy = remote(sec_sum, sec_all.at[section], r.sec_s.at[o], r.sec_r.at[o], sdev[o])
        copy.start()
        sent(copy)
    finish_item(OUT)
    finish_item(QKV)
    finish_item(UPB)
    page_here("o_block")
    page_here("o_input")
    for n in reversed(range(4 * layers)):
        item_here(n)
    for o in range(3):
        remote(sec_sum, sec_all.at[sprev[o]], r.sec_s.at[o], r.sec_r.at[o], sdev[o]).wait_recv()
    drain(len(sends))


def run_blocks(lay, operands):
    L, prow, width, own, hid, shard = lay.layers, lay.prow, lay.width, lay.own, lay.hidden, lay.shard
    halves, steps, heads, pcol, page = lay.halves, 2 * lay.halves, lay.heads, lay.pcol, lay.rows
    rows = (prow, width)
    groups = 2 * heads
    dma = pltpu.SemaphoreType.DMA
    outs, scratch = {}, {}
    items = 4 * L
    wide = {"qkv": 3 * own, "up": hid, "dn": width, "out": width}
    raw = types.SimpleNamespace(**{name: (x.shape, x.dtype) for name, x in operands.items()})
    if lay.fused:
        outs.update(o_block=((2, prow, own), BF))
        outs.update(o_input=((2, prow, own), F32))
        outs.update(t_qkv=((L, 3, shard, own), BF))
        outs.update(t_out=((L, shard, own), BF))
        outs.update(t_up=((L, 4, shard, own), BF))
        outs.update(t_dn=((L, 4, shard, own), BF))
        outs.update(o_tile=((8, width), F32))
        outs.update(o_sec=((4, lay.sec_rows, width), F32))
        scratch.update(tiles=((halves, 8, width), F32))
        scratch.update(sec=((lay.sec_rows, width), F32))
        scratch.update(vec_all=((halves, 8, width), F32))
        scratch.update(vec_own=((8, width), F32))
        for kind, c in wide.items():
            lead = (2,) if kind == "out" else (2, 2, 2)
            scratch["w_" + kind] = ((L,) + lead + (shard, c), BF)
            scratch["g_" + kind] = ((L,) + lead + (shard, c), BF)
            scratch["x_" + kind] = ((L,) + (lead if kind == "out" else lead[:-1]) + (shard, c), BF)
            scratch["n_" + kind] = ((L,) + lead[:-2] + (shard, c), BF)
            scratch["f_" + kind] = ((L, shard, c), BF)
            scratch["s_" + kind] = ((L, 3 if kind == "qkv" else 4, shard, own), BF)
        scratch.update(a_qkv=((L, shard, 3 * own), BF))
        scratch.update(a_up=((L, shard, hid), BF))
        scratch.update(raw_qkv=(raw.qkv_weight, raw.up_weight)[0], raw_up=(raw.qkv_weight, raw.up_weight)[1])
        scratch.update(raw_qvb=(raw.qv_bias, raw.up_bias)[0], raw_upb=(raw.qv_bias, raw.up_bias)[1])
        scratch.update(raw_vec=((4,) + raw.ln_gain[0], BF))
        scratch.update(qvb=(((L, 3 * own), F32), ((L, hid), F32))[0], upb=(((L, 3 * own), F32), ((L, hid), F32))[1])
        scratch.update(o_block_s=(((4, prow, own), BF), ((4, prow, own), F32))[0], o_input_s=(((4, prow, own), BF), ((4, prow, own), F32))[1])
        scratch.update(tile_in=((8, width), F32))
        scratch.update(red=((4, 8 + lay.sec_rows, width), F32))
        scratch.update(red_in=((3, 8 + lay.sec_rows, width), F32))
        scratch.update(sec_sum=((lay.sec_rows, width), F32))
    else:
        outs.update(v4=(rows, BF))
        outs.update(g0=(rows, F32))
        outs.update(tiles=((halves, 8, width), F32))
        outs.update(sec=((lay.sec_rows, width), F32))
        outs.update(g_qkv=(((L, width, 3 * own), BF), ((L, own, width), BF))[0], g_out=(((L, width, 3 * own), BF), ((L, own, width), BF))[1])
        outs.update(g_up=(((L, width, hid), BF), ((L, hid, width), BF))[0], g_dn=(((L, width, hid), BF), ((L, hid, width), BF))[1])
    scratch.update(
        raw_x=raw.patches,
        raw_g=raw.cotangent,
        raw_mask=raw.page_mask,
        raw_token=raw.mask_token,
        raw_ids=raw.buckets,
        raw_table=raw.rel_table,
        ids=((prow, pcol), jnp.int32),
        table=((pad_up(L * heads, 8), lay.highs * LANES), F32),
        bias=((L * heads, prow, pcol), BF),
        v_buf=((halves,) + rows, BF),
        normed=((halves, 2) + rows, BF),
        branch=((halves,) + rows, F32),
        qkv=((L, 2, prow, 3 * own), BF),
        probs=((L, 2, heads, prow, prow), BF),
        ctx=((L, 2, prow, own), BF),
        act=((L, 2, prow, hid), BF),
        gate=((L, 2, prow, hid), BF),
        bgrad=((halves, 2) + rows, BF),
        dqkv=((2, prow, 3 * own), BF),
        acc=(rows, F32),
        g_buf=(rows, F32),
        g4_buf=(rows, F32),
        ds=((L * groups, prow, pcol), F32),
        hist=((lay.highs * groups, LANES), F32),
        core_out=((3,) + rows, BF),
        core_in=((3,) + rows, BF),
        far_out=((3,) + rows, BF),
        far_in=((3,) + rows, BF),
    )
    each = (steps,)
    halved = (steps, 2)
    sems = dict(core_s=halved, core_r=halved, far_s=halved, far_r=halved, row_s=each, row_r=each, load_s=(16,))
    if lay.fused:
        sems.update(
            ag_zfs=(items,), ag_zfr=(items,), ag_zns=(items,), ag_znr=(items,),
            ag_xs=(items, 3), ag_xr=(items, 3), ag_ls=(items,), vec_s=(3,), vec_r=(3,),
            rs_xs=(items + 1,), rs_xr=(items + 1,), rs_ns=(items + 1,), rs_nr=(items + 1,),
            rs_fs=(items + 1,), rs_fr=(items + 1,),
            rs_ss=(items, 3), rs_sr=(items, 3), page_s=(2,), page_r=(2,), small_s=(4,), small_r=(4,),
            sec_s=(3,), sec_r=(3,),
        )
    names = list(operands) + list(outs) + list(scratch) + list(sems)
    in_vmem = ("w_qkv", "w_out", "w_up", "w_dn", "vec_all", "qvb", "upb")
    spaces = [pltpu.VMEM if name in in_vmem else pl.ANY for name in operands]
    results = pl.pallas_call(
        functools.partial(blocks_kernel, lay, names),
        out_shape=tuple(jax.ShapeDtypeStruct(*spec) for spec in outs.values()),
        in_specs=[pl.BlockSpec(memory_space=space) for space in spaces],
        out_specs=[pl.BlockSpec(memory_space=pltpu.VMEM)] * len(outs),
        scratch_shapes=[pltpu.VMEM(*spec) for spec in scratch.values()] + [dma(spec) for spec in sems.values()],
        compiler_params=pltpu.CompilerParams(
            collective_id=1, has_side_effects=True, vmem_limit_bytes=61 * 2**20
        ),
        name="blocks",
        cost_estimate=pl.CostEstimate(flops=9 * 10**9, bytes_accessed=2 * 10**7, transcendentals=10**7),
    )(*operands.values())
    return dict(zip(outs, results))


def assemble_kernel(
    lay, block_ref, input_ref, qkv_ref, out_ref, up_ref, dn_ref, tile_ref, sec_ref,
    o_block, o_input, o_qkv, o_out, o_up, o_dn, o_qv, o_upb, o_table,
    o_gain, o_shift, o_scale, o_bias, o_token,
):
    rows, own, layers, heads = lay.rows, lay.own, lay.layers, lay.heads
    unit = own // 2
    for page in range(2):
        o_block[page] = block_ref[page].astype(F32).T[:, :rows].astype(BF)
        o_input[page] = input_ref[page].T[:, :rows]
    for l in range(layers):
        o_qkv[l] = jnp.concatenate([qkv_ref[l, place] for place in range(3)], 1).astype(F32)
        o_out[l] = out_ref[l].astype(F32)
        pieces = [up_ref[l, t, :, half * unit : (half + 1) * unit] for half in range(2) for t in range(4)]
        o_up[l] = jnp.concatenate(pieces, 1).astype(F32)
        o_dn[l] = dn_ref[l].reshape(4 * lay.shard, own).astype(F32).T
    q = [sec_ref[t, lay.qv_at : lay.qv_at + layers, :own] for t in range(4)]
    v = [sec_ref[t, lay.qv_at : lay.qv_at + layers, 2 * LANES : 2 * LANES + own] for t in range(4)]
    o_qv[...] = jnp.concatenate(q + v, 1)
    up = [sec_ref[t, lay.up_at : lay.up_at + layers, :] for t in range(4)]
    count = lay.hidden // unit
    o_upb[...] = jnp.concatenate([up[t][:, d * unit : (d + 1) * unit] for d in range(count) for t in range(4)], 1)
    buckets = o_table.shape[2]
    for l in range(layers):
        for t in range(4):
            at = lay.table_at + l * heads
            for h in range(heads):
                o_table[t * heads + h, l : l + 1, :] = sec_ref[t, at + h : at + h + 1, :buckets]
    for out, at in ((o_gain, lay.gain_at), (o_shift, lay.shift_at), (o_scale, lay.scale_at), (o_bias, lay.bias_at)):
        out[...] = tile_ref[at : at + 1, :]
    o_token[...] = tile_ref[lay.token_at, :]


def assemble(lay, bucket_count, res):
    L, own, width, hid, shard = lay.layers, lay.own, lay.width, lay.hidden, lay.shard
    row = ((1, width), F32)
    outs = [
        ((2, own, lay.rows), BF), ((2, own, lay.rows), F32),
        ((L, shard, 3 * own), F32), ((L, shard, own), F32), ((L, shard, hid), F32), ((L, own, 4 * shard), F32),
        ((L, 2 * width), F32), ((L, 4 * hid), F32), ((4 * lay.heads, L, bucket_count), F32),
        row, row, row, row, ((width,), F32),
    ]
    return pl.pallas_call(
        functools.partial(assemble_kernel, lay),
        out_shape=tuple(jax.ShapeDtypeStruct(*spec) for spec in outs),
        in_specs=[pl.BlockSpec(memory_space=pltpu.VMEM)] * len(res),
        name="assemble",
        cost_estimate=pl.CostEstimate(flops=10**6, bytes_accessed=4 * 10**6, transcendentals=0),
    )(*res.values())


def per_device(
    patches, page_mask, mask_token, buckets, ln_gain, ln_shift, layer_scale, branch_bias,
    qkv_weight, qv_bias, out_weight, rel_table, up_weight, up_bias, down_weight, cotangent,
):
    section = lax.axis_index("section")
    sections = lax.axis_size("section")
    ranks = lax.axis_size("dp")
    layers = qkv_weight.shape[0]
    pages, rows, width = patches.shape
    all_heads = rel_table.shape[1]
    bucket_count = rel_table.shape[2]
    head = width // all_heads
    heads = all_heads // sections
    own = heads * head
    hidden = up_weight.shape[2]
    hid = hidden // sections
    prow, pcol = pad_up(rows, 16), pad_up(rows, LANES)
    highs = pad_up(bucket_count, LANES) // LANES
    fused = ranks == 8 and sections == 4
    shard = qkv_weight.shape[1]
    lay = Layout(layers, heads, head, rows, prow, pcol, width, hid, shard, highs, fused)

    operands = dict(
        patches=patches.transpose(1, 0, 2), page_mask=page_mask, mask_token=mask_token,
        buckets=buckets, rel_table=rel_table.transpose(1, 0, 2), cotangent=cotangent.transpose(1, 0, 2),
    )
    if fused:
        operands.update(
            ln_gain=ln_gain, ln_shift=ln_shift, layer_scale=layer_scale, branch_bias=branch_bias,
            qkv_weight=qkv_weight, out_weight=out_weight, up_weight=up_weight, down_weight=down_weight,
            qv_bias=qv_bias, up_bias=up_bias,
        )
        out = list(assemble(lay, bucket_count, run_blocks(lay, operands)))
        for at in (0, 1, 5):
            out[at] = out[at].transpose(0, 2, 1)
        out[8] = out[8].transpose(1, 0, 2)
        return tuple(out)

    unit = down_weight.shape[1] // sections
    cols = width // sections

    def pick(x, axis):
        return lax.dynamic_index_in_dim(x, section, axis, keepdims=False)

    qkv_own = pick(qkv_weight.reshape(layers, shard, 3, sections, own), 3).reshape(layers, shard, 3 * own)
    up_own = pick(up_weight.reshape(layers, shard, ranks, sections, unit), 3).reshape(layers, shard, hid)
    dn_own = pick(down_weight.reshape(layers, sections, unit, width), 1)

    vecs = jnp.concatenate([ln_gain, ln_shift, layer_scale, branch_bias], 0).astype(F32)
    vecs = jnp.pad(vecs, ((0, 4), (0, 0)))
    qv_own = pick(qv_bias.reshape(layers, 2, sections, own), 2).astype(F32)
    qv_vec = jnp.concatenate([qv_own[:, 0], jnp.zeros_like(qv_own[:, 0]), qv_own[:, 1]], 1)
    upb_own = pick(up_bias.reshape(layers, ranks, sections, unit), 2).reshape(layers, hid).astype(F32)
    operands.update(qvb=qv_vec, upb=upb_own)

    def assembled(sec_all):
        qv = sec_all[:, lay.qv_at : lay.qv_at + layers]
        qv = jnp.stack([qv[..., :own], qv[..., 2 * LANES : 2 * LANES + own]], 2)
        qv = qv.transpose(1, 2, 0, 3).reshape(layers, 2 * width)
        up = sec_all[:, lay.up_at : lay.up_at + layers].reshape(sections, layers, ranks, unit)
        up = up.transpose(1, 2, 0, 3).reshape(layers, hidden)
        table = sec_all[:, lay.table_at : lay.table_at + layers * heads, :bucket_count]
        table = table.reshape(sections, layers, heads, bucket_count)
        return qv, up, table.transpose(1, 0, 2, 3).reshape(layers, all_heads, bucket_count)

    def gathered(x):
        return lax.all_gather(x, "dp", axis=1, tiled=True)

    operands.update(
        vec_all=lax.all_gather(vecs, "section", axis=0, tiled=False),
        w_qkv=gathered(qkv_own),
        w_out=pick(gathered(out_weight).reshape(layers, sections, own, width), 1),
        w_up=gathered(up_own),
        w_dn=gathered(dn_own),
    )
    res = run_blocks(lay, operands)

    def scattered(x):
        return lax.psum_scatter(x, "dp", scatter_dimension=1, tiled=True)

    def everywhere(x, axis):
        return lax.all_gather(x, "section", axis=axis, tiled=False)

    sqkv, sup, sdn = scattered(res["g_qkv"]), scattered(res["g_up"]), scattered(res["g_dn"])
    qkv_all = everywhere(sqkv.reshape(layers, shard, 3, own), 3).reshape(layers, shard, 3 * width)
    qkv_cols = 3 * width // sections
    qkv_out = lax.dynamic_slice_in_dim(qkv_all, section * qkv_cols, qkv_cols, 2).astype(F32)
    up_all = everywhere(sup.reshape(layers, shard, ranks, unit), 3).reshape(layers, shard, hidden)
    up_out = lax.dynamic_slice_in_dim(up_all, section * hid, hid, 2).astype(F32)
    dn_all = lax.all_to_all(
        sdn.reshape(layers, unit, sections, cols), "section", split_axis=2, concat_axis=1, tiled=False
    )
    dn_out = dn_all.reshape(layers, sections * unit, cols).astype(F32)
    out_mine = scattered(everywhere(res["g_out"], 1).reshape(layers, width, width))
    out_out = lax.dynamic_slice_in_dim(out_mine, section * cols, cols, 2).astype(F32)

    def pages_of(x):
        both = lax.all_gather(x[:rows], "section", axis=0, tiled=False)[:pages]
        return lax.dynamic_slice_in_dim(both, section * cols, cols, 2)

    once = (section < 2).astype(F32)
    here = (jnp.arange(sections) == section).astype(F32)
    tiles, sec_all = lax.psum(
        (res["tiles"] * once, res["sec"][None] * here[:, None, None]), ("section", "dp")
    )
    tile = pick(tiles, 0)
    return (
        pages_of(res["v4"]), pages_of(res["g0"]), qkv_out, out_out, up_out, dn_out,
        *assembled(sec_all),
        *[tile[at : at + 1] for at in (lay.gain_at, lay.shift_at, lay.scale_at, lay.bias_at)],
        tile[lay.token_at],
    )


def solution(mesh):
    rows3 = P("dp", None, None)
    part = P("section", None)
    weight = P(None, "dp", None)
    in_specs = (
        rows3, P("dp", None), P(), P(), part, part, part, part,
        weight, P(), weight, P(), weight, P(), weight, rows3,
    )
    cut = P("dp", None, "section")
    grad = P(None, "dp", "section")
    out_specs = (cut, cut, grad, grad, grad, grad, P(), P(), P(), part, part, part, part, P())
    return jax.shard_map(per_device, mesh=mesh, in_specs=in_specs, out_specs=out_specs, check_vma=False)
```
